32 devices in a mesh: dp: 4 (over x, core), row: 4 (over z), col: 2 (over y).
Axes of the slice: x: 2, y: 2, z: 4, core: 2. Of those that a mesh axis runs over, the one named last changes fastest.
Arguments:
- states: bfloat16 [8192, 2048], P(('dp', 'row'), 'col'), may hold values from -6 to 6
- keep: int32 [8192], P(('dp', 'row')), may hold values 0 or 1
- cont_ids: int32 [4, 1024], P('dp'), may hold values from 0 to 3, never falling along the last dimension, each value on 1 to 512 neighbouring positions
- answer_len: int32 [4, 4], P('dp'), may hold values from 1 to 512
- teacher: bfloat16 [8192, 2048], P(('dp', 'row'), 'col'), may hold values from -6 to 6
- out_grad: bfloat16 [8192, 2048], P(('dp', 'row'), 'col'), may hold values from -6 to 6
- gain_attn: float32 [2048], P('col'), may hold values from 0.5 to 1.5
- w_query: bfloat16 [2048, 2048], P('col', 'row'), may hold values from -0.125 to 0.125
- key_projection: bfloat16 [2048, 512], P('col', 'row'), may hold values from -0.125 to 0.125
- value_projection: bfloat16 [2048, 512], P('col', 'row'), may hold values from -0.125 to 0.125
- w_out: bfloat16 [2048, 2048], P('row', 'col'), may hold values from -1.5 to 1.5
- gain_ffn: float32 [2048], P('col'), may hold values from 0.5 to 1.5
- w_gate: bfloat16 [2048, 5632], P('col', 'row'), may hold values from -0.125 to 0.125
- w_up: bfloat16 [2048, 5632], P('col', 'row'), may hold values from -0.125 to 0.125
- w_down: bfloat16 [5632, 2048], P('row', 'col'), may hold values from -0.078125 to 0.078125
Outputs:
- output: bfloat16 [8192, 2048], P(('dp', 'row'), 'col')
- loss: float32 [], replicated
- grad_states: float32 [8192, 2048], P(('dp', 'row'), 'col')
- grad_gain_attn: float32 [2048], P('col')
- grad_query: float32 [2048, 2048], P('col', 'row')
- grad_key: float32 [2048, 512], P('col', 'row')
- grad_value: float32 [2048, 512], P('col', 'row')
- grad_out: float32 [2048, 2048], P('row', 'col')
- grad_gain_ffn: float32 [2048], P('col')
- grad_gate: float32 [2048, 5632], P('col', 'row')
- grad_up: float32 [2048, 5632], P('col', 'row')
- grad_down: float32 [5632, 2048], P('row', 'col')
The draws below stay inside these ranges and needn't reach their ends.
Inputs may be any that keep to these rules, and one draw needn't show every extreme that they name: `cont_ids`: in each group the continuation numbers never fall along the tokens, and each continuation has 1 to 512 tokens.
All inputs are finite; a program needn't handle non-finite values. No bound on the sum of `keep` on one device may be relied on, other than what follows from the above.
Results may differ from the reference program's by a relative error of at most 0.019.
Values may be sent and summed in bfloat16 or wider, within the bound.
No kernel may reach another device: no remote copies, remote signals or barrier semaphores. Data moves between devices by JAX's collectives and lax.ppermute only.
A program may use at most 192 MiB of HBM per device.

```python
import math
import jax
import jax.numpy as jnp
import numpy as np
from jax import lax

MODEL_WIDTH = 2048
HQ = 16
KEY_VALUE_HEADS = 4
HEAD_SIZE = 128
FF = 5632
PROMPT = 1024
CONTS = 4
CONT_LEN = 256
CONT_TOK = 1024
NGROUPS = 4
TOKENS = 8192


def with_ends(values, key, low, high):
    dims = values.shape
    place = [jax.random.randint(jax.random.fold_in(key, axis), (), 0, dims[axis]) for axis in range(len(dims))]
    values = values.at[tuple(place)].set(low)
    longest = dims.index(max(dims))
    place[longest] = (place[longest] + 1) % dims[longest]
    return values.at[tuple(place)].set(high)


def level_of(own_key, extent, pieces, smallest, top_value):
    level, own = 1.0, jax.random.fold_in(own_key, 6)
    for dim, shards_of in pieces:
        steps = jnp.exp(jax.random.uniform(jax.random.fold_in(own, dim), (shards_of,), jnp.float32, smallest / len(pieces), top_value / len(pieces)))
        level = level * jnp.repeat(steps, extent[dim] // shards_of).reshape([-1 if axis == dim else 1 for axis in range(len(extent))])
    return level


def split_up(count, total, bound, slope):
    portions = [(1 << 20) // math.isqrt(grade ** slope) + 1 for grade in range(2, count + 1)]
    surplus, holding = total - bound - (count - 1), [1] * (count - 1)
    while surplus > 0:
        movable = [i for i in range(count - 1) if holding[i] < bound]
        whole, left = sum([portions[i] for i in movable]), surplus
        for i in movable:
            addition = min(bound - holding[i], max(1, left * portions[i] // whole), surplus)
            holding[i] = holding[i] + addition
            surplus = surplus - addition
    return np.array([bound] + holding)


def uneven(rng, amount, total, most, slope):
    if amount == 2:
        one = jax.random.randint(rng, (), max(1, total - most), min(most, total - 1) + 1)
        return jnp.stack([one, total - one])
    lengths = jnp.asarray(split_up(amount, total, most, slope), jnp.int32)
    couples = (amount - 1) // 2
    giver, receiver = lengths[1:1 + 2 * couples:2], lengths[2:2 + 2 * couples:2]
    margin = jnp.minimum(giver - 1, most - receiver)
    passed = jax.random.randint(jax.random.fold_in(rng, 1), (couples,), 0, 1 << 20) % (margin + 1)
    lengths = lengths.at[1:1 + 2 * couples:2].set(giver - passed).at[2:2 + 2 * couples:2].set(receiver + passed)
    return lengths[jax.random.permutation(jax.random.fold_in(rng, 2), amount)]


def centred(own_key, extent, width, bound, cuts=(), kind=jnp.bfloat16):
    factor_of = level_of(own_key, extent, cuts, -0.22, 0.18) if cuts else 1.0
    values = jax.random.normal(own_key, extent, jnp.float32) * width * factor_of
    return jnp.minimum(jnp.maximum(values, -bound), bound).astype(kind)


def setup_inputs(seed: int = 0) -> dict:
    seeds = jax.random.split(jax.random.key(seed), 16)
    return {
        "states": centred(seeds[0], (TOKENS, MODEL_WIDTH), 1.0, 6.0, ((0, 16), (1, 2))),
        "keep": with_ends((jax.random.randint(seeds[1], (TOKENS,), 0, 4) < 3).astype(jnp.int32), jax.random.fold_in(seeds[1], 1), 0, 1),
        "cont_ids": jax.vmap(lambda own: jnp.searchsorted(jnp.cumsum(uneven(own, CONTS, CONT_TOK, 2 * CONT_LEN, 0)), jnp.arange(CONT_TOK), side="right"))(jax.random.split(seeds[2], NGROUPS)).reshape((NGROUPS, CONT_TOK)).astype(jnp.int32),
        "answer_len": with_ends(jax.random.randint(seeds[3], (NGROUPS, CONTS), 1, 2 * CONT_LEN + 1), jax.random.fold_in(seeds[3], 1), 1, 2 * CONT_LEN).astype(jnp.int32),
        "teacher": centred(seeds[4], (TOKENS, MODEL_WIDTH), 1.0, 6.0, ((0, 16), (1, 2))),
        "out_grad": centred(seeds[5], (TOKENS, MODEL_WIDTH), 1.0, 6.0, ((0, 16), (1, 2))),
        "gain_attn": jnp.clip(1.0 + 0.1 * jax.random.normal(seeds[6], (MODEL_WIDTH,), jnp.float32), 0.5, 1.5),
        "w_query": centred(seeds[7], (MODEL_WIDTH, HQ * HEAD_SIZE), MODEL_WIDTH ** -0.5, 0.125, ((0, 2), (1, 4))),
        "key_projection": centred(seeds[8], (MODEL_WIDTH, KEY_VALUE_HEADS * HEAD_SIZE), MODEL_WIDTH ** -0.5, 0.125, ((0, 2), (1, 4))),
        "value_projection": centred(seeds[9], (MODEL_WIDTH, KEY_VALUE_HEADS * HEAD_SIZE), MODEL_WIDTH ** -0.5, 0.125, ((0, 2), (1, 4))),
        "w_out": centred(seeds[10], (HQ * HEAD_SIZE, MODEL_WIDTH), 16 ** -0.5, 1.5, ((0, 4), (1, 2))),
        "gain_ffn": jnp.clip(1.0 + 0.1 * jax.random.normal(seeds[11], (MODEL_WIDTH,), jnp.float32), 0.5, 1.5),
        "w_gate": centred(seeds[12], (MODEL_WIDTH, FF), MODEL_WIDTH ** -0.5, 0.125, ((0, 2), (1, 4))),
        "w_up": centred(seeds[13], (MODEL_WIDTH, FF), MODEL_WIDTH ** -0.5, 0.125, ((0, 2), (1, 4))),
        "w_down": centred(seeds[14], (FF, MODEL_WIDTH), FF ** -0.5, 0.078125, ((0, 4), (1, 2))),
    }


EPSILON = 1e-05
MASKED = -1e+30
ROPE_BASE = 10000.0

@jax.custom_vjp
def low(v):
    return lax.optimization_barrier(v.astype(jnp.bfloat16)).astype(jnp.float32)

@jax.custom_vjp
def low_back(v):
    return v

def low_keep(v):
    return (low(v), None)

def low_pass(kept, grad):
    return (grad,)

def back_keep(v):
    return (v, None)

def back_low(kept, grad):
    return (low(grad),)
low.defvjp(low_keep, low_pass)
low_back.defvjp(back_keep, back_low)

def rows_of(values, start, count):
    return lax.dynamic_slice_in_dim(values, start, count, 0)

def token_layout(cont_ids, answer_len):
    groups, cont_tokens = cont_ids.shape
    labels = jnp.arange(answer_len.shape[1], dtype=jnp.int32)
    starts = lax.optimization_barrier(jnp.sum((cont_ids[:, None, :] < labels[None, :, None]).astype(jnp.int32), axis=2))
    member = (cont_ids[:, :, None] == labels[None, None, :]).astype(jnp.int32)
    own_start = lax.optimization_barrier(jnp.sum(member * starts[:, None, :], axis=2))
    own_limit = lax.optimization_barrier(jnp.sum(member * answer_len[:, None, :], axis=2))
    offset = jnp.arange(cont_tokens, dtype=jnp.int32)[None, :] - own_start
    prompt_pos = jnp.broadcast_to(jnp.arange(PROMPT, dtype=jnp.int32)[None, :], (groups, PROMPT))
    positions = jnp.concatenate([prompt_pos, PROMPT + offset], axis=1).reshape(-1)
    segment = jnp.concatenate([jnp.full((groups, PROMPT), -1, dtype=jnp.int32), cont_ids], axis=1).reshape(-1)
    counted = jnp.concatenate([jnp.ones((groups, PROMPT), jnp.int32), (offset < own_limit).astype(jnp.int32)], axis=1).reshape(-1)
    return (positions, segment, counted)

def rotary(values, positions, sign):
    half = values.shape[-1] // 2
    freqs = ROPE_BASE ** (-2.0 * jnp.arange(half, dtype=jnp.float32) / values.shape[-1])
    angles = positions.astype(jnp.float32)[:, None] * freqs[None, :]
    cosine = jnp.cos(angles)[:, None, :]
    sine = sign * jnp.sin(angles)[:, None, :]
    first = values[..., :half]
    second = values[..., half:]
    return jnp.concatenate([first * cosine - second * sine, second * cosine + first * sine], axis=-1)

def visible(query_index, query_segment, key_index, key_segment):
    earlier = key_index[None, :] <= query_index[:, None]
    shared = (key_segment[None, :] < 0) | (key_segment[None, :] == query_segment[:, None])
    return earlier & shared

def exact_dot(left, right):
    return jnp.dot(left, right, precision=lax.Precision.HIGHEST, preferred_element_type=jnp.float32)

def exact_einsum(form, left, right):
    return jnp.einsum(form, left, right, precision=lax.Precision.HIGHEST, preferred_element_type=jnp.float32)

def group_layer(states_g, keep_g, pos_g, seg_g, gain_attn, query_weight, key_weight, value_weight, out_weight, gain_ffn, gate_weight, up_weight, down_weight):
    tokens = states_g.shape[0]
    key_heads = key_weight.shape[1] // HEAD_SIZE
    heads_per_group = query_weight.shape[1] // key_weight.shape[1]
    scale = HEAD_SIZE ** (-0.5)
    scale_attn = lax.rsqrt(lax.optimization_barrier(jnp.mean(states_g * states_g, axis=1, keepdims=True)) + EPSILON)
    normed_attn = low(states_g * scale_attn * gain_attn[None, :])
    query_raw = low_back(exact_dot(normed_attn, query_weight))
    key_raw = low_back(exact_dot(normed_attn, key_weight))
    values = low(low_back(exact_dot(normed_attn, value_weight))).reshape(tokens, key_heads, HEAD_SIZE)
    queries = low(rotary(query_raw.reshape(tokens, key_heads * heads_per_group, HEAD_SIZE), pos_g, 1.0)).reshape(tokens, key_heads, heads_per_group, HEAD_SIZE)
    keys = low(rotary(key_raw.reshape(tokens, key_heads, HEAD_SIZE), pos_g, 1.0))
    block = min(512, tokens)
    token_index = jnp.arange(tokens, dtype=jnp.int32)

    @jax.checkpoint
    def attend(query_block, first):
        raw = low_back(exact_einsum('qgjd,kgd->gjqk', query_block, keys) * scale)
        mask = visible(rows_of(token_index, first, block), rows_of(seg_g, first, block), token_index, seg_g)
        scores = jnp.where(mask[None, None], raw, MASKED)
        weights = low(jax.nn.softmax(scores, axis=-1))
        return exact_einsum('gjqk,kgd->qgjd', weights, values)
    starts = jnp.arange(tokens // block, dtype=jnp.int32) * block
    blocked = queries.reshape(tokens // block, block, key_heads, heads_per_group, HEAD_SIZE)
    mixed = lax.map(lambda item: attend(item[0], item[1]), (blocked, starts))
    context = low(low_back(mixed.reshape(tokens, key_heads * heads_per_group * HEAD_SIZE)))
    attention = low_back(exact_dot(context, out_weight))
    hidden_res = states_g + keep_g * attention
    scale_ffn = lax.rsqrt(lax.optimization_barrier(jnp.mean(hidden_res * hidden_res, axis=1, keepdims=True)) + EPSILON)
    normed_ffn = low(hidden_res * scale_ffn * gain_ffn[None, :])
    gate = low_back(exact_dot(normed_ffn, gate_weight))
    up_proj = low_back(exact_dot(normed_ffn, up_weight))
    hidden = low(jax.nn.silu(gate) * up_proj)
    feed = low_back(exact_dot(hidden, down_weight))
    return hidden_res + keep_g * feed

def reference(states, keep, cont_ids, answer_len, teacher, out_grad, gain_attn, w_query, key_projection, value_projection, w_out, gain_ffn, w_gate, w_up, w_down):
    positions, segment, counted = token_layout(cont_ids, answer_len)
    groups = cont_ids.shape[0]
    group_tokens = PROMPT + cont_ids.shape[1]
    counted_f = counted.astype(jnp.float32).reshape(groups, group_tokens, 1)
    token_count_sum = jnp.sum(counted_f)
    keep_f = keep.astype(jnp.float32).reshape(groups, group_tokens, 1)
    teacher_float = teacher.astype(jnp.float32).reshape(groups, group_tokens, MODEL_WIDTH)
    pos_all = positions.reshape(groups, group_tokens)
    seg_all = segment.reshape(groups, group_tokens)
    states_f = states.astype(jnp.float32).reshape(groups, group_tokens, MODEL_WIDTH)

    def forward(states_in, gain_a, query_weight, key_weight, value_weight, out_weight, gain_f, gate_weight, up_weight, down_weight):

        def step(total, item):
            states_g, keep_g, pos_g, seg_g, counted_g, teacher_g = item
            result = group_layer(states_g, keep_g, pos_g, seg_g, gain_a, query_weight, key_weight, value_weight, out_weight, gain_f, gate_weight, up_weight, down_weight)
            error = result - teacher_g
            return (total + jnp.sum(counted_g * error * error), result)
        error_total, results = lax.scan(step, jnp.zeros((), jnp.float32), (states_in, keep_f, pos_all, seg_all, counted_f, teacher_float))
        return (results, error_total / (token_count_sum * MODEL_WIDTH))
    primals = (states_f, gain_attn, w_query.astype(jnp.float32), key_projection.astype(jnp.float32), value_projection.astype(jnp.float32), w_out.astype(jnp.float32), gain_ffn, w_gate.astype(jnp.float32), w_up.astype(jnp.float32), w_down.astype(jnp.float32))
    (results, loss), pull = jax.vjp(forward, *primals)
    grads = pull((out_grad.astype(jnp.float32).reshape(groups, group_tokens, MODEL_WIDTH), jnp.ones((), jnp.float32)))
    return (results.reshape(-1, MODEL_WIDTH).astype(jnp.bfloat16), loss, grads[0].reshape(-1, MODEL_WIDTH), grads[1], grads[2], grads[3], grads[4], grads[5], grads[6], grads[7], grads[8], grads[9])
```

```python
import functools

import jax
import jax.numpy as jnp
from jax import lax
from jax.experimental import pallas as pl
from jax.experimental.pallas import tpu as pltpu
from jax.sharding import PartitionSpec as P

MODEL_WIDTH = 2048
HEAD_SIZE = 128
PROMPT = 1024


EPSILON = 1e-05
MASKED = -1e30
ROPE_BASE = 10000.0


def rows_of(values, start, count, axis=0):
    return lax.dynamic_slice_in_dim(values, start, count, axis)


def token_layout(cont_ids, answer_len):
    groups, cont_tokens = cont_ids.shape
    labels = jnp.arange(answer_len.shape[1], dtype=jnp.int32)
    starts = jnp.sum((cont_ids[:, None, :] < labels[None, :, None]).astype(jnp.int32), axis=2)
    member = (cont_ids[:, :, None] == labels[None, None, :]).astype(jnp.int32)
    own_start = jnp.sum(member * starts[:, None, :], axis=2)
    own_limit = jnp.sum(member * answer_len[:, None, :], axis=2)
    offset = jnp.arange(cont_tokens, dtype=jnp.int32)[None, :] - own_start
    prompt_pos = jnp.arange(PROMPT, dtype=jnp.int32)[None, :]
    positions = jnp.concatenate([prompt_pos, PROMPT + offset], axis=1).reshape(-1)
    segment = jnp.concatenate(
        [jnp.full((groups, PROMPT), -1, dtype=jnp.int32), cont_ids], axis=1
    ).reshape(-1)
    counted = jnp.concatenate(
        [jnp.ones((groups, PROMPT), jnp.int32), (offset < own_limit).astype(jnp.int32)], axis=1
    ).reshape(-1)
    return (positions, segment, counted)


def rotary(values, positions, sign):
    half = values.shape[-1] // 2
    freqs = ROPE_BASE ** (-2.0 * jnp.arange(half, dtype=jnp.float32) / values.shape[-1])
    angles = positions.astype(jnp.float32)[:, None] * freqs[None, :]
    cosine = jnp.cos(angles)[:, None, :]
    sine = sign * jnp.sin(angles)[:, None, :]
    first = values[..., :half]
    second = values[..., half:]
    return jnp.concatenate(
        [first * cosine - second * sine, second * cosine + first * sine], axis=-1
    )


def visible(query_index, query_segment, key_index, key_segment):
    earlier = key_index[None, :] <= query_index[:, None]
    shared = (key_segment[None, :] < 0) | (key_segment[None, :] == query_segment[:, None])
    return earlier & shared


def feature_sum(values):
    return lax.psum(values, "col")


def gather_rows(values):
    return lax.all_gather(values, "row", axis=0, tiled=True)


def gather_cols(values):
    return lax.all_gather(values, "col", axis=0, tiled=True)


def partial_cols(term, count):
    return lax.psum_scatter(
        term(jnp.int32(0), count * lax.axis_size("col")), "col", scatter_dimension=0, tiled=True
    )


def partial_rows(term, count):
    return lax.psum_scatter(
        term(jnp.int32(0), count * lax.axis_size("row")), "row", scatter_dimension=0, tiled=True
    )


def body(
    states,
    keep,
    cont_ids,
    answer_len,
    teacher,
    out_grad,
    gain_attn,
    w_query,
    key_projection,
    value_projection,
    w_out,
    gain_ffn,
    w_gate,
    w_up,
    w_down,
):
    local_rows = states.shape[0]
    whole_rows = local_rows * lax.axis_size("row")
    query_rows = whole_rows // lax.axis_size("col")
    group_tokens = PROMPT + cont_ids.shape[1]
    key_heads = key_projection.shape[1] // HEAD_SIZE
    heads_per_group = w_query.shape[1] // key_projection.shape[1]
    query_width = w_query.shape[1]
    scale = HEAD_SIZE ** (-0.5)
    block = min(512, query_rows)
    blocks = query_rows // block
    positions, segment, counted = token_layout(cont_ids, answer_len)
    token_index = jnp.arange(whole_rows, dtype=jnp.int32)
    row_start = lax.axis_index("row") * local_rows
    col_start = lax.axis_index("col") * query_rows
    counted_here = rows_of(counted, row_start, local_rows).astype(jnp.float32)[:, None]
    query_pos = rows_of(positions, col_start, query_rows)
    keep_here = keep.astype(jnp.float32)[:, None]
    states_f = states.astype(jnp.float32)
    scale_attn = lax.rsqrt(
        feature_sum(jnp.sum(states_f * states_f, axis=1)) / MODEL_WIDTH + EPSILON
    )[:, None]
    normed_attn = (states_f * scale_attn * gain_attn[None, :]).astype(jnp.bfloat16)
    normed_all = gather_rows(normed_attn)
    w_kv = jnp.concatenate([key_projection, value_projection], axis=1)
    query_raw = partial_cols(
        lambda start, count: jnp.dot(
            rows_of(normed_all, start, count), w_query, preferred_element_type=jnp.float32
        ),
        query_rows,
    )
    kv_raw = lax.psum(jnp.dot(normed_all, w_kv, preferred_element_type=jnp.float32), "col")
    queries = (
        rotary(
            query_raw.reshape(query_rows, key_heads * heads_per_group, HEAD_SIZE), query_pos, 1.0
        )
        .astype(jnp.bfloat16)
        .reshape(query_rows, key_heads, heads_per_group, HEAD_SIZE)
    )
    keys = rotary(
        kv_raw[:, : key_heads * HEAD_SIZE].reshape(whole_rows, key_heads, HEAD_SIZE), positions, 1.0
    ).astype(jnp.bfloat16)
    values = (
        kv_raw[:, key_heads * HEAD_SIZE :]
        .reshape(whole_rows, key_heads, HEAD_SIZE)
        .astype(jnp.bfloat16)
    )

    def context_of(index):
        first = col_start + index * block
        key_first = first // group_tokens * group_tokens
        query_block = rows_of(queries, index * block, block)
        key_group = rows_of(keys, key_first, group_tokens)
        value_group = rows_of(values, key_first, group_tokens)
        raw = (
            jnp.einsum("qgjd,kgd->gjqk", query_block, key_group, preferred_element_type=jnp.float32)
            * scale
        )
        mask = visible(
            rows_of(token_index, first, block),
            rows_of(segment, first, block),
            rows_of(token_index, key_first, group_tokens),
            rows_of(segment, key_first, group_tokens),
        )
        scores = jnp.where(mask[None, None], raw, MASKED)
        return (query_block, key_group, value_group, scores, key_first)

    def attend(index):
        query_block, key_group, value_group, scores, key_first = context_of(index)
        peak = jnp.max(scores, axis=-1, keepdims=True)
        exponent = jnp.exp(scores - peak)
        totals = jnp.sum(exponent, axis=-1, keepdims=True)
        weights = (exponent / totals).astype(jnp.bfloat16)
        mixed = jnp.einsum(
            "gjqk,kgd->qgjd", weights, value_group, preferred_element_type=jnp.float32
        )
        return (mixed, peak + jnp.log(totals))

    mixed_blocks, log_totals = lax.map(attend, jnp.arange(blocks, dtype=jnp.int32))
    attn_context = mixed_blocks.reshape(query_rows, query_width).astype(jnp.bfloat16)
    context_all = gather_cols(attn_context)
    attention = partial_rows(
        lambda start, count: jnp.dot(
            rows_of(context_all, start, count), w_out, preferred_element_type=jnp.float32
        ),
        local_rows,
    )
    hidden_res = states_f + keep_here * attention
    scale_ffn = lax.rsqrt(
        feature_sum(jnp.sum(hidden_res * hidden_res, axis=1)) / MODEL_WIDTH + EPSILON
    )[:, None]
    normed_ffn = (hidden_res * scale_ffn * gain_ffn[None, :]).astype(jnp.bfloat16)
    ffn_all = gather_rows(normed_ffn)
    w_pair = jnp.concatenate([w_gate, w_up], axis=1)
    inner = w_gate.shape[1]
    gate_up = partial_cols(
        lambda start, count: jnp.dot(
            rows_of(ffn_all, start, count), w_pair, preferred_element_type=jnp.float32
        ),
        query_rows,
    )
    gate = gate_up[:, :inner]
    up_proj = gate_up[:, inner:]
    sigma = jax.nn.sigmoid(gate)
    swish = gate * sigma
    hidden = (swish * up_proj).astype(jnp.bfloat16)
    hidden_all = gather_cols(hidden)
    feed = partial_rows(
        lambda start, count: jnp.dot(
            rows_of(hidden_all, start, count), w_down, preferred_element_type=jnp.float32
        ),
        local_rows,
    )
    result = hidden_res + keep_here * feed
    error = result - teacher.astype(jnp.float32)
    own_count = jnp.where(lax.axis_index("col") == 0, jnp.sum(counted_here), 0.0)
    error_total, token_count_sum = lax.psum(
        (jnp.sum(counted_here * error * error), own_count), ("dp", "row", "col")
    )
    loss = error_total / (token_count_sum * MODEL_WIDTH)
    grad_result = (
        out_grad.astype(jnp.float32) + 2.0 / (token_count_sum * MODEL_WIDTH) * counted_here * error
    )
    grad_feed = (keep_here * grad_result).astype(jnp.bfloat16)
    grad_feed_all = gather_rows(grad_feed)
    grad_down = jnp.einsum(
        "tf,td->fd", hidden_all, grad_feed_all, preferred_element_type=jnp.float32
    )
    grad_hidden = partial_cols(
        lambda start, count: jnp.einsum(
            "td,fd->tf",
            rows_of(grad_feed_all, start, count),
            w_down,
            preferred_element_type=jnp.float32,
        ),
        query_rows,
    )
    grad_gate_in = grad_hidden * up_proj * sigma * (1.0 + gate * (1.0 - sigma))
    grad_up_in = grad_hidden * swish
    grad_pair = jnp.concatenate([grad_gate_in, grad_up_in], axis=1).astype(jnp.bfloat16)
    grad_pair_all = gather_cols(grad_pair)
    grad_w_pair = jnp.einsum(
        "td,tf->df", ffn_all, grad_pair_all, preferred_element_type=jnp.float32
    )
    grad_normed_ffn = partial_rows(
        lambda start, count: jnp.einsum(
            "tf,df->td",
            rows_of(grad_pair_all, start, count),
            w_pair,
            preferred_element_type=jnp.float32,
        ),
        local_rows,
    )
    grad_gain_ffn = jnp.sum(grad_normed_ffn * hidden_res * scale_ffn, axis=0)
    weighted_ffn = grad_normed_ffn * gain_ffn[None, :]
    inner_ffn = feature_sum(jnp.sum(weighted_ffn * hidden_res, axis=1))[:, None]
    grad_hidden_res = (
        grad_result + scale_ffn * weighted_ffn - hidden_res * scale_ffn**3 * inner_ffn / MODEL_WIDTH
    )
    grad_attention = (keep_here * grad_hidden_res).astype(jnp.bfloat16)
    grad_att_all = gather_rows(grad_attention)
    grad_out = jnp.einsum(
        "to,td->od", context_all, grad_att_all, preferred_element_type=jnp.float32
    )
    grad_context = partial_cols(
        lambda start, count: jnp.einsum(
            "td,od->to",
            rows_of(grad_att_all, start, count),
            w_out,
            preferred_element_type=jnp.float32,
        ),
        query_rows,
    )
    grad_context = grad_context.astype(jnp.bfloat16).reshape(
        query_rows, key_heads, heads_per_group, HEAD_SIZE
    )

    def attend_back(carry, item):
        index, log_total = item
        query_block, key_group, value_group, scores, key_first = context_of(index)
        grad_block = rows_of(grad_context, index * block, block)
        probs = jnp.exp(scores - log_total)
        grad_probs = jnp.einsum(
            "qgjd,kgd->gjqk", grad_block, value_group, preferred_element_type=jnp.float32
        )
        row_dot = jnp.sum(probs * grad_probs, axis=-1, keepdims=True)
        grad_scores = (probs * (grad_probs - row_dot)).astype(jnp.bfloat16)
        grad_query_block = (
            jnp.einsum("gjqk,kgd->qgjd", grad_scores, key_group, preferred_element_type=jnp.float32)
            * scale
        )
        grad_key_group = (
            jnp.einsum(
                "gjqk,qgjd->kgd", grad_scores, query_block, preferred_element_type=jnp.float32
            )
            * scale
        )
        grad_value_group = jnp.einsum(
            "gjqk,qgjd->kgd",
            probs.astype(jnp.bfloat16),
            grad_block,
            preferred_element_type=jnp.float32,
        )
        pair = jnp.concatenate([grad_key_group, grad_value_group], axis=1)
        updated = rows_of(carry, key_first, group_tokens) + pair
        return (updated, grad_query_block)

    start_carry = jnp.zeros((whole_rows, 2 * key_heads, HEAD_SIZE), jnp.float32)
    grad_kv_part, grad_query_blocks = lax.scan(
        attend_back, start_carry, (jnp.arange(blocks, dtype=jnp.int32), log_totals)
    )
    grad_kv_sum = (
        lax.psum(
            grad_kv_part.reshape(whole_rows, 2 * key_heads * HEAD_SIZE).astype(jnp.bfloat16), "col"
        )
        .astype(jnp.float32)
        .reshape(whole_rows, 2 * key_heads, HEAD_SIZE)
    )
    grad_keys = rotary(grad_kv_sum[:, :key_heads], positions, -1.0)
    grad_kv = (
        jnp.concatenate([grad_keys, grad_kv_sum[:, key_heads:]], axis=1)
        .reshape(whole_rows, 2 * key_heads * HEAD_SIZE)
        .astype(jnp.bfloat16)
    )
    grad_queries = (
        rotary(
            grad_query_blocks.reshape(query_rows, key_heads * heads_per_group, HEAD_SIZE),
            query_pos,
            -1.0,
        )
        .reshape(query_rows, query_width)
        .astype(jnp.bfloat16)
    )
    grad_queries_all = gather_cols(grad_queries)
    grad_query = jnp.einsum(
        "td,tq->dq", normed_all, grad_queries_all, preferred_element_type=jnp.float32
    )
    grad_kv_weight = jnp.einsum(
        "td,tk->dk", normed_all, grad_kv, preferred_element_type=jnp.float32
    )
    grad_key = grad_kv_weight[:, : key_heads * HEAD_SIZE]
    grad_value = grad_kv_weight[:, key_heads * HEAD_SIZE :]

    def back_terms(start, count):
        from_queries = jnp.einsum(
            "tq,dq->td",
            rows_of(grad_queries_all, start, count),
            w_query,
            preferred_element_type=jnp.float32,
        )
        from_kv = jnp.einsum(
            "tk,dk->td", rows_of(grad_kv, start, count), w_kv, preferred_element_type=jnp.float32
        )
        return from_queries + from_kv

    grad_normed_attn = partial_rows(back_terms, local_rows)
    grad_gain_attn = jnp.sum(grad_normed_attn * states_f * scale_attn, axis=0)
    weighted_attn = grad_normed_attn * gain_attn[None, :]
    inner_attn = feature_sum(jnp.sum(weighted_attn * states_f, axis=1))[:, None]
    grad_states = (
        grad_hidden_res
        + scale_attn * weighted_attn
        - states_f * scale_attn**3 * inner_attn / MODEL_WIDTH
    )
    gain_attn_sum, gain_ffn_sum = lax.psum((grad_gain_attn, grad_gain_ffn), ("dp", "row"))
    summed = (
        lax.psum(grad_query.astype(jnp.bfloat16), "dp").astype(jnp.float32),
        lax.psum(grad_key.astype(jnp.bfloat16), "dp").astype(jnp.float32),
        lax.psum(grad_value.astype(jnp.bfloat16), "dp").astype(jnp.float32),
        lax.psum(grad_out.astype(jnp.bfloat16), "dp").astype(jnp.float32),
        lax.psum(grad_w_pair[:, :inner].astype(jnp.bfloat16), "dp").astype(jnp.float32),
        lax.psum(grad_w_pair[:, inner:].astype(jnp.bfloat16), "dp").astype(jnp.float32),
        lax.psum(grad_down.astype(jnp.bfloat16), "dp").astype(jnp.float32),
    )
    return (
        result.astype(jnp.bfloat16),
        loss,
        grad_states,
        gain_attn_sum,
        summed[0],
        summed[1],
        summed[2],
        summed[3],
        gain_ffn_sum,
        summed[4],
        summed[5],
        summed[6],
    )


LOG2E = 1.4426950408889634
VMEM_BYTES = 58 << 20
ORDER = (0, 2, 1, 3)


def swap(values, axis, mask):
    size = lax.axis_size(axis)
    return lax.ppermute(values, axis, [(i, i ^ mask) for i in range(size)])


def xor_order(slots, mask):
    bit = 1
    while bit < len(slots):
        odd = (mask & bit) != 0
        slots = [jnp.where(odd, slots[i ^ bit], slots[i]) for i in range(len(slots))]
        bit *= 2
    return slots


def low(values):
    return values.astype(jnp.bfloat16)


def wide(values):
    return values.astype(jnp.float32)


def dot_nn(left, right):
    return lax.dot_general(left, right, (((1,), (0,)), ((), ())), preferred_element_type=jnp.float32)


def dot_nt(left, right):
    return lax.dot_general(left, right, (((1,), (1,)), ((), ())), preferred_element_type=jnp.float32)


def dot_tn(left, right):
    return lax.dot_general(left, right, (((0,), (0,)), ((), ())), preferred_element_type=jnp.float32)


def attend_kernel(slots, scale, flags, q_ref, qseg_ref, kseg_ref, *refs):
    kv_refs = refs[:slots]
    o_ref, lse_ref, peak_ref, total_ref, acc_ref = refs[slots:]
    query = q_ref[...]
    rows = query.shape[0]

    def scores(slot):
        return dot_nt(kv_refs[slot][:, :HEAD_SIZE], query) * (scale * LOG2E)

    def seen(slot):
        key_seg = kseg_ref[slot * rows : (slot + 1) * rows, :]
        return (key_seg < 0) | (key_seg == qseg_ref[...])

    def add(slot, s):
        peak = peak_ref[...]
        higher = jnp.maximum(peak, jnp.max(s, axis=0, keepdims=True))
        fade = jnp.exp2(peak - higher)
        e = jnp.exp2(s - higher)
        total_ref[...] = total_ref[...] * fade + jnp.sum(e, axis=0, keepdims=True)
        acc_ref[...] = acc_ref[...] * fade + dot_tn(kv_refs[slot][:, HEAD_SIZE:], low(e))
        peak_ref[...] = higher

    key_index = lax.broadcasted_iota(jnp.int32, (rows, rows), 0)
    query_index = lax.broadcasted_iota(jnp.int32, (rows, rows), 1)
    s = jnp.where((key_index <= query_index) & seen(0), scores(0), MASKED)
    peak = jnp.max(s, axis=0, keepdims=True)
    e = jnp.exp2(s - peak)
    peak_ref[...] = peak
    total_ref[...] = jnp.sum(e, axis=0, keepdims=True)
    acc_ref[...] = dot_tn(kv_refs[0][:, HEAD_SIZE:], low(e))
    for slot in range(1, slots):

        @pl.when(flags[slot] == 1)
        def _(slot=slot):
            add(slot, scores(slot))

        @pl.when(flags[slot] == 2)
        def _(slot=slot):
            add(slot, jnp.where(seen(slot), scores(slot), MASKED))

    o_ref[...] = low(jnp.transpose(acc_ref[...] / total_ref[...]))
    lse_ref[0] = peak_ref[...] + jnp.log2(total_ref[...])


def attend_back_kernel(slots, scale, flags, q_ref, do_ref, lse_ref, cos_ref, sin_ref, qseg_ref, kseg_ref, *refs):
    kv_refs = refs[:slots]
    dq_ref = refs[slots]
    dkv_refs = refs[slots + 1 : 2 * slots + 1]
    p_ref, dp_ref, dot_ref, dq_acc, dkv_acc = refs[2 * slots + 1 :]
    step, steps = pl.program_id(1), pl.num_programs(1)
    query, grad = q_ref[...], do_ref[...]
    rows = query.shape[0]

    @pl.when(step == 0)
    def _():
        dkv_acc[...] = jnp.zeros_like(dkv_acc)

    def seen(slot):
        key_seg = kseg_ref[slot * rows : (slot + 1) * rows, :]
        return (key_seg < 0) | (key_seg == qseg_ref[...])

    def first(slot, mask):
        e = jnp.exp2(dot_nt(kv_refs[slot][:, :HEAD_SIZE], query) * (scale * LOG2E) - lse_ref[0])
        if mask is not None:
            e = jnp.where(mask, e, 0.0)
        dp = dot_nt(kv_refs[slot][:, HEAD_SIZE:], grad)
        p_ref[slot] = e
        dp_ref[slot] = dp
        part = jnp.sum(e * dp, axis=0, keepdims=True)
        if slot == 0:
            dot_ref[...] = part
        else:
            dot_ref[...] += part

    def second(slot):
        p = p_ref[slot]
        ds = low(p * (dp_ref[slot] - dot_ref[...]))
        dkv_acc[slot, :, :HEAD_SIZE] += dot_nn(ds, query)
        dkv_acc[slot, :, HEAD_SIZE:] += dot_nn(low(p), grad)
        part = dot_tn(kv_refs[slot][:, :HEAD_SIZE], ds)
        if slot == 0:
            dq_acc[...] = part
        else:
            dq_acc[...] += part

    key_index = lax.broadcasted_iota(jnp.int32, (rows, rows), 0)
    query_index = lax.broadcasted_iota(jnp.int32, (rows, rows), 1)
    first(0, (key_index <= query_index) & seen(0))
    for slot in range(1, slots):

        @pl.when(flags[slot] == 1)
        def _(slot=slot):
            first(slot, None)

        @pl.when(flags[slot] == 2)
        def _(slot=slot):
            first(slot, seen(slot))

    second(0)
    for slot in range(1, slots):

        @pl.when(flags[slot] > 0)
        def _(slot=slot):
            second(slot)

    half = HEAD_SIZE // 2
    upper, lower = dq_acc[:half, :] * scale, dq_acc[half:, :] * scale
    cosine, sine = cos_ref[...], sin_ref[...]
    turned = jnp.concatenate([upper * cosine + lower * sine, lower * cosine - upper * sine], axis=0)
    dq_ref[...] = low(jnp.transpose(turned))

    @pl.when(step == steps - 1)
    def _():
        for slot in range(slots):
            out = dkv_refs[slot]
            out[:, :HEAD_SIZE] = (dkv_acc[slot, :, :HEAD_SIZE] * scale).astype(out.dtype)
            out[:, HEAD_SIZE:] = dkv_acc[slot, :, HEAD_SIZE:].astype(out.dtype)


def attend(flags, queries, query_seg, key_seg, key_values):
    rows, width = queries.shape
    slots, groups = len(key_values), key_values[0].shape[1] // (2 * HEAD_SIZE)
    share = width // HEAD_SIZE // groups
    whole = lambda g, m, f: (0, 0)
    head = lambda g, m, f: (0, m * groups + g)
    return pl.pallas_call(
        functools.partial(attend_kernel, slots, HEAD_SIZE ** (-0.5)),
        out_shape=(
            jax.ShapeDtypeStruct((rows, width), jnp.bfloat16),
            jax.ShapeDtypeStruct((share * groups, 1, rows), jnp.float32),
        ),
        grid_spec=pltpu.PrefetchScalarGridSpec(
            num_scalar_prefetch=1,
            grid=(groups, share),
            in_specs=[
                pl.BlockSpec((rows, HEAD_SIZE), head),
                pl.BlockSpec((1, rows), whole),
                pl.BlockSpec((slots * rows, 1), whole),
            ]
            + [pl.BlockSpec((rows, 2 * HEAD_SIZE), lambda g, m, f: (0, g))] * slots,
            out_specs=(
                pl.BlockSpec((rows, HEAD_SIZE), head),
                pl.BlockSpec((1, 1, rows), lambda g, m, f: (m * groups + g, 0, 0)),
            ),
            scratch_shapes=[
                pltpu.VMEM((1, rows), jnp.float32),
                pltpu.VMEM((1, rows), jnp.float32),
                pltpu.VMEM((HEAD_SIZE, rows), jnp.float32),
            ],
        ),
        compiler_params=pltpu.CompilerParams(vmem_limit_bytes=VMEM_BYTES),
        cost_estimate=pl.CostEstimate(
            flops=3 * rows * rows * width * 4, transcendentals=3 * rows * rows * share * groups, bytes_accessed=8 << 20
        ),
        name="attend",
    )(flags, queries, query_seg, key_seg, *key_values)


def attend_back(flags, queries, grads, lse, cosine, sine, query_seg, key_seg, key_values):
    rows, width = queries.shape
    slots, groups = len(key_values), key_values[0].shape[1] // (2 * HEAD_SIZE)
    share = width // HEAD_SIZE // groups
    whole = lambda g, m, f: (0, 0)
    head = lambda g, m, f: (0, m * groups + g)
    pair = pl.BlockSpec((rows, 2 * HEAD_SIZE), lambda g, m, f: (0, g))
    return pl.pallas_call(
        functools.partial(attend_back_kernel, slots, HEAD_SIZE ** (-0.5)),
        out_shape=(
            jax.ShapeDtypeStruct((rows, width), jnp.bfloat16),
            jax.ShapeDtypeStruct(key_values[0].shape, jnp.float32),
        )
        + (jax.ShapeDtypeStruct(key_values[0].shape, jnp.bfloat16),) * (slots - 1),
        grid_spec=pltpu.PrefetchScalarGridSpec(
            num_scalar_prefetch=1,
            grid=(groups, share),
            in_specs=[
                pl.BlockSpec((rows, HEAD_SIZE), head),
                pl.BlockSpec((rows, HEAD_SIZE), head),
                pl.BlockSpec((1, 1, rows), lambda g, m, f: (m * groups + g, 0, 0)),
                pl.BlockSpec((HEAD_SIZE // 2, rows), whole),
                pl.BlockSpec((HEAD_SIZE // 2, rows), whole),
                pl.BlockSpec((1, rows), whole),
                pl.BlockSpec((slots * rows, 1), whole),
            ]
            + [pair] * slots,
            out_specs=(pl.BlockSpec((rows, HEAD_SIZE), head),) + (pair,) * slots,
            scratch_shapes=[
                pltpu.VMEM((slots, rows, rows), jnp.float32),
                pltpu.VMEM((slots, rows, rows), jnp.float32),
                pltpu.VMEM((1, rows), jnp.float32),
                pltpu.VMEM((HEAD_SIZE, rows), jnp.float32),
                pltpu.VMEM((slots, rows, 2 * HEAD_SIZE), jnp.float32),
            ],
        ),
        compiler_params=pltpu.CompilerParams(vmem_limit_bytes=VMEM_BYTES),
        cost_estimate=pl.CostEstimate(
            flops=3 * rows * rows * width * 10, transcendentals=3 * rows * rows * share * groups, bytes_accessed=12 << 20
        ),
        name="attend_back",
    )(flags, queries, grads, lse, cosine, sine, query_seg, key_seg, *key_values)


def feed_kernel(a_ref, wg_ref, wu_ref, wd_ref, gate_ref, up_ref, hid_ref, out_ref):
    gate = dot_nt(a_ref[...], wg_ref[...])
    up = dot_nt(a_ref[...], wu_ref[...])
    hid = low(gate * jax.nn.sigmoid(gate) * up)
    gate_ref[...] = gate
    up_ref[...] = up
    hid_ref[...] = hid
    out_ref[...] = low(dot_nn(hid, wd_ref[...]))


def feed_back_kernel(gm_ref, gate_ref, up_ref, wg_ref, wu_ref, wd_ref, dgate_ref, dup_ref, out_ref):
    dhid = dot_nt(gm_ref[...], wd_ref[...])
    gate, up = gate_ref[...], up_ref[...]
    sigma = jax.nn.sigmoid(gate)
    dgate = low(dhid * up * sigma * (1.0 + gate * (1.0 - sigma)))
    dup = low(dhid * (gate * sigma))
    dgate_ref[...] = dgate
    dup_ref[...] = dup
    out_ref[...] = low(dot_nn(dgate, wg_ref[...]) + dot_nn(dup, wu_ref[...]))


def feed_call(kernel, name, wide_in, narrow_in, weights, narrow_out, rows=256):
    tokens, features = wide_in.shape
    hidden = weights[0].shape[0]
    by_rows = lambda width: pl.BlockSpec((rows, width), lambda i: (i, 0))
    fixed = pl.BlockSpec((hidden, features), lambda i: (0, 0), pipeline_mode=pl.Buffered(1))
    return pl.pallas_call(
        kernel,
        out_shape=tuple(jax.ShapeDtypeStruct((tokens, hidden), t) for t in narrow_out)
        + (jax.ShapeDtypeStruct((tokens, features), jnp.bfloat16),),
        grid=(tokens // rows,),
        in_specs=[by_rows(features)] + [by_rows(hidden) for _ in narrow_in] + [fixed] * len(weights),
        out_specs=tuple(by_rows(hidden) for _ in narrow_out) + (by_rows(features),),
        compiler_params=pltpu.CompilerParams(vmem_limit_bytes=VMEM_BYTES),
        cost_estimate=pl.CostEstimate(
            flops=6 * tokens * hidden * features, transcendentals=tokens * hidden, bytes_accessed=40 << 20
        ),
        name=name,
    )(wide_in, *narrow_in, *weights)


def feed(tokens, wg, wu, wd):
    return feed_call(feed_kernel, "feed", tokens, [], [wg, wu, wd], (jnp.float32, jnp.float32, jnp.bfloat16))


def feed_back(grads, gate, up, wg, wu, wd):
    return feed_call(feed_back_kernel, "feed_back", grads, [gate, up], [wg, wu, wd], (jnp.bfloat16, jnp.bfloat16))


def plane_gather(x):
    half = x.shape[0] // 2
    a, b = x[:half], x[half:]
    a_x = swap(a, "dp", 2)
    b_y = swap(b, "col", 1)
    a_y = swap(jnp.concatenate([a, a_x], axis=0), "col", 1)
    b_x = swap(jnp.concatenate([b, b_y], axis=1), "dp", 2)
    pieces = [x, a_x, b_y, a_y, b_x]
    sides = []
    for x_, a_x_, b_y_, a_y_, b_x_ in (pieces, [swap(piece, "dp", 1) for piece in pieces]):
        own = jnp.concatenate([x_, a_x_, b_x_[:, : x.shape[1]]], axis=0)
        other = jnp.concatenate([a_y_[:half], b_y_, a_y_[half:], b_x_[:, x.shape[1] :]], axis=0)
        sides.append(jnp.concatenate([own, other], axis=1))
    return jnp.concatenate(sides, axis=0)


def plane_scatter(p):
    rows, width = p.shape[0] // 2, p.shape[1] // 2
    half = rows // 4
    q = wide(p[:rows]) + wide(swap(p[rows:], "dp", 1))
    a_x = swap(low(q[2 * half : 3 * half]), "dp", 2)
    b_y = swap(low(jnp.concatenate([q[half : 2 * half, width:], q[3 * half :, width:]], axis=0)), "col", 1)
    a = q[:half] + wide(a_x)
    b = jnp.concatenate([q[half : 2 * half, :width], q[3 * half :, :width]], axis=0) + wide(b_y)
    a_y = swap(low(a[:, width:]), "col", 1)
    b_x = swap(low(b[half:]), "dp", 2)
    return jnp.concatenate([a[:, :width] + wide(a_y), b[:half] + wide(b_x)], axis=0)


def dp_slots(x):
    far = swap(x, "dp", 2)
    return [x, swap(x, "dp", 1), far, swap(far, "dp", 1)]


def home(slots, order):
    odd = swap(low(jnp.concatenate([slots[1], slots[3]], axis=0)), "dp", 1)
    count = slots[0].shape[0]
    near = wide(slots[0]) + wide(odd[:count])
    far = swap(low(wide(slots[2]) + wide(odd[count:])), "dp", 2)
    total = near + wide(far)
    parts = xor_order([low(total[i]) for i in range(count)], order)
    summed = wide(parts[0])
    for k in range(1, count):
        summed += wide(swap(parts[k], "row", k))
    return xor_order(dp_slots(low(summed)), lax.axis_index("dp"))


def fast_body(
    states,
    keep,
    cont_ids,
    answer_len,
    teacher,
    out_grad,
    gain_attn,
    w_query,
    key_projection,
    value_projection,
    w_out,
    gain_ffn,
    w_gate,
    w_up,
    w_down,
):
    rows, width = states.shape
    n_row, n_col, n_dp = lax.axis_size("row"), lax.axis_size("col"), lax.axis_size("dp")
    d, r, y = lax.axis_index("dp"), lax.axis_index("row"), lax.axis_index("col")
    groups = n_row // n_col
    features = width * n_col
    heads_row = w_query.shape[1] // HEAD_SIZE
    order = r ^ (y * groups)

    def along_row(x):
        return xor_order([x] + [swap(x, "row", k) for k in range(1, n_row)], order)

    kv_t = jnp.concatenate([key_projection.T, value_projection.T], axis=0)
    kv_part = kv_t.shape[0] // n_dp
    kv_rows = jnp.concatenate(along_row(rows_of(kv_t, d * kv_part, kv_part)), axis=0)
    kv_slots = xor_order(dp_slots(kv_rows), d)

    def kv_weights(side):
        lo = side * groups * kv_part
        return jnp.concatenate(
            [s[lo + g * kv_part : lo + (g + 1) * kv_part] for g in range(groups) for s in kv_slots], axis=0
        )

    wkv = [kv_weights(0), kv_weights(1)]
    q_part = jnp.concatenate(along_row(rows_of(w_query, d * HEAD_SIZE, HEAD_SIZE, 1).T), axis=0)
    q_slots = dp_slots(q_part)
    side_rows = groups * HEAD_SIZE
    wq = [
        jnp.concatenate([q_slots[m][s * side_rows : (s + 1) * side_rows] for m in ORDER], axis=0) for s in (0, 1)
    ]
    o_part = jnp.concatenate(along_row(rows_of(w_out, d * HEAD_SIZE, HEAD_SIZE)), axis=0)
    o_slots = dp_slots(o_part)
    wo = [
        jnp.concatenate([o_slots[m][s * side_rows : (s + 1) * side_rows] for m in ORDER], axis=0) for s in (0, 1)
    ]

    inner = w_down.shape[0]
    inner_part = inner // (n_dp * n_col)

    def hidden_rows(w):
        own = rows_of(w, (d * n_col + y) * inner_part, inner_part)
        other = rows_of(w, (d * n_col + (1 - y)) * inner_part, inner_part)
        return gather_rows(jnp.concatenate([own, swap(other, "col", 1)], axis=1))

    wg, wu, wd = hidden_rows(w_gate.T), hidden_rows(w_up.T), hidden_rows(w_down)

    positions, segment, counted = token_layout(cont_ids, answer_len)
    row_start = r * rows
    count = jnp.sum(counted.astype(jnp.float32)).reshape(1)
    count = count + swap(count, "dp", 1)
    count = (count + swap(count, "dp", 2))[0]
    counted_here = rows_of(counted, row_start, rows).astype(jnp.float32)[:, None]
    keep_here = keep.astype(jnp.float32)[:, None]
    position = rows_of(positions, row_start, rows).astype(jnp.float32)
    query_seg = rows_of(segment, row_start, rows)
    key_segs = [rows_of(segment, jnp.maximum(r - k, 0) * rows, rows) for k in range(n_row)]
    flags = [jnp.int32(2)]
    for k in range(1, n_row):
        least, most = jnp.min(key_segs[k]), jnp.max(key_segs[k])
        active = (r >= k) & ((least < 0) | (most >= jnp.min(query_seg)))
        flags.append(jnp.where(active, jnp.where(most < 0, 1, 2), 0).astype(jnp.int32))
    flags = jnp.stack(flags)
    key_seg = jnp.concatenate(key_segs)[:, None]
    query_seg = query_seg[None, :]
    freqs = ROPE_BASE ** (-2.0 * jnp.arange(HEAD_SIZE // 2, dtype=jnp.float32) / HEAD_SIZE)
    angles_t = freqs[:, None] * position[None, :]
    cos_t, sin_t = jnp.cos(angles_t), jnp.sin(angles_t)
    cos_n, sin_n = cos_t.T, sin_t.T
    cos_n = jnp.concatenate([cos_n, cos_n], axis=1)
    sin_n = jnp.concatenate([-sin_n, sin_n], axis=1)

    def turn(x, sign):
        half = HEAD_SIZE // 2
        turned = jnp.concatenate([x[:, half:], x[:, :half]], axis=1)
        return x * cos_n + turned * (sign * sin_n)

    def turn_heads(x, sign):
        return jnp.concatenate(
            [turn(x[:, i : i + HEAD_SIZE], sign) for i in range(0, x.shape[1], HEAD_SIZE)], axis=1
        )

    def turn_keys(x, sign):
        return jnp.concatenate(
            [
                turn(x[:, i : i + HEAD_SIZE], sign) if i % (2 * HEAD_SIZE) == 0 else x[:, i : i + HEAD_SIZE]
                for i in range(0, x.shape[1], HEAD_SIZE)
            ],
            axis=1,
        )

    states_f = wide(states)
    squares = jnp.sum(states_f * states_f, axis=1)
    scale_attn = lax.rsqrt((squares + swap(squares, "col", 1)) / features + EPSILON)[:, None]
    a1 = low(states_f * scale_attn * gain_attn[None, :])
    kv_sum = dot_nt(a1, wkv[0]) + wide(swap(low(dot_nt(a1, wkv[1])), "col", 1))
    key_value = low(turn_keys(kv_sum, 1.0))
    key_values = [key_value] + [
        lax.ppermute(key_value, "row", [(i, i + k) for i in range(n_row - k)]) for k in range(1, n_row)
    ]
    q_sum = dot_nt(a1, wq[0]) + wide(swap(low(dot_nt(a1, wq[1])), "col", 1))
    queries = low(turn_heads(q_sum, 1.0))
    context, lse = attend(flags, queries, query_seg, key_seg, key_values)
    context_other = swap(context, "col", 1)
    attention = dot_nn(context, wo[0]) + dot_nn(context_other, wo[1])
    hidden_res = states_f + keep_here * attention

    squares = jnp.sum(hidden_res * hidden_res, axis=1)
    scale_ffn = lax.rsqrt((squares + swap(squares, "col", 1)) / features + EPSILON)[:, None]
    a2 = low(hidden_res * scale_ffn * gain_ffn[None, :])
    a2_all = plane_gather(a2)
    gate, up, hidden, parts = feed(a2_all, wg, wu, wd)
    result = hidden_res + keep_here * plane_scatter(parts)
    error = result - wide(teacher)
    error_total = jnp.sum(counted_here * error * error).reshape(1)
    for axis, mask in (("dp", 1), ("dp", 2), ("col", 1), ("row", 1), ("row", 2)):
        error_total = error_total + swap(error_total, axis, mask)
    loss = error_total[0] / (count * features)
    grad_result = wide(out_grad) + 2.0 / (count * features) * counted_here * error

    gm_all = plane_gather(low(keep_here * grad_result))
    dgate, dup, parts = feed_back(gm_all, gate, up, wg, wu, wd)
    grad_normed_ffn = plane_scatter(parts)

    def hidden_home(left, right):
        part = lax.psum_scatter(low(dot_tn(left, right)), "row", scatter_dimension=0, tiled=True)
        own, other = part[:, :width], swap(part[:, width:], "col", 1)
        pair = jnp.concatenate(xor_order([own, other], y), axis=0)
        return lax.all_gather(pair, "dp", axis=0, tiled=True)

    grad_down = wide(hidden_home(hidden, gm_all))
    grad_gate = wide(hidden_home(dgate, a2_all).T)
    grad_up = wide(hidden_home(dup, a2_all).T)
    gain_ffn_sum = jnp.sum(grad_normed_ffn * hidden_res * scale_ffn, axis=0)
    weighted = grad_normed_ffn * gain_ffn[None, :]
    inner_sum = jnp.sum(weighted * hidden_res, axis=1)
    inner_sum = (inner_sum + swap(inner_sum, "col", 1))[:, None]
    grad_hidden_res = grad_result + scale_ffn * weighted - hidden_res * scale_ffn**3 * inner_sum / features

    ga = low(keep_here * grad_hidden_res)
    grad_context = low(dot_nt(ga, wo[0]) + wide(swap(low(dot_nt(ga, wo[1])), "col", 1)))
    dq, *dkv_parts = attend_back(flags, queries, grad_context, lse, cos_t, sin_t, query_seg, key_seg, key_values)
    dkv_sum = dkv_parts[0]
    for k in range(1, n_row):
        dkv_sum += wide(lax.ppermute(dkv_parts[k], "row", [(i + k, i) for i in range(n_row - k)]))
    dkv = low(turn_keys(wide(low(dkv_sum)), -1.0))
    dq_other = swap(dq, "col", 1)
    dkv_other = swap(dkv, "col", 1)
    grad_normed_attn = (
        dot_nn(dq, wq[0]) + dot_nn(dq_other, wq[1]) + dot_nn(dkv, wkv[0]) + dot_nn(dkv_other, wkv[1])
    )

    def head_slots(own, other):
        sides = [x.reshape(n_dp, groups, HEAD_SIZE, width) for x in (own, other)]
        return [jnp.concatenate([s[ORDER.index(m)] for s in sides], axis=0) for m in range(n_dp)]

    grad_out = wide(jnp.concatenate(home(head_slots(dot_tn(context, ga), dot_tn(context_other, ga)), order), axis=0))
    grad_query = wide(jnp.concatenate(home(head_slots(dot_tn(dq, a1), dot_tn(dq_other, a1)), order), axis=0).T)
    dwkv = jnp.concatenate(
        [x.reshape(groups, n_dp, kv_part, width) for x in (dot_tn(dkv, a1), dot_tn(dkv_other, a1))], axis=0
    )
    dwkv = jnp.concatenate(home(xor_order([dwkv[:, i] for i in range(n_dp)], d), order), axis=0)
    grad_key = wide(dwkv[: kv_t.shape[0] // 2].T)
    grad_value = wide(dwkv[kv_t.shape[0] // 2 :].T)

    gain_attn_sum = jnp.sum(grad_normed_attn * states_f * scale_attn, axis=0)
    weighted = grad_normed_attn * gain_attn[None, :]
    inner_sum = jnp.sum(weighted * states_f, axis=1)
    inner_sum = (inner_sum + swap(inner_sum, "col", 1))[:, None]
    grad_states = grad_hidden_res + scale_attn * weighted - states_f * scale_attn**3 * inner_sum / features

    gains = []
    for gain in (gain_attn_sum, gain_ffn_sum):
        for axis, mask in (("dp", 1), ("dp", 2), ("row", 1), ("row", 2)):
            gain = gain + swap(gain, axis, mask)
        gains.append(gain)
    return (
        low(result),
        loss,
        grad_states,
        gains[0],
        grad_query,
        grad_key,
        grad_value,
        grad_out,
        gains[1],
        grad_gate,
        grad_up,
        grad_down,
    )


def solution(mesh):
    return jax.shard_map(
        fast_body if dict(mesh.shape) == {"dp": 4, "row": 4, "col": 2} else body,
        mesh=mesh,
        in_specs=(
            P(("dp", "row"), "col"),
            P(("dp", "row")),
            P("dp", None),
            P("dp", None),
            P(("dp", "row"), "col"),
            P(("dp", "row"), "col"),
            P("col"),
            P("col", "row"),
            P("col", "row"),
            P("col", "row"),
            P("row", "col"),
            P("col"),
            P("col", "row"),
            P("col", "row"),
            P("row", "col"),
        ),
        out_specs=(
            P(("dp", "row"), "col"),
            P(),
            P(("dp", "row"), "col"),
            P("col"),
            P("col", "row"),
            P("col", "row"),
            P("col", "row"),
            P("row", "col"),
            P("col"),
            P("col", "row"),
            P("col", "row"),
            P("row", "col"),
        ),
        check_vma=False,
    )
```

```python
import functools

import jax
import jax.numpy as jnp
from jax import lax
from jax.experimental import pallas as pl
from jax.experimental.pallas import tpu as pltpu
from jax.sharding import PartitionSpec as P

MODEL_WIDTH = 2048
HEAD_SIZE = 128
PROMPT = 1024


EPSILON = 1e-05
MASKED = -1e30
ROPE_BASE = 10000.0


def rows_of(values, start, count, axis=0):
    return lax.dynamic_slice_in_dim(values, start, count, axis)


def token_layout(cont_ids, answer_len):
    groups, cont_tokens = cont_ids.shape
    labels = jnp.arange(answer_len.shape[1], dtype=jnp.int32)
    starts = jnp.sum((cont_ids[:, None, :] < labels[None, :, None]).astype(jnp.int32), axis=2)
    member = (cont_ids[:, :, None] == labels[None, None, :]).astype(jnp.int32)
    own_start = jnp.sum(member * starts[:, None, :], axis=2)
    own_limit = jnp.sum(member * answer_len[:, None, :], axis=2)
    offset = jnp.arange(cont_tokens, dtype=jnp.int32)[None, :] - own_start
    prompt_pos = jnp.arange(PROMPT, dtype=jnp.int32)[None, :]
    positions = jnp.concatenate([prompt_pos, PROMPT + offset], axis=1).reshape(-1)
    segment = jnp.concatenate(
        [jnp.full((groups, PROMPT), -1, dtype=jnp.int32), cont_ids], axis=1
    ).reshape(-1)
    counted = jnp.concatenate(
        [jnp.ones((groups, PROMPT), jnp.int32), (offset < own_limit).astype(jnp.int32)], axis=1
    ).reshape(-1)
    return (positions, segment, counted)


def rotary(values, positions, sign):
    half = values.shape[-1] // 2
    freqs = ROPE_BASE ** (-2.0 * jnp.arange(half, dtype=jnp.float32) / values.shape[-1])
    angles = positions.astype(jnp.float32)[:, None] * freqs[None, :]
    cosine = jnp.cos(angles)[:, None, :]
    sine = sign * jnp.sin(angles)[:, None, :]
    first = values[..., :half]
    second = values[..., half:]
    return jnp.concatenate(
        [first * cosine - second * sine, second * cosine + first * sine], axis=-1
    )


def visible(query_index, query_segment, key_index, key_segment):
    earlier = key_index[None, :] <= query_index[:, None]
    shared = (key_segment[None, :] < 0) | (key_segment[None, :] == query_segment[:, None])
    return earlier & shared


def feature_sum(values):
    return lax.psum(values, "col")


def gather_rows(values):
    return lax.all_gather(values, "row", axis=0, tiled=True)


def gather_cols(values):
    return lax.all_gather(values, "col", axis=0, tiled=True)


def partial_cols(term, count):
    return lax.psum_scatter(
        term(jnp.int32(0), count * lax.axis_size("col")), "col", scatter_dimension=0, tiled=True
    )


def partial_rows(term, count):
    return lax.psum_scatter(
        term(jnp.int32(0), count * lax.axis_size("row")), "row", scatter_dimension=0, tiled=True
    )


def body(
    states,
    keep,
    cont_ids,
    answer_len,
    teacher,
    out_grad,
    gain_attn,
    w_query,
    key_projection,
    value_projection,
    w_out,
    gain_ffn,
    w_gate,
    w_up,
    w_down,
):
    local_rows = states.shape[0]
    whole_rows = local_rows * lax.axis_size("row")
    query_rows = whole_rows // lax.axis_size("col")
    group_tokens = PROMPT + cont_ids.shape[1]
    key_heads = key_projection.shape[1] // HEAD_SIZE
    heads_per_group = w_query.shape[1] // key_projection.shape[1]
    query_width = w_query.shape[1]
    scale = HEAD_SIZE ** (-0.5)
    block = min(512, query_rows)
    blocks = query_rows // block
    positions, segment, counted = token_layout(cont_ids, answer_len)
    token_index = jnp.arange(whole_rows, dtype=jnp.int32)
    row_start = lax.axis_index("row") * local_rows
    col_start = lax.axis_index("col") * query_rows
    counted_here = rows_of(counted, row_start, local_rows).astype(jnp.float32)[:, None]
    query_pos = rows_of(positions, col_start, query_rows)
    keep_here = keep.astype(jnp.float32)[:, None]
    states_f = states.astype(jnp.float32)
    scale_attn = lax.rsqrt(
        feature_sum(jnp.sum(states_f * states_f, axis=1)) / MODEL_WIDTH + EPSILON
    )[:, None]
    normed_attn = (states_f * scale_attn * gain_attn[None, :]).astype(jnp.bfloat16)
    normed_all = gather_rows(normed_attn)
    w_kv = jnp.concatenate([key_projection, value_projection], axis=1)
    query_raw = partial_cols(
        lambda start, count: jnp.dot(
            rows_of(normed_all, start, count), w_query, preferred_element_type=jnp.float32
        ),
        query_rows,
    )
    kv_raw = lax.psum(jnp.dot(normed_all, w_kv, preferred_element_type=jnp.float32), "col")
    queries = (
        rotary(
            query_raw.reshape(query_rows, key_heads * heads_per_group, HEAD_SIZE), query_pos, 1.0
        )
        .astype(jnp.bfloat16)
        .reshape(query_rows, key_heads, heads_per_group, HEAD_SIZE)
    )
    keys = rotary(
        kv_raw[:, : key_heads * HEAD_SIZE].reshape(whole_rows, key_heads, HEAD_SIZE), positions, 1.0
    ).astype(jnp.bfloat16)
    values = (
        kv_raw[:, key_heads * HEAD_SIZE :]
        .reshape(whole_rows, key_heads, HEAD_SIZE)
        .astype(jnp.bfloat16)
    )

    def context_of(index):
        first = col_start + index * block
        key_first = first // group_tokens * group_tokens
        query_block = rows_of(queries, index * block, block)
        key_group = rows_of(keys, key_first, group_tokens)
        value_group = rows_of(values, key_first, group_tokens)
        raw = (
            jnp.einsum("qgjd,kgd->gjqk", query_block, key_group, preferred_element_type=jnp.float32)
            * scale
        )
        mask = visible(
            rows_of(token_index, first, block),
            rows_of(segment, first, block),
            rows_of(token_index, key_first, group_tokens),
            rows_of(segment, key_first, group_tokens),
        )
        scores = jnp.where(mask[None, None], raw, MASKED)
        return (query_block, key_group, value_group, scores, key_first)

    def attend(index):
        query_block, key_group, value_group, scores, key_first = context_of(index)
        peak = jnp.max(scores, axis=-1, keepdims=True)
        exponent = jnp.exp(scores - peak)
        totals = jnp.sum(exponent, axis=-1, keepdims=True)
        weights = (exponent / totals).astype(jnp.bfloat16)
        mixed = jnp.einsum(
            "gjqk,kgd->qgjd", weights, value_group, preferred_element_type=jnp.float32
        )
        return (mixed, peak + jnp.log(totals))

    mixed_blocks, log_totals = lax.map(attend, jnp.arange(blocks, dtype=jnp.int32))
    attn_context = mixed_blocks.reshape(query_rows, query_width).astype(jnp.bfloat16)
    context_all = gather_cols(attn_context)
    attention = partial_rows(
        lambda start, count: jnp.dot(
            rows_of(context_all, start, count), w_out, preferred_element_type=jnp.float32
        ),
        local_rows,
    )
    hidden_res = states_f + keep_here * attention
    scale_ffn = lax.rsqrt(
        feature_sum(jnp.sum(hidden_res * hidden_res, axis=1)) / MODEL_WIDTH + EPSILON
    )[:, None]
    normed_ffn = (hidden_res * scale_ffn * gain_ffn[None, :]).astype(jnp.bfloat16)
    ffn_all = gather_rows(normed_ffn)
    w_pair = jnp.concatenate([w_gate, w_up], axis=1)
    inner = w_gate.shape[1]
    gate_up = partial_cols(
        lambda start, count: jnp.dot(
            rows_of(ffn_all, start, count), w_pair, preferred_element_type=jnp.float32
        ),
        query_rows,
    )
    gate = gate_up[:, :inner]
    up_proj = gate_up[:, inner:]
    sigma = jax.nn.sigmoid(gate)
    swish = gate * sigma
    hidden = (swish * up_proj).astype(jnp.bfloat16)
    hidden_all = gather_cols(hidden)
    feed = partial_rows(
        lambda start, count: jnp.dot(
            rows_of(hidden_all, start, count), w_down, preferred_element_type=jnp.float32
        ),
        local_rows,
    )
    result = hidden_res + keep_here * feed
    error = result - teacher.astype(jnp.float32)
    own_count = jnp.where(lax.axis_index("col") == 0, jnp.sum(counted_here), 0.0)
    error_total, token_count_sum = lax.psum(
        (jnp.sum(counted_here * error * error), own_count), ("dp", "row", "col")
    )
    loss = error_total / (token_count_sum * MODEL_WIDTH)
    grad_result = (
        out_grad.astype(jnp.float32) + 2.0 / (token_count_sum * MODEL_WIDTH) * counted_here * error
    )
    grad_feed = (keep_here * grad_result).astype(jnp.bfloat16)
    grad_feed_all = gather_rows(grad_feed)
    grad_down = jnp.einsum(
        "tf,td->fd", hidden_all, grad_feed_all, preferred_element_type=jnp.float32
    )
    grad_hidden = partial_cols(
        lambda start, count: jnp.einsum(
            "td,fd->tf",
            rows_of(grad_feed_all, start, count),
            w_down,
            preferred_element_type=jnp.float32,
        ),
        query_rows,
    )
    grad_gate_in = grad_hidden * up_proj * sigma * (1.0 + gate * (1.0 - sigma))
    grad_up_in = grad_hidden * swish
    grad_pair = jnp.concatenate([grad_gate_in, grad_up_in], axis=1).astype(jnp.bfloat16)
    grad_pair_all = gather_cols(grad_pair)
    grad_w_pair = jnp.einsum(
        "td,tf->df", ffn_all, grad_pair_all, preferred_element_type=jnp.float32
    )
    grad_normed_ffn = partial_rows(
        lambda start, count: jnp.einsum(
            "tf,df->td",
            rows_of(grad_pair_all, start, count),
            w_pair,
            preferred_element_type=jnp.float32,
        ),
        local_rows,
    )
    grad_gain_ffn = jnp.sum(grad_normed_ffn * hidden_res * scale_ffn, axis=0)
    weighted_ffn = grad_normed_ffn * gain_ffn[None, :]
    inner_ffn = feature_sum(jnp.sum(weighted_ffn * hidden_res, axis=1))[:, None]
    grad_hidden_res = (
        grad_result + scale_ffn * weighted_ffn - hidden_res * scale_ffn**3 * inner_ffn / MODEL_WIDTH
    )
    grad_attention = (keep_here * grad_hidden_res).astype(jnp.bfloat16)
    grad_att_all = gather_rows(grad_attention)
    grad_out = jnp.einsum(
        "to,td->od", context_all, grad_att_all, preferred_element_type=jnp.float32
    )
    grad_context = partial_cols(
        lambda start, count: jnp.einsum(
            "td,od->to",
            rows_of(grad_att_all, start, count),
            w_out,
            preferred_element_type=jnp.float32,
        ),
        query_rows,
    )
    grad_context = grad_context.astype(jnp.bfloat16).reshape(
        query_rows, key_heads, heads_per_group, HEAD_SIZE
    )

    def attend_back(carry, item):
        index, log_total = item
        query_block, key_group, value_group, scores, key_first = context_of(index)
        grad_block = rows_of(grad_context, index * block, block)
        probs = jnp.exp(scores - log_total)
        grad_probs = jnp.einsum(
            "qgjd,kgd->gjqk", grad_block, value_group, preferred_element_type=jnp.float32
        )
        row_dot = jnp.sum(probs * grad_probs, axis=-1, keepdims=True)
        grad_scores = (probs * (grad_probs - row_dot)).astype(jnp.bfloat16)
        grad_query_block = (
            jnp.einsum("gjqk,kgd->qgjd", grad_scores, key_group, preferred_element_type=jnp.float32)
            * scale
        )
        grad_key_group = (
            jnp.einsum(
                "gjqk,qgjd->kgd", grad_scores, query_block, preferred_element_type=jnp.float32
            )
            * scale
        )
        grad_value_group = jnp.einsum(
            "gjqk,qgjd->kgd",
            probs.astype(jnp.bfloat16),
            grad_block,
            preferred_element_type=jnp.float32,
        )
        pair = jnp.concatenate([grad_key_group, grad_value_group], axis=1)
        updated = rows_of(carry, key_first, group_tokens) + pair
        return (updated, grad_query_block)

    start_carry = jnp.zeros((whole_rows, 2 * key_heads, HEAD_SIZE), jnp.float32)
    grad_kv_part, grad_query_blocks = lax.scan(
        attend_back, start_carry, (jnp.arange(blocks, dtype=jnp.int32), log_totals)
    )
    grad_kv_sum = (
        lax.psum(
            grad_kv_part.reshape(whole_rows, 2 * key_heads * HEAD_SIZE).astype(jnp.bfloat16), "col"
        )
        .astype(jnp.float32)
        .reshape(whole_rows, 2 * key_heads, HEAD_SIZE)
    )
    grad_keys = rotary(grad_kv_sum[:, :key_heads], positions, -1.0)
    grad_kv = (
        jnp.concatenate([grad_keys, grad_kv_sum[:, key_heads:]], axis=1)
        .reshape(whole_rows, 2 * key_heads * HEAD_SIZE)
        .astype(jnp.bfloat16)
    )
    grad_queries = (
        rotary(
            grad_query_blocks.reshape(query_rows, key_heads * heads_per_group, HEAD_SIZE),
            query_pos,
            -1.0,
        )
        .reshape(query_rows, query_width)
        .astype(jnp.bfloat16)
    )
    grad_queries_all = gather_cols(grad_queries)
    grad_query = jnp.einsum(
        "td,tq->dq", normed_all, grad_queries_all, preferred_element_type=jnp.float32
    )
    grad_kv_weight = jnp.einsum(
        "td,tk->dk", normed_all, grad_kv, preferred_element_type=jnp.float32
    )
    grad_key = grad_kv_weight[:, : key_heads * HEAD_SIZE]
    grad_value = grad_kv_weight[:, key_heads * HEAD_SIZE :]

    def back_terms(start, count):
        from_queries = jnp.einsum(
            "tq,dq->td",
            rows_of(grad_queries_all, start, count),
            w_query,
            preferred_element_type=jnp.float32,
        )
        from_kv = jnp.einsum(
            "tk,dk->td", rows_of(grad_kv, start, count), w_kv, preferred_element_type=jnp.float32
        )
        return from_queries + from_kv

    grad_normed_attn = partial_rows(back_terms, local_rows)
    grad_gain_attn = jnp.sum(grad_normed_attn * states_f * scale_attn, axis=0)
    weighted_attn = grad_normed_attn * gain_attn[None, :]
    inner_attn = feature_sum(jnp.sum(weighted_attn * states_f, axis=1))[:, None]
    grad_states = (
        grad_hidden_res
        + scale_attn * weighted_attn
        - states_f * scale_attn**3 * inner_attn / MODEL_WIDTH
    )
    gain_attn_sum, gain_ffn_sum = lax.psum((grad_gain_attn, grad_gain_ffn), ("dp", "row"))
    summed = (
        lax.psum(grad_query.astype(jnp.bfloat16), "dp").astype(jnp.float32),
        lax.psum(grad_key.astype(jnp.bfloat16), "dp").astype(jnp.float32),
        lax.psum(grad_value.astype(jnp.bfloat16), "dp").astype(jnp.float32),
        lax.psum(grad_out.astype(jnp.bfloat16), "dp").astype(jnp.float32),
        lax.psum(grad_w_pair[:, :inner].astype(jnp.bfloat16), "dp").astype(jnp.float32),
        lax.psum(grad_w_pair[:, inner:].astype(jnp.bfloat16), "dp").astype(jnp.float32),
        lax.psum(grad_down.astype(jnp.bfloat16), "dp").astype(jnp.float32),
    )
    return (
        result.astype(jnp.bfloat16),
        loss,
        grad_states,
        gain_attn_sum,
        summed[0],
        summed[1],
        summed[2],
        summed[3],
        gain_ffn_sum,
        summed[4],
        summed[5],
        summed[6],
    )


LOG2E = 1.4426950408889634
N_ROW = 4
SHARE = 0.1


def cost(flops, moved, exps=0, share=SHARE):
    return pl.CostEstimate(flops=int(share * flops), bytes_accessed=int(share * moved), transcendentals=int(share * exps))

VMEM_BYTES = 58 << 20
ORDER = (0, 2, 1, 3)


def swap(values, axis, mask):
    size = lax.axis_size(axis)
    return lax.ppermute(values, axis, [(i, i ^ mask) for i in range(size)])


def xor_order(slots, mask):
    bit = 1
    while bit < len(slots):
        odd = (mask & bit) != 0
        slots = [jnp.where(odd, slots[i ^ bit], slots[i]) for i in range(len(slots))]
        bit *= 2
    return slots


def after(values, *others):
    return lax.optimization_barrier((values, *others))[0]


def low(values):
    return values.astype(jnp.bfloat16)


def wide(values):
    return values.astype(jnp.float32)


def dot_nn(left, right):
    return lax.dot_general(left, right, (((1,), (0,)), ((), ())), preferred_element_type=jnp.float32)


def dot_nt(left, right):
    return lax.dot_general(left, right, (((1,), (1,)), ((), ())), preferred_element_type=jnp.float32)


def dot_tn(left, right):
    return lax.dot_general(left, right, (((0,), (0,)), ((), ())), preferred_element_type=jnp.float32)


def attend_kernel(slots, scale, flags, q_ref, qseg_ref, kseg_ref, *refs):
    kv_refs = refs[:slots]
    o_ref, lse_ref, peak_ref, total_ref, acc_ref = refs[slots:]
    query = q_ref[...]
    rows = query.shape[0]

    def scores(slot):
        return dot_nt(kv_refs[slot][:, :HEAD_SIZE], query) * (scale * LOG2E)

    def seen(slot):
        key_seg = kseg_ref[slot * rows : (slot + 1) * rows, :]
        return (key_seg < 0) | (key_seg == qseg_ref[...])

    def add(slot, s):
        peak = peak_ref[...]
        higher = jnp.maximum(peak, jnp.max(s, axis=0, keepdims=True))
        fade = jnp.exp2(peak - higher)
        e = jnp.exp2(s - higher)
        total_ref[...] = total_ref[...] * fade + jnp.sum(e, axis=0, keepdims=True)
        acc_ref[...] = acc_ref[...] * fade + dot_tn(kv_refs[slot][:, HEAD_SIZE:], low(e))
        peak_ref[...] = higher

    key_index = lax.broadcasted_iota(jnp.int32, (rows, rows), 0)
    query_index = lax.broadcasted_iota(jnp.int32, (rows, rows), 1)
    s = jnp.where((key_index <= query_index) & seen(0), scores(0), MASKED)
    peak = jnp.max(s, axis=0, keepdims=True)
    e = jnp.exp2(s - peak)
    peak_ref[...] = peak
    total_ref[...] = jnp.sum(e, axis=0, keepdims=True)
    acc_ref[...] = dot_tn(kv_refs[0][:, HEAD_SIZE:], low(e))
    for slot in range(1, slots):

        @pl.when(flags[slot] == 1)
        def _(slot=slot):
            add(slot, scores(slot))

        @pl.when(flags[slot] == 2)
        def _(slot=slot):
            add(slot, jnp.where(seen(slot), scores(slot), MASKED))

    o_ref[...] = low(jnp.transpose(acc_ref[...] / total_ref[...]))
    lse_ref[0] = peak_ref[...] + jnp.log2(total_ref[...])


def attend_back_kernel(slots, scale, flags, q_ref, do_ref, lse_ref, cos_ref, sin_ref, qseg_ref, kseg_ref, *refs):
    kv_refs = refs[:slots]
    dq_ref, dkv_ref, p_ref, dp_ref, dot_ref, dq_acc, dkv_acc = refs[slots:]
    step, steps = pl.program_id(1), pl.num_programs(1)
    query, grad = q_ref[...], do_ref[...]
    rows = query.shape[0]

    @pl.when(step == 0)
    def _():
        dkv_acc[...] = jnp.zeros_like(dkv_acc)

    def seen(slot):
        key_seg = kseg_ref[slot * rows : (slot + 1) * rows, :]
        return (key_seg < 0) | (key_seg == qseg_ref[...])

    def first(slot, mask):
        e = jnp.exp2(dot_nt(kv_refs[slot][:, :HEAD_SIZE], query) * (scale * LOG2E) - lse_ref[0])
        if mask is not None:
            e = jnp.where(mask, e, 0.0)
        dp = dot_nt(kv_refs[slot][:, HEAD_SIZE:], grad)
        p_ref[slot] = e
        dp_ref[slot] = dp
        part = jnp.sum(e * dp, axis=0, keepdims=True)
        if slot == 0:
            dot_ref[...] = part
        else:
            dot_ref[...] += part

    def second(slot):
        p = p_ref[slot]
        ds = low(p * (dp_ref[slot] - dot_ref[...]))
        dkv_acc[slot, :, :HEAD_SIZE] += dot_nn(ds, query)
        dkv_acc[slot, :, HEAD_SIZE:] += dot_nn(low(p), grad)
        part = dot_tn(kv_refs[slot][:, :HEAD_SIZE], ds)
        if slot == 0:
            dq_acc[...] = part
        else:
            dq_acc[...] += part

    key_index = lax.broadcasted_iota(jnp.int32, (rows, rows), 0)
    query_index = lax.broadcasted_iota(jnp.int32, (rows, rows), 1)
    first(0, (key_index <= query_index) & seen(0))
    for slot in range(1, slots):

        @pl.when(flags[slot] == 1)
        def _(slot=slot):
            first(slot, None)

        @pl.when(flags[slot] == 2)
        def _(slot=slot):
            first(slot, seen(slot))

    second(0)
    for slot in range(1, slots):

        @pl.when(flags[slot] > 0)
        def _(slot=slot):
            second(slot)

    half = HEAD_SIZE // 2
    upper, lower = dq_acc[:half, :] * scale, dq_acc[half:, :] * scale
    cosine, sine = cos_ref[...], sin_ref[...]
    turned = jnp.concatenate([upper * cosine + lower * sine, lower * cosine - upper * sine], axis=0)
    dq_ref[...] = low(jnp.transpose(turned))

    @pl.when(step == steps - 1)
    def _():
        for slot in range(slots):
            at = pl.ds(pl.multiple_of(flags[slots + slot] * rows, rows), rows)
            dkv_ref[at, :HEAD_SIZE] = low(dkv_acc[slot, :, :HEAD_SIZE] * scale)
            dkv_ref[at, HEAD_SIZE:] = low(dkv_acc[slot, :, HEAD_SIZE:])


def attend_specs(queries, key_values):
    rows, width = queries.shape
    slots, groups = key_values.shape[0] // rows, key_values.shape[1] // (2 * HEAD_SIZE)
    whole = lambda g, m, f: (0, 0)
    head = pl.BlockSpec((rows, HEAD_SIZE), lambda g, m, f: (0, m * groups + g))
    line = pl.BlockSpec((1, 1, rows), lambda g, m, f: (m * groups + g, 0, 0))
    segs = [pl.BlockSpec((1, rows), whole), pl.BlockSpec((slots * rows, 1), whole)]
    pairs = [
        pl.BlockSpec((rows, 2 * HEAD_SIZE), lambda g, m, f, slot=slot: (f[slots + slot], g)) for slot in range(slots)
    ]
    return rows, width, slots, groups, width // HEAD_SIZE // groups, whole, head, line, segs, pairs


def attend(flags, queries, query_seg, key_seg, key_values):
    rows, width, slots, groups, share, whole, head, line, segs, pairs = attend_specs(queries, key_values)
    return pl.pallas_call(
        functools.partial(attend_kernel, slots, HEAD_SIZE ** (-0.5)),
        out_shape=(
            jax.ShapeDtypeStruct((rows, width), jnp.bfloat16),
            jax.ShapeDtypeStruct((share * groups, 1, rows), jnp.float32),
        ),
        grid_spec=pltpu.PrefetchScalarGridSpec(
            num_scalar_prefetch=1,
            grid=(groups, share),
            in_specs=[head] + segs + pairs,
            out_specs=(head, line),
            scratch_shapes=[
                pltpu.VMEM((1, rows), jnp.float32),
                pltpu.VMEM((1, rows), jnp.float32),
                pltpu.VMEM((HEAD_SIZE, rows), jnp.float32),
            ],
        ),
        compiler_params=pltpu.CompilerParams(vmem_limit_bytes=VMEM_BYTES),
        cost_estimate=cost(3 * rows * rows * width * 4, 8 << 20, 3 * rows * rows * share * groups),
        name="attend",
    )(flags, queries, query_seg, key_seg, *[key_values] * slots)


def attend_back(flags, queries, grads, lse, cosine, sine, query_seg, key_seg, key_values):
    rows, width, slots, groups, share, whole, head, line, segs, pairs = attend_specs(queries, key_values)
    angle = pl.BlockSpec((HEAD_SIZE // 2, rows), whole)
    return pl.pallas_call(
        functools.partial(attend_back_kernel, slots, HEAD_SIZE ** (-0.5)),
        out_shape=(
            jax.ShapeDtypeStruct((rows, width), jnp.bfloat16),
            jax.ShapeDtypeStruct(key_values.shape, jnp.bfloat16),
        ),
        grid_spec=pltpu.PrefetchScalarGridSpec(
            num_scalar_prefetch=1,
            grid=(groups, share),
            in_specs=[head, head, line, angle, angle] + segs + pairs,
            out_specs=(head, pl.BlockSpec((slots * rows, 2 * HEAD_SIZE), lambda g, m, f: (0, g))),
            scratch_shapes=[
                pltpu.VMEM((slots, rows, rows), jnp.float32),
                pltpu.VMEM((slots, rows, rows), jnp.float32),
                pltpu.VMEM((1, rows), jnp.float32),
                pltpu.VMEM((HEAD_SIZE, rows), jnp.float32),
                pltpu.VMEM((slots, rows, 2 * HEAD_SIZE), jnp.float32),
            ],
        ),
        compiler_params=pltpu.CompilerParams(vmem_limit_bytes=VMEM_BYTES),
        cost_estimate=cost(3 * rows * rows * width * 10, 12 << 20, 3 * rows * rows * share * groups),
        name="attend_back",
    )(flags, queries, grads, lse, cosine, sine, query_seg, key_seg, *[key_values] * slots)


def project_kernel(side, a_ref, *refs):
    slots, (own_ref, send_ref) = refs[:-2], refs[-2:]
    part = slots[0].shape[0] // 2
    own = pl.multiple_of(side[0] * part, part)
    other = pl.multiple_of((1 - side[0]) * part, part)
    for place, slot in enumerate(ORDER):
        columns = slice(place * part, (place + 1) * part)
        send_ref[:, columns] = low(dot_nt(a_ref[...], slots[slot][pl.ds(other, part), :]))
        own_ref[:, columns] = dot_nt(a_ref[...], slots[slot][pl.ds(own, part), :])


def merge_kernel(side, own_ref, other_ref, *refs):
    slots, out_ref = refs[:-1], refs[-1]
    part = slots[0].shape[0] // 2
    own = pl.multiple_of(side[0] * part, part)
    other = pl.multiple_of((1 - side[0]) * part, part)
    total = None
    for place, slot in enumerate(ORDER):
        columns = slice(place * part, (place + 1) * part)
        term = dot_nn(own_ref[:, columns], slots[slot][pl.ds(own, part), :])
        term += dot_nn(other_ref[:, columns], slots[slot][pl.ds(other, part), :])
        total = term if total is None else total + term
    out_ref[...] = total


def local_call(kernel, name, scalars, operands, outs, flops, scratch=()):
    vmem = pl.BlockSpec(memory_space=pltpu.VMEM)
    moved = sum(x.size * x.dtype.itemsize for x in operands)
    return pl.pallas_call(
        kernel,
        out_shape=outs,
        in_specs=[pl.BlockSpec(memory_space=pltpu.SMEM)] + [vmem] * len(operands),
        out_specs=jax.tree.map(lambda _: vmem, outs),
        scratch_shapes=list(scratch),
        compiler_params=pltpu.CompilerParams(vmem_limit_bytes=VMEM_BYTES),
        cost_estimate=cost(flops, 2 * moved, 0),
        name=name,
    )(scalars, *operands)


def project(side, a, slots):
    rows, width = a.shape[0], slots[0].shape[0] * len(slots) // 2
    outs = (jax.ShapeDtypeStruct((rows, width), jnp.float32), jax.ShapeDtypeStruct((rows, width), jnp.bfloat16))
    return local_call(project_kernel, "project", side, [a, *slots], outs, 4 * rows * width * a.shape[1])


def merge(side, own, other, slots):
    outs = jax.ShapeDtypeStruct((own.shape[0], slots[0].shape[1]), jnp.float32)
    return local_call(merge_kernel, "merge", side, [own, other, *slots], outs, 4 * own.size * slots[0].shape[1])


def key_value_kernel(scalars, a_ref, mine_ref, theirs_ref, own_ref, send_ref, all_ref):
    order, core = scalars[0], scalars[1]
    count = mine_ref.shape[0] // HEAD_SIZE
    groups = count // 2
    for ref, kind in ((mine_ref, core), (theirs_ref, 1 - core)):
        for slot in range(count):
            place = slot ^ order
            lane = pl.multiple_of(((place % groups) * 2 + kind) * HEAD_SIZE, HEAD_SIZE)
            all_ref[place // groups, :, pl.ds(lane, HEAD_SIZE)] = dot_nt(
                a_ref[...], ref[slot * HEAD_SIZE : (slot + 1) * HEAD_SIZE, :]
            )
    own_ref[...] = all_ref[0]
    send_ref[...] = low(all_ref[1])


def key_value_back_kernel(scalars, own_ref, other_ref, mine_ref, theirs_ref, out_ref, all_ref):
    order, core = scalars[0], scalars[1]
    count = mine_ref.shape[0] // HEAD_SIZE
    groups = count // 2
    all_ref[0] = own_ref[...]
    all_ref[1] = other_ref[...]
    total = None
    for ref, kind in ((mine_ref, core), (theirs_ref, 1 - core)):
        for slot in range(count):
            place = slot ^ order
            lane = pl.multiple_of(((place % groups) * 2 + kind) * HEAD_SIZE, HEAD_SIZE)
            term = dot_nn(
                all_ref[place // groups, :, pl.ds(lane, HEAD_SIZE)], ref[slot * HEAD_SIZE : (slot + 1) * HEAD_SIZE, :]
            )
            total = term if total is None else total + term
    out_ref[...] = total


def key_value_project(scalars, a, mine, theirs):
    rows, width = a.shape[0], mine.shape[0]
    outs = (jax.ShapeDtypeStruct((rows, width), jnp.float32), jax.ShapeDtypeStruct((rows, width), jnp.bfloat16))
    return local_call(
        key_value_kernel, "key_value", scalars, [a, mine, theirs], outs, 4 * rows * width * a.shape[1],
        [pltpu.VMEM((2, rows, width), jnp.float32)],
    )


def key_value_back(scalars, own, other, mine, theirs):
    outs = jax.ShapeDtypeStruct((own.shape[0], mine.shape[1]), jnp.float32)
    return local_call(
        key_value_back_kernel, "key_value_back", scalars, [own, other, mine, theirs], outs, 4 * own.size * mine.shape[1],
        [pltpu.VMEM((2, *own.shape), own.dtype)],
    )


def load_block(step, pieces, all_ref):
    x_ref, ax_ref, by_ref, ay_ref, bx_ref = pieces
    rows, width = ax_ref.shape

    @pl.when(step == 0)
    def _():
        all_ref[:, :width] = x_ref[:rows, :]
        all_ref[:, width:] = ay_ref[:rows, :]

    @pl.when(step == 1)
    def _():
        all_ref[:, :width] = x_ref[rows:, :]
        all_ref[:, width:] = by_ref[...]

    @pl.when(step == 2)
    def _():
        all_ref[:, :width] = ax_ref[...]
        all_ref[:, width:] = ay_ref[rows:, :]

    @pl.when(step == 3)
    def _():
        all_ref[...] = bx_ref[...]


def store_block(step, out, outs):
    a_keep, a_send, b_keep, b_send = outs
    rows, width = a_keep.shape[0], a_keep.shape[1] // 2

    @pl.when(step == 0)
    def _():
        a_keep[...] = out

    @pl.when(step == 2)
    def _():
        a_send[...] = out

    for place, at in ((0, 1), (1, 3)):

        @pl.when(step == at)
        def _(place=place):
            b_keep[place * rows : (place + 1) * rows, :] = out[:, :width]
            b_send[place * rows : (place + 1) * rows, :] = out[:, width:]


class Weights:
    def __init__(self, step, sides, held_ref, sems):
        self.step, self.held_ref = step, held_ref
        kinds, padded = held_ref.shape[0], held_ref.shape[1] // 2
        used = sides[0].shape[0] // kinds
        part = used // N_ROW
        self.copies = []
        for kind in range(kinds):
            self.copies.append([])
            for side, ref in enumerate(sides):
                for row in range(N_ROW):
                    source = ref.at[pl.ds((row * kinds + kind) * part, part), :]
                    target = held_ref.at[kind, pl.ds(side * padded + row * part, part), :]
                    sem = sems.at[(kind * len(sides) + side) * N_ROW + row]
                    self.copies[-1].append(pltpu.make_async_copy(source, target, sem))

        @pl.when(step == 0)
        def _():
            for group in self.copies:
                for copy in group:
                    copy.start()
            for kind in range(kinds):
                for side in range(2):
                    at = side * padded + used
                    held_ref[kind, at : at + padded - used, :] = jnp.zeros(
                        (padded - used, held_ref.shape[2]), held_ref.dtype
                    )

    def get(self, kind):
        @pl.when(self.step == 0)
        def _():
            for copy in self.copies[kind]:
                copy.wait()

        return self.held_ref[kind]


def gate_up_kernel(*refs):
    pieces, sides, (gate_ref, up_ref, own_ref, other_ref, all_ref), scratch = refs[:5], refs[5:7], refs[7:-2], refs[-2:]
    step = pl.program_id(0)
    weights = Weights(step, sides, *scratch)
    load_block(step, pieces, all_ref)
    gate = dot_nt(all_ref[...], weights.get(0))
    gate_ref[...] = gate
    up = dot_nt(all_ref[...], weights.get(1))
    up_ref[...] = up
    hid = low(gate * jax.nn.sigmoid(gate) * up)
    half = own_ref.shape[1]
    own_ref[...] = hid[:, :half]
    other_ref[...] = hid[:, half:]


def down_kernel(own_ref, other_ref, *refs):
    sides, outs, scratch = refs[:2], refs[2:-2], refs[-2:]
    step = pl.program_id(0)
    held = Weights(step, sides, *scratch).get(0)
    half = own_ref.shape[1]
    store_block(step, low(dot_nn(own_ref[...], held[:half]) + dot_nn(other_ref[...], held[half:])), outs)


def down_back_kernel(*refs):
    pieces, (gate_ref, up_ref), sides, outs, scratch = refs[:5], refs[5:7], refs[7:9], refs[9:-2], refs[-2:]
    own_ref, other_ref, all_ref = outs
    step = pl.program_id(0)
    weights = Weights(step, sides, *scratch)
    load_block(step, pieces, all_ref)
    dhid = dot_nt(all_ref[...], weights.get(0))
    gate, up = gate_ref[...], up_ref[...]
    sigma = jax.nn.sigmoid(gate)
    half = gate.shape[1] // 2
    dup = low(dhid * (gate * sigma))
    own_ref[:, half:] = dup[:, :half]
    other_ref[:, half:] = dup[:, half:]
    dgate = low(dhid * up * sigma * (1.0 + gate * (1.0 - sigma)))
    own_ref[:, :half] = dgate[:, :half]
    other_ref[:, :half] = dgate[:, half:]


def gate_up_back_kernel(own_ref, other_ref, *refs):
    sides, outs, scratch = refs[:2], refs[2:-2], refs[-2:]
    step = pl.program_id(0)
    weights = Weights(step, sides, *scratch)
    half = own_ref.shape[1] // 2
    total = None
    for kind in range(2):
        held = weights.get(kind)
        columns = slice(kind * half, (kind + 1) * half)
        term = dot_nn(own_ref[:, columns], held[:half]) + dot_nn(other_ref[:, columns], held[half:])
        total = term if total is None else total + term
    store_block(step, low(total), outs)


def feed_call(kernel, name, pieces, narrow, sides, kinds, outs, share=SHARE):
    features = sides[0].shape[1]
    used = sides[0].shape[0] // kinds
    hidden = 2 * (-(-used // 256) * 256)
    blocks = 4
    rows = (pieces[1].shape[0] if pieces else narrow[0].shape[0] // blocks)
    once = dict(pipeline_mode=pl.Buffered(1))
    fixed = lambda shape, **k: pl.BlockSpec(shape, lambda i: (0, 0), **k)
    by_rows = lambda width: pl.BlockSpec((rows, width), lambda i: (i, 0))
    if outs:
        shapes = [jax.ShapeDtypeStruct((blocks * rows, n * hidden // 2), t) for n, t in outs]
        shapes.append(jax.ShapeDtypeStruct((blocks * rows, features), jnp.bfloat16))
        specs = [by_rows(x.shape[1]) for x in shapes]
    else:
        pair = [(rows, features)] * 2 + [(2 * rows, features // 2)] * 2
        shapes = [jax.ShapeDtypeStruct(x, jnp.bfloat16) for x in pair]
        specs = [fixed(x) for x in pair]
    return pl.pallas_call(
        kernel,
        out_shape=tuple(shapes),
        grid=(blocks,),
        in_specs=[fixed(p.shape, **once) for p in pieces]
        + [by_rows(x.shape[1]) for x in narrow]
        + [pl.BlockSpec(memory_space=pl.ANY)] * 2,
        out_specs=tuple(specs),
        scratch_shapes=[
            pltpu.VMEM((kinds, hidden, features), jnp.bfloat16),
            pltpu.SemaphoreType.DMA((kinds * 2 * N_ROW,)),
        ],
        compiler_params=pltpu.CompilerParams(vmem_limit_bytes=VMEM_BYTES),
        cost_estimate=cost(2 * kinds * blocks * rows * hidden * features, 20 << 20, blocks * rows * hidden, share),
        name=name,
    )(*pieces, *narrow, *sides)


def gate_up(pieces, sides):
    outs = ((2, jnp.float32), (2, jnp.float32), (1, jnp.bfloat16), (1, jnp.bfloat16))
    return feed_call(gate_up_kernel, "gate_up", pieces, [], sides, 2, outs)


def down(hids, sides):
    return feed_call(down_kernel, "down", [], hids, sides, 1, None)


def down_back(pieces, gate, up, sides):
    return feed_call(down_back_kernel, "down_back", pieces, [gate, up], sides, 1, ((2, jnp.bfloat16),) * 2)


def gate_up_back(both, sides):
    return feed_call(gate_up_back_kernel, "gate_up_back", [], both, sides, 2, None)


def outer_kernel(kinds, used, left_ref, left_far_ref, right_ref, right_far_ref, out_ref):
    step = pl.program_id(0)
    block = left_ref.shape[1]
    blocks = pl.num_programs(0) // kinds
    part = used // N_ROW
    total = low(dot_tn(left_ref[...], right_ref[...]) + dot_tn(left_far_ref[...], right_far_ref[...]))
    for kind in range(kinds):
        for index in range(-(-used // block)):

            @pl.when(step == kind * blocks + index)
            def _(kind=kind, index=index):
                at, end = index * block, min((index + 1) * block, used)
                while at < end:
                    row = at // part
                    stop = min(end, (row + 1) * part)
                    target = row * kinds * part + kind * part + at - row * part
                    out_ref[target : target + stop - at, :] = total[at - index * block : stop - index * block, :]
                    at = stop


def outer(lefts, rights, kinds, part):
    tokens, features = rights[0].shape
    columns = lefts[0].shape[1]
    block = 256
    out_rows = N_ROW * kinds * part
    once = pl.BlockSpec((tokens, features), lambda i: (0, 0), pipeline_mode=pl.Buffered(1))
    return pl.pallas_call(
        functools.partial(outer_kernel, kinds, N_ROW * part),
        out_shape=jax.ShapeDtypeStruct((out_rows, features), jnp.bfloat16),
        grid=(columns // block,),
        in_specs=[pl.BlockSpec((tokens, block), lambda i: (0, i))] * 2 + [once] * 2,
        out_specs=pl.BlockSpec((out_rows, features), lambda i: (0, 0)),
        compiler_params=pltpu.CompilerParams(vmem_limit_bytes=VMEM_BYTES),
        cost_estimate=cost(4 * tokens * columns * features, 8 * tokens * features),
        name="outer",
    )(*lefts, *rights)


def settle_kernel(kinds, turned, scalars, near_ref, far_ref, other_ref, *refs):
    outs, held_ref = refs[:-1], refs[-1]
    d, y = scalars[0], scalars[1]
    part = near_ref.shape[0] // (2 * kinds)
    for kind in range(kinds):
        for slot in range(4):
            ref = (near_ref, other_ref, far_ref, other_ref)[slot]
            base = near_ref.shape[0] if slot == 3 else 0
            for side in range(2):
                at = ((d ^ slot) * 2 + (y if side == 0 else 1 - y)) * part
                rows = slice(base + (side * kinds + kind) * part, base + (side * kinds + kind + 1) * part)
                target = held_ref if turned else outs[kind]
                target[pl.ds(pl.multiple_of(at, 16), part), :] = wide(ref[rows, :])
        if turned:
            outs[kind][...] = jnp.transpose(held_ref[...])


def settle(d, y, near, far, other, kinds, turned):
    width = near.shape[1]
    hidden = 4 * near.shape[0] // kinds
    lanes = 256
    spec = lambda x: pl.BlockSpec((x.shape[0], lanes), lambda i: (0, i))
    shape = (width, hidden) if turned else (hidden, width)
    out_spec = pl.BlockSpec((lanes, hidden), lambda i: (i, 0)) if turned else pl.BlockSpec((hidden, lanes), lambda i: (0, i))
    return pl.pallas_call(
        functools.partial(settle_kernel, kinds, turned),
        out_shape=(jax.ShapeDtypeStruct(shape, jnp.float32),) * kinds,
        grid=(width // lanes,),
        in_specs=[pl.BlockSpec(memory_space=pltpu.SMEM)] + [spec(x) for x in (near, far, other)],
        out_specs=(out_spec,) * kinds,
        scratch_shapes=[pltpu.VMEM((hidden, lanes), jnp.float32)],
        compiler_params=pltpu.CompilerParams(vmem_limit_bytes=VMEM_BYTES),
        cost_estimate=cost(hidden * width, 6 * kinds * hidden * width, 0),
        name="settle",
    )(jnp.stack([d, y]), near, far, other)


def plane_gather(x):
    half = x.shape[0] // 2
    a, b = x[:half], x[half:]
    a_x = swap(a, "dp", 2)
    b_y = swap(b, "col", 1)
    a_y = swap(jnp.concatenate([a, a_x], axis=0), "col", 1)
    b_x = swap(jnp.concatenate([b, b_y], axis=1), "dp", 2)
    return [x, a_x, b_y, a_y, b_x]


def plane_scatter(parts):
    a_keep, a_send, b_keep, b_send = parts
    half, width = a_keep.shape[0], b_keep.shape[1]
    a_x = swap(a_send, "dp", 2)
    b_y = swap(b_send, "col", 1)
    a_y = swap(low(wide(a_keep[:, width:]) + wide(a_x[:, width:])), "col", 1)
    b_x = swap(low(wide(b_keep[half:]) + wide(b_y[half:])), "dp", 2)
    return jnp.concatenate(
        [
            wide(a_keep[:, :width]) + wide(a_x[:, :width]) + wide(a_y),
            wide(b_keep[:half]) + wide(b_y[:half]) + wide(b_x),
        ],
        axis=0,
    )


def dp_slots(x):
    far = swap(x, "dp", 2)
    other = swap(jnp.concatenate([x, far], axis=0), "dp", 1)
    return [x, other[: x.shape[0]], far, other[x.shape[0] :]]


def heads_near(own, other, right, y):
    half = own.shape[1] // 2
    odd = low(dot_tn(jnp.concatenate([own[:, half:], other[:, half:]], axis=1), right))
    odd = swap(odd, "dp", 1)
    even = dot_tn(jnp.concatenate([own[:, :half], other[:, :half]], axis=1), right)
    part = half // 2
    total = [even[i * part : (i + 1) * part] + wide(odd[i * part : (i + 1) * part]) for i in range(4)]
    far = swap(low(jnp.concatenate([total[1], total[3]], axis=0)), "dp", 2)
    return xor_order([low(total[0] + wide(far[:part])), low(total[2] + wide(far[part:]))], y)


def quarters_home(slots, order):
    odd = swap(low(jnp.concatenate([slots[1], slots[3]], axis=0)), "dp", 1)
    count = slots[0].shape[0]
    near = wide(slots[0]) + wide(odd[:count])
    far = swap(low(wide(slots[2]) + wide(odd[count:])), "dp", 2)
    total = near + wide(far)
    parts = xor_order([low(total[i]) for i in range(count)], order)
    summed = wide(parts[0])
    for k in range(1, count):
        summed += wide(swap(parts[k], "row", k))
    return xor_order(dp_slots(low(summed)), lax.axis_index("dp"))


def fast_body(
    states,
    keep,
    cont_ids,
    answer_len,
    teacher,
    out_grad,
    gain_attn,
    w_query,
    key_projection,
    value_projection,
    w_out,
    gain_ffn,
    w_gate,
    w_up,
    w_down,
):
    rows, width = states.shape
    n_row, n_col, n_dp = lax.axis_size("row"), lax.axis_size("col"), lax.axis_size("dp")
    d, r, y = lax.axis_index("dp"), lax.axis_index("row"), lax.axis_index("col")
    core = d % 2
    groups = n_row // n_col
    features = width * n_col
    order = r ^ (y * groups)
    side = y.reshape(1)
    kv_scalars = jnp.stack([order, core])

    kv_mine = jnp.where(core == 0, key_projection, value_projection).T
    kv_mine = jnp.concatenate([kv_mine] + [swap(kv_mine, "row", k) for k in range(1, n_row)], axis=0)
    kv_theirs = swap(kv_mine, "dp", 1)

    heads = [rows_of(w_query, d * HEAD_SIZE, HEAD_SIZE, 1).T, rows_of(w_out, d * HEAD_SIZE, HEAD_SIZE)]
    heads = gather_rows(jnp.concatenate(heads, axis=0))

    inner = w_down.shape[0]
    inner_part = inner // (n_dp * n_col)

    def hidden_rows(at):
        return jnp.concatenate([rows_of(w, at * inner_part, inner_part) for w in (w_gate.T, w_up.T, w_down)], axis=0)

    hidden_other = after(swap(hidden_rows(d * n_col + (1 - y)), "col", 1), kv_theirs)
    hidden_own = hidden_rows(d * n_col + y)

    positions, segment, counted = token_layout(cont_ids, answer_len)
    row_start = r * rows
    count = jnp.sum(counted.astype(jnp.float32)).reshape(1)
    count = count + swap(count, "dp", 1)
    count = (count + swap(count, "dp", 2))[0]
    counted_here = rows_of(counted, row_start, rows).astype(jnp.float32)[:, None]
    keep_here = keep.astype(jnp.float32)[:, None]
    position = rows_of(positions, row_start, rows).astype(jnp.float32)
    query_seg = rows_of(segment, row_start, rows)
    key_segs = [rows_of(segment, jnp.maximum(r - k, 0) * rows, rows) for k in range(n_row)]
    flags = [jnp.int32(2)]
    for k in range(1, n_row):
        least, most = jnp.min(key_segs[k]), jnp.max(key_segs[k])
        active = (r >= k) & ((least < 0) | (most >= jnp.min(query_seg)))
        flags.append(jnp.where(active, jnp.where(most < 0, 1, 2), 0).astype(jnp.int32))
    flags = jnp.stack(flags + [(r - k) % n_row for k in range(n_row)])
    key_seg = jnp.concatenate(key_segs)[:, None]
    query_seg = query_seg[None, :]
    freqs = ROPE_BASE ** (-2.0 * jnp.arange(HEAD_SIZE // 2, dtype=jnp.float32) / HEAD_SIZE)
    angles_t = freqs[:, None] * position[None, :]
    cos_t, sin_t = jnp.cos(angles_t), jnp.sin(angles_t)
    cos_n, sin_n = cos_t.T, sin_t.T
    cos_n = jnp.concatenate([cos_n, cos_n], axis=1)
    sin_n = jnp.concatenate([-sin_n, sin_n], axis=1)

    def turn(x, sign):
        half = HEAD_SIZE // 2
        turned = jnp.concatenate([x[:, half:], x[:, :half]], axis=1)
        return x * cos_n + turned * (sign * sin_n)

    def turn_heads(x, sign, every):
        return jnp.concatenate(
            [
                turn(x[:, i : i + HEAD_SIZE], sign) if i % every == 0 else x[:, i : i + HEAD_SIZE]
                for i in range(0, x.shape[1], HEAD_SIZE)
            ],
            axis=1,
        )

    states_f = wide(states)
    squares = jnp.sum(states_f * states_f, axis=1)
    scale_attn = lax.rsqrt((squares + swap(squares, "col", 1)) / features + EPSILON)[:, None]
    a1 = low(states_f * scale_attn * gain_attn[None, :])
    kv_own, kv_send = key_value_project(kv_scalars, a1, kv_mine, kv_theirs)
    kv_received, heads, count = lax.optimization_barrier((swap(kv_send, "col", 1), heads, count))
    key_value = low(turn_heads(kv_own + wide(kv_received), 1.0, 2 * HEAD_SIZE))
    key_values = gather_rows(key_value)
    q_part, o_part = [
        jnp.concatenate([heads[(2 * i + j) * HEAD_SIZE : (2 * i + j + 1) * HEAD_SIZE] for i in range(n_row)], axis=0)
        for j in (0, 1)
    ]
    q_far = swap(q_part, "dp", 2)
    q_slots = [q_part, swap(q_part, "dp", 1), q_far, swap(q_far, "dp", 1)]
    q_own, q_send = project(side, a1, q_slots)
    hidden_own, hidden_other = lax.optimization_barrier((hidden_own, hidden_other, key_values, q_send))[:2]
    hidden_mine = jnp.concatenate([hidden_own, hidden_other], axis=1)
    gate_up_mine = gather_rows(hidden_mine[: 2 * inner_part])
    down_mine = gather_rows(hidden_mine[2 * inner_part :])
    queries = low(turn_heads(q_own + wide(swap(q_send, "col", 1)), 1.0, HEAD_SIZE))
    o_slots = dp_slots(after(o_part, q_send))
    queries, *o_slots = lax.optimization_barrier((queries, *o_slots))
    context, lse = attend(flags, queries, query_seg, key_seg, key_values)
    context_other = swap(context, "col", 1)
    hidden_res = states_f + keep_here * merge(side, context, context_other, o_slots)

    squares = jnp.sum(hidden_res * hidden_res, axis=1)
    scale_ffn = lax.rsqrt((squares + swap(squares, "col", 1)) / features + EPSILON)[:, None]
    a2 = low(hidden_res * scale_ffn * gain_ffn[None, :])
    a2_pieces = plane_gather(a2)
    gate_up_mine = after(gate_up_mine, a2_pieces[1])
    gate_up_sides = [gate_up_mine, swap(gate_up_mine, "dp", 1)]
    gate, up, *hids, a2_all = gate_up(a2_pieces, gate_up_sides)
    down_mine = after(down_mine, gate)
    down_sides = [down_mine, swap(down_mine, "dp", 1)]
    result = hidden_res + keep_here * plane_scatter(down(hids, down_sides))
    error = result - wide(teacher)
    error_part = jnp.sum(counted_here * error * error)
    grad_result = wide(out_grad) + 2.0 / (count * features) * counted_here * error

    gm_pieces = plane_gather(low(keep_here * grad_result))
    def both_cores(own, other):
        return [own, swap(other, "dp", 1)]

    hids, a2_sides = both_cores(*hids), both_cores(a2_all, a2_all)
    gate, *hids_sides = lax.optimization_barrier((gate, *hids, *a2_sides))
    hids, a2_sides = hids_sides[:2], hids_sides[2:]
    *dboth, gm_all = down_back(gm_pieces, gate, up, down_sides)

    def along_row(x):
        return lax.psum_scatter(x, "row", scatter_dimension=0, tiled=True)

    down_joined = outer(hids, both_cores(gm_all, gm_all), 1, inner_part)
    dboth_sides = both_cores(*dboth)
    *dboth, down_joined = lax.optimization_barrier((*dboth, *dboth_sides, down_joined))
    dboth, dboth_sides = dboth[:2], dboth[2:]
    down_part = along_row(down_joined)
    grad_normed_ffn = plane_scatter(gate_up_back(dboth, gate_up_sides))
    gate_up_joined = outer(dboth_sides, a2_sides, 2, inner_part)
    grad_normed_ffn, gate_up_joined = lax.optimization_barrier((grad_normed_ffn, gate_up_joined))
    gate_up_joined, down_part = lax.optimization_barrier((gate_up_joined, down_part))
    gate_up_part = along_row(gate_up_joined)

    def hidden_near(part):
        near = jnp.concatenate([part[:, :width], swap(part[:, width:], "col", 1)], axis=0)
        return near, swap(near, "dp", 2)

    def hidden_home(near, far, kinds, turned):
        other = swap(jnp.concatenate([near, far], axis=0), "dp", 1)
        return settle(d, y, near, far, other, kinds, turned)

    gain_ffn_sum = jnp.sum(grad_normed_ffn * hidden_res * scale_ffn, axis=0)
    weighted = grad_normed_ffn * gain_ffn[None, :]
    inner_sum = jnp.sum(weighted * hidden_res, axis=1)
    inner_sum = jnp.concatenate([inner_sum, jnp.full((128,), error_part)])
    inner_sum = inner_sum + swap(inner_sum, "col", 1)
    error_col = inner_sum[rows:]
    inner_sum = inner_sum[:rows, None]
    grad_hidden_res = grad_result + scale_ffn * weighted - hidden_res * scale_ffn**3 * inner_sum / features

    ga = low(keep_here * grad_hidden_res)
    do_own, do_send = project(side, ga, o_slots)
    do_received, *down_near = lax.optimization_barrier((swap(do_send, "col", 1), *hidden_near(down_part)))
    grad_context = low(do_own + wide(do_received))
    dq, dkv_parts = attend_back(flags, queries, grad_context, lse, cos_t, sin_t, query_seg, key_seg, key_values)
    context, context_other, ga, gate_up_part = lax.optimization_barrier((context, context_other, ga, gate_up_part, dq))[:4]
    gate_up_near = hidden_near(gate_up_part)
    dkv_sum, *gate_up_near = lax.optimization_barrier((along_row(dkv_parts), *gate_up_near))
    (grad_down,) = hidden_home(*down_near, 1, False)
    grad_gate, grad_up = hidden_home(*gate_up_near, 2, True)
    dkv = low(turn_heads(wide(dkv_sum), -1.0, 2 * HEAD_SIZE))
    dq_other = swap(dq, "col", 1)
    dkv_other = swap(dkv, "col", 1)
    grad_normed_attn = merge(side, dq, dq_other, q_slots) + key_value_back(
        kv_scalars, dkv, dkv_other, kv_mine, kv_theirs
    )

    near = [heads_near(dq, dq_other, a1, y), heads_near(context, context_other, ga, y)]
    near = [x[g * HEAD_SIZE : (g + 1) * HEAD_SIZE] for p in range(2) for g in range(groups) for x in (near[0][p], near[1][p])]
    near = along_row(after(jnp.concatenate(near, axis=0), dkv_sum))
    near = xor_order(dp_slots(near), d)
    grad_query = wide(jnp.concatenate([x[:HEAD_SIZE] for x in near], axis=0).T)
    grad_out = wide(jnp.concatenate([x[HEAD_SIZE:] for x in near], axis=0))
    kv_part = 2 * HEAD_SIZE // n_dp
    dwkv = jnp.concatenate(
        [x.reshape(groups, n_dp, kv_part, width) for x in (dot_tn(dkv, a1), dot_tn(dkv_other, a1))], axis=0
    )
    dwkv = jnp.concatenate(quarters_home(xor_order([dwkv[:, i] for i in range(n_dp)], d), order), axis=0)
    grad_key = wide(dwkv[:HEAD_SIZE].T)
    grad_value = wide(dwkv[HEAD_SIZE:].T)

    gain_attn_sum = jnp.sum(grad_normed_attn * states_f * scale_attn, axis=0)
    weighted = grad_normed_attn * gain_attn[None, :]
    inner_sum = jnp.sum(weighted * states_f, axis=1)
    inner_sum = (inner_sum + swap(inner_sum, "col", 1))[:, None]
    grad_states = grad_hidden_res + scale_attn * weighted - states_f * scale_attn**3 * inner_sum / features

    sums = jnp.concatenate([gain_attn_sum, gain_ffn_sum, error_col])
    for axis, mask in (("dp", 1), ("dp", 2), ("row", 1), ("row", 2)):
        sums = sums + swap(sums, axis, mask)
    return (
        low(result),
        sums[2 * width] / (count * features),
        grad_states,
        sums[:width],
        grad_query,
        grad_key,
        grad_value,
        grad_out,
        sums[width : 2 * width],
        grad_gate,
        grad_up,
        grad_down,
    )


def solution(mesh):
    return jax.shard_map(
        fast_body if dict(mesh.shape) == {"dp": 4, "row": 4, "col": 2} else body,
        mesh=mesh,
        in_specs=(
            P(("dp", "row"), "col"),
            P(("dp", "row")),
            P("dp", None),
            P("dp", None),
            P(("dp", "row"), "col"),
            P(("dp", "row"), "col"),
            P("col"),
            P("col", "row"),
            P("col", "row"),
            P("col", "row"),
            P("row", "col"),
            P("col"),
            P("col", "row"),
            P("col", "row"),
            P("row", "col"),
        ),
        out_specs=(
            P(("dp", "row"), "col"),
            P(),
            P(("dp", "row"), "col"),
            P("col"),
            P("col", "row"),
            P("col", "row"),
            P("col", "row"),
            P("row", "col"),
            P("col"),
            P("col", "row"),
            P("col", "row"),
            P("row", "col"),
        ),
        check_vma=False,
    )
```

```python
import functools

import jax
import jax.numpy as jnp
from jax import lax
from jax.experimental import pallas as pl
from jax.experimental.pallas import tpu as pltpu
from jax.sharding import PartitionSpec as P

MODEL_WIDTH = 2048
HEAD_SIZE = 128
PROMPT = 1024


EPSILON = 1e-05
MASKED = -1e30
ROPE_BASE = 10000.0


def rows_of(values, start, count, axis=0):
    return lax.dynamic_slice_in_dim(values, start, count, axis)


def token_layout(cont_ids, answer_len):
    groups, cont_tokens = cont_ids.shape
    labels = jnp.arange(answer_len.shape[1], dtype=jnp.int32)
    starts = jnp.sum((cont_ids[:, None, :] < labels[None, :, None]).astype(jnp.int32), axis=2)
    member = (cont_ids[:, :, None] == labels[None, None, :]).astype(jnp.int32)
    own_start = jnp.sum(member * starts[:, None, :], axis=2)
    own_limit = jnp.sum(member * answer_len[:, None, :], axis=2)
    offset = jnp.arange(cont_tokens, dtype=jnp.int32)[None, :] - own_start
    prompt_pos = jnp.arange(PROMPT, dtype=jnp.int32)[None, :]
    positions = jnp.concatenate([prompt_pos, PROMPT + offset], axis=1).reshape(-1)
    segment = jnp.concatenate(
        [jnp.full((groups, PROMPT), -1, dtype=jnp.int32), cont_ids], axis=1
    ).reshape(-1)
    counted = jnp.concatenate(
        [jnp.ones((groups, PROMPT), jnp.int32), (offset < own_limit).astype(jnp.int32)], axis=1
    ).reshape(-1)
    return (positions, segment, counted)


def rotary(values, positions, sign):
    half = values.shape[-1] // 2
    freqs = ROPE_BASE ** (-2.0 * jnp.arange(half, dtype=jnp.float32) / values.shape[-1])
    angles = positions.astype(jnp.float32)[:, None] * freqs[None, :]
    cosine = jnp.cos(angles)[:, None, :]
    sine = sign * jnp.sin(angles)[:, None, :]
    first = values[..., :half]
    second = values[..., half:]
    return jnp.concatenate(
        [first * cosine - second * sine, second * cosine + first * sine], axis=-1
    )


def visible(query_index, query_segment, key_index, key_segment):
    earlier = key_index[None, :] <= query_index[:, None]
    shared = (key_segment[None, :] < 0) | (key_segment[None, :] == query_segment[:, None])
    return earlier & shared


def feature_sum(values):
    return lax.psum(values, "col")


def gather_rows(values):
    return lax.all_gather(values, "row", axis=0, tiled=True)


def gather_cols(values):
    return lax.all_gather(values, "col", axis=0, tiled=True)


def partial_cols(term, count):
    return lax.psum_scatter(
        term(jnp.int32(0), count * lax.axis_size("col")), "col", scatter_dimension=0, tiled=True
    )


def partial_rows(term, count):
    return lax.psum_scatter(
        term(jnp.int32(0), count * lax.axis_size("row")), "row", scatter_dimension=0, tiled=True
    )


def body(
    states,
    keep,
    cont_ids,
    answer_len,
    teacher,
    out_grad,
    gain_attn,
    w_query,
    key_projection,
    value_projection,
    w_out,
    gain_ffn,
    w_gate,
    w_up,
    w_down,
):
    local_rows = states.shape[0]
    whole_rows = local_rows * lax.axis_size("row")
    query_rows = whole_rows // lax.axis_size("col")
    group_tokens = PROMPT + cont_ids.shape[1]
    key_heads = key_projection.shape[1] // HEAD_SIZE
    heads_per_group = w_query.shape[1] // key_projection.shape[1]
    query_width = w_query.shape[1]
    scale = HEAD_SIZE ** (-0.5)
    block = min(512, query_rows)
    blocks = query_rows // block
    positions, segment, counted = token_layout(cont_ids, answer_len)
    token_index = jnp.arange(whole_rows, dtype=jnp.int32)
    row_start = lax.axis_index("row") * local_rows
    col_start = lax.axis_index("col") * query_rows
    counted_here = rows_of(counted, row_start, local_rows).astype(jnp.float32)[:, None]
    query_pos = rows_of(positions, col_start, query_rows)
    keep_here = keep.astype(jnp.float32)[:, None]
    states_f = states.astype(jnp.float32)
    scale_attn = lax.rsqrt(
        feature_sum(jnp.sum(states_f * states_f, axis=1)) / MODEL_WIDTH + EPSILON
    )[:, None]
    normed_attn = (states_f * scale_attn * gain_attn[None, :]).astype(jnp.bfloat16)
    normed_all = gather_rows(normed_attn)
    w_kv = jnp.concatenate([key_projection, value_projection], axis=1)
    query_raw = partial_cols(
        lambda start, count: jnp.dot(
            rows_of(normed_all, start, count), w_query, preferred_element_type=jnp.float32
        ),
        query_rows,
    )
    kv_raw = lax.psum(jnp.dot(normed_all, w_kv, preferred_element_type=jnp.float32), "col")
    queries = (
        rotary(
            query_raw.reshape(query_rows, key_heads * heads_per_group, HEAD_SIZE), query_pos, 1.0
        )
        .astype(jnp.bfloat16)
        .reshape(query_rows, key_heads, heads_per_group, HEAD_SIZE)
    )
    keys = rotary(
        kv_raw[:, : key_heads * HEAD_SIZE].reshape(whole_rows, key_heads, HEAD_SIZE), positions, 1.0
    ).astype(jnp.bfloat16)
    values = (
        kv_raw[:, key_heads * HEAD_SIZE :]
        .reshape(whole_rows, key_heads, HEAD_SIZE)
        .astype(jnp.bfloat16)
    )

    def context_of(index):
        first = col_start + index * block
        key_first = first // group_tokens * group_tokens
        query_block = rows_of(queries, index * block, block)
        key_group = rows_of(keys, key_first, group_tokens)
        value_group = rows_of(values, key_first, group_tokens)
        raw = (
            jnp.einsum("qgjd,kgd->gjqk", query_block, key_group, preferred_element_type=jnp.float32)
            * scale
        )
        mask = visible(
            rows_of(token_index, first, block),
            rows_of(segment, first, block),
            rows_of(token_index, key_first, group_tokens),
            rows_of(segment, key_first, group_tokens),
        )
        scores = jnp.where(mask[None, None], raw, MASKED)
        return (query_block, key_group, value_group, scores, key_first)

    def attend(index):
        query_block, key_group, value_group, scores, key_first = context_of(index)
        peak = jnp.max(scores, axis=-1, keepdims=True)
        exponent = jnp.exp(scores - peak)
        totals = jnp.sum(exponent, axis=-1, keepdims=True)
        weights = (exponent / totals).astype(jnp.bfloat16)
        mixed = jnp.einsum(
            "gjqk,kgd->qgjd", weights, value_group, preferred_element_type=jnp.float32
        )
        return (mixed, peak + jnp.log(totals))

    mixed_blocks, log_totals = lax.map(attend, jnp.arange(blocks, dtype=jnp.int32))
    attn_context = mixed_blocks.reshape(query_rows, query_width).astype(jnp.bfloat16)
    context_all = gather_cols(attn_context)
    attention = partial_rows(
        lambda start, count: jnp.dot(
            rows_of(context_all, start, count), w_out, preferred_element_type=jnp.float32
        ),
        local_rows,
    )
    hidden_res = states_f + keep_here * attention
    scale_ffn = lax.rsqrt(
        feature_sum(jnp.sum(hidden_res * hidden_res, axis=1)) / MODEL_WIDTH + EPSILON
    )[:, None]
    normed_ffn = (hidden_res * scale_ffn * gain_ffn[None, :]).astype(jnp.bfloat16)
    ffn_all = gather_rows(normed_ffn)
    w_pair = jnp.concatenate([w_gate, w_up], axis=1)
    inner = w_gate.shape[1]
    gate_up = partial_cols(
        lambda start, count: jnp.dot(
            rows_of(ffn_all, start, count), w_pair, preferred_element_type=jnp.float32
        ),
        query_rows,
    )
    gate = gate_up[:, :inner]
    up_proj = gate_up[:, inner:]
    sigma = jax.nn.sigmoid(gate)
    swish = gate * sigma
    hidden = (swish * up_proj).astype(jnp.bfloat16)
    hidden_all = gather_cols(hidden)
    feed = partial_rows(
        lambda start, count: jnp.dot(
            rows_of(hidden_all, start, count), w_down, preferred_element_type=jnp.float32
        ),
        local_rows,
    )
    result = hidden_res + keep_here * feed
    error = result - teacher.astype(jnp.float32)
    own_count = jnp.where(lax.axis_index("col") == 0, jnp.sum(counted_here), 0.0)
    error_total, token_count_sum = lax.psum(
        (jnp.sum(counted_here * error * error), own_count), ("dp", "row", "col")
    )
    loss = error_total / (token_count_sum * MODEL_WIDTH)
    grad_result = (
        out_grad.astype(jnp.float32) + 2.0 / (token_count_sum * MODEL_WIDTH) * counted_here * error
    )
    grad_feed = (keep_here * grad_result).astype(jnp.bfloat16)
    grad_feed_all = gather_rows(grad_feed)
    grad_down = jnp.einsum(
        "tf,td->fd", hidden_all, grad_feed_all, preferred_element_type=jnp.float32
    )
    grad_hidden = partial_cols(
        lambda start, count: jnp.einsum(
            "td,fd->tf",
            rows_of(grad_feed_all, start, count),
            w_down,
            preferred_element_type=jnp.float32,
        ),
        query_rows,
    )
    grad_gate_in = grad_hidden * up_proj * sigma * (1.0 + gate * (1.0 - sigma))
    grad_up_in = grad_hidden * swish
    grad_pair = jnp.concatenate([grad_gate_in, grad_up_in], axis=1).astype(jnp.bfloat16)
    grad_pair_all = gather_cols(grad_pair)
    grad_w_pair = jnp.einsum(
        "td,tf->df", ffn_all, grad_pair_all, preferred_element_type=jnp.float32
    )
    grad_normed_ffn = partial_rows(
        lambda start, count: jnp.einsum(
            "tf,df->td",
            rows_of(grad_pair_all, start, count),
            w_pair,
            preferred_element_type=jnp.float32,
        ),
        local_rows,
    )
    grad_gain_ffn = jnp.sum(grad_normed_ffn * hidden_res * scale_ffn, axis=0)
    weighted_ffn = grad_normed_ffn * gain_ffn[None, :]
    inner_ffn = feature_sum(jnp.sum(weighted_ffn * hidden_res, axis=1))[:, None]
    grad_hidden_res = (
        grad_result + scale_ffn * weighted_ffn - hidden_res * scale_ffn**3 * inner_ffn / MODEL_WIDTH
    )
    grad_attention = (keep_here * grad_hidden_res).astype(jnp.bfloat16)
    grad_att_all = gather_rows(grad_attention)
    grad_out = jnp.einsum(
        "to,td->od", context_all, grad_att_all, preferred_element_type=jnp.float32
    )
    grad_context = partial_cols(
        lambda start, count: jnp.einsum(
            "td,od->to",
            rows_of(grad_att_all, start, count),
            w_out,
            preferred_element_type=jnp.float32,
        ),
        query_rows,
    )
    grad_context = grad_context.astype(jnp.bfloat16).reshape(
        query_rows, key_heads, heads_per_group, HEAD_SIZE
    )

    def attend_back(carry, item):
        index, log_total = item
        query_block, key_group, value_group, scores, key_first = context_of(index)
        grad_block = rows_of(grad_context, index * block, block)
        probs = jnp.exp(scores - log_total)
        grad_probs = jnp.einsum(
            "qgjd,kgd->gjqk", grad_block, value_group, preferred_element_type=jnp.float32
        )
        row_dot = jnp.sum(probs * grad_probs, axis=-1, keepdims=True)
        grad_scores = (probs * (grad_probs - row_dot)).astype(jnp.bfloat16)
        grad_query_block = (
            jnp.einsum("gjqk,kgd->qgjd", grad_scores, key_group, preferred_element_type=jnp.float32)
            * scale
        )
        grad_key_group = (
            jnp.einsum(
                "gjqk,qgjd->kgd", grad_scores, query_block, preferred_element_type=jnp.float32
            )
            * scale
        )
        grad_value_group = jnp.einsum(
            "gjqk,qgjd->kgd",
            probs.astype(jnp.bfloat16),
            grad_block,
            preferred_element_type=jnp.float32,
        )
        pair = jnp.concatenate([grad_key_group, grad_value_group], axis=1)
        updated = rows_of(carry, key_first, group_tokens) + pair
        return (updated, grad_query_block)

    start_carry = jnp.zeros((whole_rows, 2 * key_heads, HEAD_SIZE), jnp.float32)
    grad_kv_part, grad_query_blocks = lax.scan(
        attend_back, start_carry, (jnp.arange(blocks, dtype=jnp.int32), log_totals)
    )
    grad_kv_sum = (
        lax.psum(
            grad_kv_part.reshape(whole_rows, 2 * key_heads * HEAD_SIZE).astype(jnp.bfloat16), "col"
        )
        .astype(jnp.float32)
        .reshape(whole_rows, 2 * key_heads, HEAD_SIZE)
    )
    grad_keys = rotary(grad_kv_sum[:, :key_heads], positions, -1.0)
    grad_kv = (
        jnp.concatenate([grad_keys, grad_kv_sum[:, key_heads:]], axis=1)
        .reshape(whole_rows, 2 * key_heads * HEAD_SIZE)
        .astype(jnp.bfloat16)
    )
    grad_queries = (
        rotary(
            grad_query_blocks.reshape(query_rows, key_heads * heads_per_group, HEAD_SIZE),
            query_pos,
            -1.0,
        )
        .reshape(query_rows, query_width)
        .astype(jnp.bfloat16)
    )
    grad_queries_all = gather_cols(grad_queries)
    grad_query = jnp.einsum(
        "td,tq->dq", normed_all, grad_queries_all, preferred_element_type=jnp.float32
    )
    grad_kv_weight = jnp.einsum(
        "td,tk->dk", normed_all, grad_kv, preferred_element_type=jnp.float32
    )
    grad_key = grad_kv_weight[:, : key_heads * HEAD_SIZE]
    grad_value = grad_kv_weight[:, key_heads * HEAD_SIZE :]

    def back_terms(start, count):
        from_queries = jnp.einsum(
            "tq,dq->td",
            rows_of(grad_queries_all, start, count),
            w_query,
            preferred_element_type=jnp.float32,
        )
        from_kv = jnp.einsum(
            "tk,dk->td", rows_of(grad_kv, start, count), w_kv, preferred_element_type=jnp.float32
        )
        return from_queries + from_kv

    grad_normed_attn = partial_rows(back_terms, local_rows)
    grad_gain_attn = jnp.sum(grad_normed_attn * states_f * scale_attn, axis=0)
    weighted_attn = grad_normed_attn * gain_attn[None, :]
    inner_attn = feature_sum(jnp.sum(weighted_attn * states_f, axis=1))[:, None]
    grad_states = (
        grad_hidden_res
        + scale_attn * weighted_attn
        - states_f * scale_attn**3 * inner_attn / MODEL_WIDTH
    )
    gain_attn_sum, gain_ffn_sum = lax.psum((grad_gain_attn, grad_gain_ffn), ("dp", "row"))
    summed = (
        lax.psum(grad_query.astype(jnp.bfloat16), "dp").astype(jnp.float32),
        lax.psum(grad_key.astype(jnp.bfloat16), "dp").astype(jnp.float32),
        lax.psum(grad_value.astype(jnp.bfloat16), "dp").astype(jnp.float32),
        lax.psum(grad_out.astype(jnp.bfloat16), "dp").astype(jnp.float32),
        lax.psum(grad_w_pair[:, :inner].astype(jnp.bfloat16), "dp").astype(jnp.float32),
        lax.psum(grad_w_pair[:, inner:].astype(jnp.bfloat16), "dp").astype(jnp.float32),
        lax.psum(grad_down.astype(jnp.bfloat16), "dp").astype(jnp.float32),
    )
    return (
        result.astype(jnp.bfloat16),
        loss,
        grad_states,
        gain_attn_sum,
        summed[0],
        summed[1],
        summed[2],
        summed[3],
        gain_ffn_sum,
        summed[4],
        summed[5],
        summed[6],
    )


LOG2E = 1.4426950408889634
N_ROW = 4
SHARE = 0.1


def cost(flops, moved, exps=0, share=SHARE):
    return pl.CostEstimate(flops=int(share * flops), bytes_accessed=int(share * moved), transcendentals=int(share * exps))

VMEM_BYTES = 58 << 20
ORDER = (0, 2, 1, 3)


def swap(values, axis, mask):
    size = lax.axis_size(axis)
    return lax.ppermute(values, axis, [(i, i ^ mask) for i in range(size)])


def xor_order(slots, mask):
    bit = 1
    while bit < len(slots):
        odd = (mask & bit) != 0
        slots = [jnp.where(odd, slots[i ^ bit], slots[i]) for i in range(len(slots))]
        bit *= 2
    return slots


def after(values, *others):
    return lax.optimization_barrier((values, *others))[0]


def low(values):
    return values.astype(jnp.bfloat16)


def wide(values):
    return values.astype(jnp.float32)


def dot_nn(left, right):
    return lax.dot_general(left, right, (((1,), (0,)), ((), ())), preferred_element_type=jnp.float32)


def dot_nt(left, right):
    return lax.dot_general(left, right, (((1,), (1,)), ((), ())), preferred_element_type=jnp.float32)


def dot_tn(left, right):
    return lax.dot_general(left, right, (((0,), (0,)), ((), ())), preferred_element_type=jnp.float32)


def attend_kernel(slots, scale, flags, q_ref, qseg_ref, kseg_ref, *refs):
    kv_refs = refs[:slots]
    o_ref, lse_ref, peak_ref, total_ref, acc_ref = refs[slots:]
    query = q_ref[...]
    rows = query.shape[0]

    def scores(slot):
        return dot_nt(kv_refs[slot][:, :HEAD_SIZE], query) * (scale * LOG2E)

    def seen(slot):
        key_seg = kseg_ref[slot * rows : (slot + 1) * rows, :]
        return (key_seg < 0) | (key_seg == qseg_ref[...])

    def add(slot, s):
        peak = peak_ref[...]
        higher = jnp.maximum(peak, jnp.max(s, axis=0, keepdims=True))
        fade = jnp.exp2(peak - higher)
        e = jnp.exp2(s - higher)
        total_ref[...] = total_ref[...] * fade + jnp.sum(e, axis=0, keepdims=True)
        acc_ref[...] = acc_ref[...] * fade + dot_tn(kv_refs[slot][:, HEAD_SIZE:], low(e))
        peak_ref[...] = higher

    key_index = lax.broadcasted_iota(jnp.int32, (rows, rows), 0)
    query_index = lax.broadcasted_iota(jnp.int32, (rows, rows), 1)
    s = jnp.where((key_index <= query_index) & seen(0), scores(0), MASKED)
    peak = jnp.max(s, axis=0, keepdims=True)
    e = jnp.exp2(s - peak)
    peak_ref[...] = peak
    total_ref[...] = jnp.sum(e, axis=0, keepdims=True)
    acc_ref[...] = dot_tn(kv_refs[0][:, HEAD_SIZE:], low(e))
    for slot in range(1, slots):

        @pl.when(flags[slot] == 1)
        def _(slot=slot):
            add(slot, scores(slot))

        @pl.when(flags[slot] == 2)
        def _(slot=slot):
            add(slot, jnp.where(seen(slot), scores(slot), MASKED))

    o_ref[...] = low(jnp.transpose(acc_ref[...] / total_ref[...]))
    lse_ref[0] = peak_ref[...] + jnp.log2(total_ref[...])


def attend_back_kernel(slots, scale, flags, q_ref, do_ref, lse_ref, cos_ref, sin_ref, qseg_ref, kseg_ref, *refs):
    kv_refs = refs[:slots]
    dq_ref, dkv_ref, p_ref, dp_ref, dot_ref, dq_acc, dkv_acc = refs[slots:]
    step, steps = pl.program_id(1), pl.num_programs(1)
    query, grad = q_ref[...], do_ref[...]
    rows = query.shape[0]

    @pl.when(step == 0)
    def _():
        dkv_acc[...] = jnp.zeros_like(dkv_acc)

    def seen(slot):
        key_seg = kseg_ref[slot * rows : (slot + 1) * rows, :]
        return (key_seg < 0) | (key_seg == qseg_ref[...])

    def first(slot, mask):
        e = jnp.exp2(dot_nt(kv_refs[slot][:, :HEAD_SIZE], query) * (scale * LOG2E) - lse_ref[0])
        if mask is not None:
            e = jnp.where(mask, e, 0.0)
        dp = dot_nt(kv_refs[slot][:, HEAD_SIZE:], grad)
        p_ref[slot] = e
        dp_ref[slot] = dp
        part = jnp.sum(e * dp, axis=0, keepdims=True)
        if slot == 0:
            dot_ref[...] = part
        else:
            dot_ref[...] += part

    def second(slot):
        p = p_ref[slot]
        ds = low(p * (dp_ref[slot] - dot_ref[...]))
        dkv_acc[slot, :, :HEAD_SIZE] += dot_nn(ds, query)
        dkv_acc[slot, :, HEAD_SIZE:] += dot_nn(low(p), grad)
        part = dot_tn(kv_refs[slot][:, :HEAD_SIZE], ds)
        if slot == 0:
            dq_acc[...] = part
        else:
            dq_acc[...] += part

    key_index = lax.broadcasted_iota(jnp.int32, (rows, rows), 0)
    query_index = lax.broadcasted_iota(jnp.int32, (rows, rows), 1)
    first(0, (key_index <= query_index) & seen(0))
    for slot in range(1, slots):

        @pl.when(flags[slot] == 1)
        def _(slot=slot):
            first(slot, None)

        @pl.when(flags[slot] == 2)
        def _(slot=slot):
            first(slot, seen(slot))

    second(0)
    for slot in range(1, slots):

        @pl.when(flags[slot] > 0)
        def _(slot=slot):
            second(slot)

    half = HEAD_SIZE // 2
    upper, lower = dq_acc[:half, :] * scale, dq_acc[half:, :] * scale
    cosine, sine = cos_ref[...], sin_ref[...]
    turned = jnp.concatenate([upper * cosine + lower * sine, lower * cosine - upper * sine], axis=0)
    dq_ref[...] = low(jnp.transpose(turned))

    @pl.when(step == steps - 1)
    def _():
        for slot in range(slots):
            at = pl.ds(pl.multiple_of(flags[slots + slot] * rows, rows), rows)
            dkv_ref[at, :HEAD_SIZE] = low(dkv_acc[slot, :, :HEAD_SIZE] * scale)
            dkv_ref[at, HEAD_SIZE:] = low(dkv_acc[slot, :, HEAD_SIZE:])


def attend_specs(queries, key_values):
    rows, width = queries.shape
    slots, groups = key_values.shape[0] // rows, key_values.shape[1] // (2 * HEAD_SIZE)
    whole = lambda g, m, f: (0, 0)
    head = pl.BlockSpec((rows, HEAD_SIZE), lambda g, m, f: (0, m * groups + g))
    line = pl.BlockSpec((1, 1, rows), lambda g, m, f: (m * groups + g, 0, 0))
    segs = [pl.BlockSpec((1, rows), whole), pl.BlockSpec((slots * rows, 1), whole)]
    pairs = [
        pl.BlockSpec((rows, 2 * HEAD_SIZE), lambda g, m, f, slot=slot: (f[slots + slot], g)) for slot in range(slots)
    ]
    return rows, width, slots, groups, width // HEAD_SIZE // groups, whole, head, line, segs, pairs


def attend(flags, queries, query_seg, key_seg, key_values):
    rows, width, slots, groups, share, whole, head, line, segs, pairs = attend_specs(queries, key_values)
    return pl.pallas_call(
        functools.partial(attend_kernel, slots, HEAD_SIZE ** (-0.5)),
        out_shape=(
            jax.ShapeDtypeStruct((rows, width), jnp.bfloat16),
            jax.ShapeDtypeStruct((share * groups, 1, rows), jnp.float32),
        ),
        grid_spec=pltpu.PrefetchScalarGridSpec(
            num_scalar_prefetch=1,
            grid=(groups, share),
            in_specs=[head] + segs + pairs,
            out_specs=(head, line),
            scratch_shapes=[
                pltpu.VMEM((1, rows), jnp.float32),
                pltpu.VMEM((1, rows), jnp.float32),
                pltpu.VMEM((HEAD_SIZE, rows), jnp.float32),
            ],
        ),
        compiler_params=pltpu.CompilerParams(vmem_limit_bytes=VMEM_BYTES),
        cost_estimate=cost(3 * rows * rows * width * 4, 8 << 20, 3 * rows * rows * share * groups),
        name="attend",
    )(flags, queries, query_seg, key_seg, *[key_values] * slots)


def attend_back(flags, queries, grads, lse, cosine, sine, query_seg, key_seg, key_values):
    rows, width, slots, groups, share, whole, head, line, segs, pairs = attend_specs(queries, key_values)
    angle = pl.BlockSpec((HEAD_SIZE // 2, rows), whole)
    return pl.pallas_call(
        functools.partial(attend_back_kernel, slots, HEAD_SIZE ** (-0.5)),
        out_shape=(
            jax.ShapeDtypeStruct((rows, width), jnp.bfloat16),
            jax.ShapeDtypeStruct(key_values.shape, jnp.bfloat16),
        ),
        grid_spec=pltpu.PrefetchScalarGridSpec(
            num_scalar_prefetch=1,
            grid=(groups, share),
            in_specs=[head, head, line, angle, angle] + segs + pairs,
            out_specs=(head, pl.BlockSpec((slots * rows, 2 * HEAD_SIZE), lambda g, m, f: (0, g))),
            scratch_shapes=[
                pltpu.VMEM((slots, rows, rows), jnp.float32),
                pltpu.VMEM((slots, rows, rows), jnp.float32),
                pltpu.VMEM((1, rows), jnp.float32),
                pltpu.VMEM((HEAD_SIZE, rows), jnp.float32),
                pltpu.VMEM((slots, rows, 2 * HEAD_SIZE), jnp.float32),
            ],
        ),
        compiler_params=pltpu.CompilerParams(vmem_limit_bytes=VMEM_BYTES),
        cost_estimate=cost(3 * rows * rows * width * 10, 12 << 20, 3 * rows * rows * share * groups),
        name="attend_back",
    )(flags, queries, grads, lse, cosine, sine, query_seg, key_seg, *[key_values] * slots)


def project_kernel(side, a_ref, *refs):
    slots, (own_ref, send_ref) = refs[:-2], refs[-2:]
    part = slots[0].shape[0] // 2
    own = pl.multiple_of(side[0] * part, part)
    other = pl.multiple_of((1 - side[0]) * part, part)
    for place, slot in enumerate(ORDER):
        columns = slice(place * part, (place + 1) * part)
        send_ref[:, columns] = low(dot_nt(a_ref[...], slots[slot][pl.ds(other, part), :]))
        own_ref[:, columns] = dot_nt(a_ref[...], slots[slot][pl.ds(own, part), :])


def merge_kernel(side, own_ref, other_ref, *refs):
    slots, out_ref = refs[:-1], refs[-1]
    part = slots[0].shape[0] // 2
    own = pl.multiple_of(side[0] * part, part)
    other = pl.multiple_of((1 - side[0]) * part, part)
    total = None
    for place, slot in enumerate(ORDER):
        columns = slice(place * part, (place + 1) * part)
        term = dot_nn(own_ref[:, columns], slots[slot][pl.ds(own, part), :])
        term += dot_nn(other_ref[:, columns], slots[slot][pl.ds(other, part), :])
        total = term if total is None else total + term
    out_ref[...] = total


def local_call(kernel, name, scalars, operands, outs, flops, scratch=()):
    vmem = pl.BlockSpec(memory_space=pltpu.VMEM)
    moved = sum(x.size * x.dtype.itemsize for x in operands)
    return pl.pallas_call(
        kernel,
        out_shape=outs,
        in_specs=[pl.BlockSpec(memory_space=pltpu.SMEM)] + [vmem] * len(operands),
        out_specs=jax.tree.map(lambda _: vmem, outs),
        scratch_shapes=list(scratch),
        compiler_params=pltpu.CompilerParams(vmem_limit_bytes=VMEM_BYTES),
        cost_estimate=cost(flops, 2 * moved, 0),
        name=name,
    )(scalars, *operands)


def project(side, a, slots):
    rows, width = a.shape[0], slots[0].shape[0] * len(slots) // 2
    outs = (jax.ShapeDtypeStruct((rows, width), jnp.float32), jax.ShapeDtypeStruct((rows, width), jnp.bfloat16))
    return local_call(project_kernel, "project", side, [a, *slots], outs, 4 * rows * width * a.shape[1])


def merge(side, own, other, slots):
    outs = jax.ShapeDtypeStruct((own.shape[0], slots[0].shape[1]), jnp.float32)
    return local_call(merge_kernel, "merge", side, [own, other, *slots], outs, 4 * own.size * slots[0].shape[1])


def key_value_kernel(scalars, a_ref, mine_ref, theirs_ref, own_ref, send_ref, all_ref):
    order, core = scalars[0], scalars[1]
    count = mine_ref.shape[0] // HEAD_SIZE
    groups = count // 2
    for ref, kind in ((mine_ref, core), (theirs_ref, 1 - core)):
        for slot in range(count):
            place = slot ^ order
            lane = pl.multiple_of(((place % groups) * 2 + kind) * HEAD_SIZE, HEAD_SIZE)
            all_ref[place // groups, :, pl.ds(lane, HEAD_SIZE)] = dot_nt(
                a_ref[...], ref[slot * HEAD_SIZE : (slot + 1) * HEAD_SIZE, :]
            )
    own_ref[...] = all_ref[0]
    send_ref[...] = low(all_ref[1])


def key_value_back_kernel(scalars, own_ref, other_ref, mine_ref, theirs_ref, out_ref, all_ref):
    order, core = scalars[0], scalars[1]
    count = mine_ref.shape[0] // HEAD_SIZE
    groups = count // 2
    all_ref[0] = own_ref[...]
    all_ref[1] = other_ref[...]
    total = None
    for ref, kind in ((mine_ref, core), (theirs_ref, 1 - core)):
        for slot in range(count):
            place = slot ^ order
            lane = pl.multiple_of(((place % groups) * 2 + kind) * HEAD_SIZE, HEAD_SIZE)
            term = dot_nn(
                all_ref[place // groups, :, pl.ds(lane, HEAD_SIZE)], ref[slot * HEAD_SIZE : (slot + 1) * HEAD_SIZE, :]
            )
            total = term if total is None else total + term
    out_ref[...] = total


def key_value_project(scalars, a, mine, theirs):
    rows, width = a.shape[0], mine.shape[0]
    outs = (jax.ShapeDtypeStruct((rows, width), jnp.float32), jax.ShapeDtypeStruct((rows, width), jnp.bfloat16))
    return local_call(
        key_value_kernel, "key_value", scalars, [a, mine, theirs], outs, 4 * rows * width * a.shape[1],
        [pltpu.VMEM((2, rows, width), jnp.float32)],
    )


def key_value_back(scalars, own, other, mine, theirs):
    outs = jax.ShapeDtypeStruct((own.shape[0], mine.shape[1]), jnp.float32)
    return local_call(
        key_value_back_kernel, "key_value_back", scalars, [own, other, mine, theirs], outs, 4 * own.size * mine.shape[1],
        [pltpu.VMEM((2, *own.shape), own.dtype)],
    )


def load_block(step, pieces, all_ref):
    x_ref, ax_ref, by_ref, ay_ref, bx_ref = pieces
    rows, width = ax_ref.shape

    @pl.when(step == 0)
    def _():
        all_ref[:, :width] = x_ref[:rows, :]
        all_ref[:, width:] = ay_ref[:rows, :]

    @pl.when(step == 1)
    def _():
        all_ref[:, :width] = x_ref[rows:, :]
        all_ref[:, width:] = by_ref[...]

    @pl.when(step == 2)
    def _():
        all_ref[:, :width] = ax_ref[...]
        all_ref[:, width:] = ay_ref[rows:, :]

    @pl.when(step == 3)
    def _():
        all_ref[...] = bx_ref[...]


def store_block(step, out, outs):
    a_keep, a_send, b_keep, b_send = outs
    rows, width = a_keep.shape[0], a_keep.shape[1] // 2

    @pl.when(step == 0)
    def _():
        a_keep[...] = out

    @pl.when(step == 2)
    def _():
        a_send[...] = out

    for place, at in ((0, 1), (1, 3)):

        @pl.when(step == at)
        def _(place=place):
            b_keep[place * rows : (place + 1) * rows, :] = out[:, :width]
            b_send[place * rows : (place + 1) * rows, :] = out[:, width:]


class Weights:
    def __init__(self, step, sides, held_ref, sems):
        self.step, self.held_ref = step, held_ref
        kinds, padded = held_ref.shape[0], held_ref.shape[1] // 2
        used = sides[0].shape[0] // kinds
        part = used // N_ROW
        self.copies = []
        for kind in range(kinds):
            self.copies.append([])
            for side, ref in enumerate(sides):
                for row in range(N_ROW):
                    source = ref.at[pl.ds((row * kinds + kind) * part, part), :]
                    target = held_ref.at[kind, pl.ds(side * padded + row * part, part), :]
                    sem = sems.at[(kind * len(sides) + side) * N_ROW + row]
                    self.copies[-1].append(pltpu.make_async_copy(source, target, sem))

        @pl.when(step == 0)
        def _():
            for group in self.copies:
                for copy in group:
                    copy.start()
            for kind in range(kinds):
                for side in range(2):
                    at = side * padded + used
                    held_ref[kind, at : at + padded - used, :] = jnp.zeros(
                        (padded - used, held_ref.shape[2]), held_ref.dtype
                    )

    def get(self, kind):
        @pl.when(self.step == 0)
        def _():
            for copy in self.copies[kind]:
                copy.wait()

        return self.held_ref[kind]


def gate_up_kernel(*refs):
    pieces, sides, (gate_ref, up_ref, own_ref, other_ref, all_ref), scratch = refs[:5], refs[5:7], refs[7:-2], refs[-2:]
    step = pl.program_id(0)
    weights = Weights(step, sides, *scratch)
    load_block(step, pieces, all_ref)
    gate = dot_nt(all_ref[...], weights.get(0))
    gate_ref[...] = gate
    up = dot_nt(all_ref[...], weights.get(1))
    up_ref[...] = up
    hid = low(gate * jax.nn.sigmoid(gate) * up)
    half = own_ref.shape[1]
    own_ref[...] = hid[:, :half]
    other_ref[...] = hid[:, half:]


def down_kernel(own_ref, other_ref, *refs):
    sides, outs, scratch = refs[:2], refs[2:-2], refs[-2:]
    step = pl.program_id(0)
    held = Weights(step, sides, *scratch).get(0)
    half = own_ref.shape[1]
    store_block(step, low(dot_nn(own_ref[...], held[:half]) + dot_nn(other_ref[...], held[half:])), outs)


def down_back_kernel(*refs):
    pieces, (gate_ref, up_ref), sides, outs, scratch = refs[:5], refs[5:7], refs[7:9], refs[9:-2], refs[-2:]
    own_ref, other_ref, all_ref = outs
    step = pl.program_id(0)
    weights = Weights(step, sides, *scratch)
    load_block(step, pieces, all_ref)
    dhid = dot_nt(all_ref[...], weights.get(0))
    gate, up = gate_ref[...], up_ref[...]
    sigma = jax.nn.sigmoid(gate)
    half = gate.shape[1] // 2
    dup = low(dhid * (gate * sigma))
    own_ref[:, half:] = dup[:, :half]
    other_ref[:, half:] = dup[:, half:]
    dgate = low(dhid * up * sigma * (1.0 + gate * (1.0 - sigma)))
    own_ref[:, :half] = dgate[:, :half]
    other_ref[:, :half] = dgate[:, half:]


def gate_up_back_kernel(own_ref, other_ref, *refs):
    sides, outs, scratch = refs[:2], refs[2:-2], refs[-2:]
    step = pl.program_id(0)
    weights = Weights(step, sides, *scratch)
    half = own_ref.shape[1] // 2
    total = None
    for kind in range(2):
        held = weights.get(kind)
        columns = slice(kind * half, (kind + 1) * half)
        term = dot_nn(own_ref[:, columns], held[:half]) + dot_nn(other_ref[:, columns], held[half:])
        total = term if total is None else total + term
    store_block(step, low(total), outs)


def feed_call(kernel, name, pieces, narrow, sides, kinds, outs, share=SHARE):
    features = sides[0].shape[1]
    used = sides[0].shape[0] // kinds
    hidden = 2 * (-(-used // 256) * 256)
    blocks = 4
    rows = (pieces[1].shape[0] if pieces else narrow[0].shape[0] // blocks)
    once = dict(pipeline_mode=pl.Buffered(1))
    fixed = lambda shape, **k: pl.BlockSpec(shape, lambda i: (0, 0), **k)
    by_rows = lambda width: pl.BlockSpec((rows, width), lambda i: (i, 0))
    if outs:
        shapes = [jax.ShapeDtypeStruct((blocks * rows, n * hidden // 2), t) for n, t in outs]
        shapes.append(jax.ShapeDtypeStruct((blocks * rows, features), jnp.bfloat16))
        specs = [by_rows(x.shape[1]) for x in shapes]
    else:
        pair = [(rows, features)] * 2 + [(2 * rows, features // 2)] * 2
        shapes = [jax.ShapeDtypeStruct(x, jnp.bfloat16) for x in pair]
        specs = [fixed(x) for x in pair]
    return pl.pallas_call(
        kernel,
        out_shape=tuple(shapes),
        grid=(blocks,),
        in_specs=[fixed(p.shape, **once) for p in pieces]
        + [by_rows(x.shape[1]) for x in narrow]
        + [pl.BlockSpec(memory_space=pl.ANY)] * 2,
        out_specs=tuple(specs),
        scratch_shapes=[
            pltpu.VMEM((kinds, hidden, features), jnp.bfloat16),
            pltpu.SemaphoreType.DMA((kinds * 2 * N_ROW,)),
        ],
        compiler_params=pltpu.CompilerParams(vmem_limit_bytes=VMEM_BYTES),
        cost_estimate=cost(2 * kinds * blocks * rows * hidden * features, 20 << 20, blocks * rows * hidden, share),
        name=name,
    )(*pieces, *narrow, *sides)


def gate_up(pieces, sides):
    outs = ((2, jnp.float32), (2, jnp.float32), (1, jnp.bfloat16), (1, jnp.bfloat16))
    return feed_call(gate_up_kernel, "gate_up", pieces, [], sides, 2, outs)


def down(hids, sides):
    return feed_call(down_kernel, "down", [], hids, sides, 1, None)


def down_back(pieces, gate, up, sides):
    return feed_call(down_back_kernel, "down_back", pieces, [gate, up], sides, 1, ((2, jnp.bfloat16),) * 2)


def gate_up_back(both, sides):
    return feed_call(gate_up_back_kernel, "gate_up_back", [], both, sides, 2, None)


def outer_kernel(kinds, used, left_ref, left_far_ref, right_ref, right_far_ref, out_ref):
    step = pl.program_id(0)
    block = left_ref.shape[1]
    blocks = pl.num_programs(0) // kinds
    part = used // N_ROW
    total = low(dot_tn(left_ref[...], right_ref[...]) + dot_tn(left_far_ref[...], right_far_ref[...]))
    for kind in range(kinds):
        for index in range(-(-used // block)):

            @pl.when(step == kind * blocks + index)
            def _(kind=kind, index=index):
                at, end = index * block, min((index + 1) * block, used)
                while at < end:
                    row = at // part
                    stop = min(end, (row + 1) * part)
                    target = row * kinds * part + kind * part + at - row * part
                    out_ref[target : target + stop - at, :] = total[at - index * block : stop - index * block, :]
                    at = stop


def outer(lefts, rights, kinds, part):
    tokens, features = rights[0].shape
    columns = lefts[0].shape[1]
    block = 256
    out_rows = N_ROW * kinds * part
    once = pl.BlockSpec((tokens, features), lambda i: (0, 0), pipeline_mode=pl.Buffered(1))
    return pl.pallas_call(
        functools.partial(outer_kernel, kinds, N_ROW * part),
        out_shape=jax.ShapeDtypeStruct((out_rows, features), jnp.bfloat16),
        grid=(columns // block,),
        in_specs=[pl.BlockSpec((tokens, block), lambda i: (0, i))] * 2 + [once] * 2,
        out_specs=pl.BlockSpec((out_rows, features), lambda i: (0, 0)),
        compiler_params=pltpu.CompilerParams(vmem_limit_bytes=VMEM_BYTES),
        cost_estimate=cost(4 * tokens * columns * features, 8 * tokens * features),
        name="outer",
    )(*lefts, *rights)


def settle_kernel(kinds, turned, scalars, near_ref, far_ref, other_ref, *refs):
    outs, held_ref = refs[:-1], refs[-1]
    d, y = scalars[0], scalars[1]
    part = near_ref.shape[0] // (2 * kinds)
    for kind in range(kinds):
        for slot in range(4):
            ref = (near_ref, other_ref, far_ref, other_ref)[slot]
            base = near_ref.shape[0] if slot == 3 else 0
            for side in range(2):
                at = ((d ^ slot) * 2 + (y if side == 0 else 1 - y)) * part
                rows = slice(base + (side * kinds + kind) * part, base + (side * kinds + kind + 1) * part)
                target = held_ref if turned else outs[kind]
                target[pl.ds(pl.multiple_of(at, 16), part), :] = wide(ref[rows, :])
        if turned:
            outs[kind][...] = jnp.transpose(held_ref[...])


def settle(d, y, near, far, other, kinds, turned):
    width = near.shape[1]
    hidden = 4 * near.shape[0] // kinds
    lanes = 256
    spec = lambda x: pl.BlockSpec((x.shape[0], lanes), lambda i: (0, i))
    shape = (width, hidden) if turned else (hidden, width)
    out_spec = pl.BlockSpec((lanes, hidden), lambda i: (i, 0)) if turned else pl.BlockSpec((hidden, lanes), lambda i: (0, i))
    return pl.pallas_call(
        functools.partial(settle_kernel, kinds, turned),
        out_shape=(jax.ShapeDtypeStruct(shape, jnp.float32),) * kinds,
        grid=(width // lanes,),
        in_specs=[pl.BlockSpec(memory_space=pltpu.SMEM)] + [spec(x) for x in (near, far, other)],
        out_specs=(out_spec,) * kinds,
        scratch_shapes=[pltpu.VMEM((hidden, lanes), jnp.float32)],
        compiler_params=pltpu.CompilerParams(vmem_limit_bytes=VMEM_BYTES),
        cost_estimate=cost(hidden * width, 6 * kinds * hidden * width, 0),
        name="settle",
    )(jnp.stack([d, y]), near, far, other)


def plane_gather(x):
    half = x.shape[0] // 2
    a, b = x[:half], x[half:]
    a_x = swap(a, "dp", 2)
    b_y = swap(b, "col", 1)
    a_y = swap(jnp.concatenate([a, a_x], axis=0), "col", 1)
    b_x = swap(jnp.concatenate([b, b_y], axis=1), "dp", 2)
    return [x, a_x, b_y, a_y, b_x]


def plane_scatter(parts, *others):
    a_keep, a_send, b_keep, b_send = parts
    half, width = a_keep.shape[0], b_keep.shape[1]
    a_x = swap(a_send, "dp", 2)
    b_y = swap(b_send, "col", 1)
    a_x, b_y, *others = lax.optimization_barrier((a_x, b_y, *others))
    a_y = swap(low(wide(a_keep[:, width:]) + wide(a_x[:, width:])), "col", 1)
    b_x = swap(low(wide(b_keep[half:]) + wide(b_y[half:])), "dp", 2)
    total = jnp.concatenate(
        [
            wide(a_keep[:, :width]) + wide(a_x[:, :width]) + wide(a_y),
            wide(b_keep[:half]) + wide(b_y[:half]) + wide(b_x),
        ],
        axis=0,
    )
    return (total, *others)


def dp_slots(x):
    far = swap(x, "dp", 2)
    other = swap(jnp.concatenate([x, far], axis=0), "dp", 1)
    return [x, other[: x.shape[0]], far, other[x.shape[0] :]]


def with_core(x):
    return jnp.concatenate([x, swap(x, "dp", 1)], axis=0)


def heads_sum(left, right):
    half = left.shape[1] // 2
    both = jnp.concatenate([left[:, :half], swap(left[:, half:], "dp", 1)], axis=0)
    even = low(dot_tn(both, right))
    part = half // 2
    return even, swap(even[part:], "dp", 2)


def heads_home(own, other, y, later):
    near = jnp.concatenate(xor_order([low(own), low(other)], y), axis=0)
    near = lax.psum_scatter(after(near, later), "row", scatter_dimension=0, tiled=True)
    return jnp.concatenate(xor_order(dp_slots(near), lax.axis_index("dp")), axis=0)


def quarters_home(pieces, r):
    n_row, n_col = lax.axis_size("row"), lax.axis_size("col")
    groups = n_row // n_col
    slots = xor_order(pieces, r)
    received = []
    for k in range(n_row):
        pairs = []
        for row in range(n_row):
            for col in range(n_col):
                head, half = divmod(row ^ k, n_col)
                pairs.append((row * n_col + col, (col * groups + head) * n_col + half))
        received.append(wide(lax.ppermute(slots[k], ("row", "col"), pairs)))
    return low(sum(received[1:], received[0]))


def fast_body(
    states,
    keep,
    cont_ids,
    answer_len,
    teacher,
    out_grad,
    gain_attn,
    w_query,
    key_projection,
    value_projection,
    w_out,
    gain_ffn,
    w_gate,
    w_up,
    w_down,
):
    rows, width = states.shape
    n_row, n_col, n_dp = lax.axis_size("row"), lax.axis_size("col"), lax.axis_size("dp")
    d, r, y = lax.axis_index("dp"), lax.axis_index("row"), lax.axis_index("col")
    core = d % 2
    groups = n_row // n_col
    features = width * n_col
    order = r ^ (y * groups)
    side = y.reshape(1)
    kv_scalars = jnp.stack([order, core])

    kv_mine = jnp.where(core == 0, key_projection, value_projection).T
    kv_mine = jnp.concatenate([kv_mine] + [swap(kv_mine, "row", k) for k in range(1, n_row)], axis=0)
    kv_theirs = swap(kv_mine, "dp", 1)

    heads = [rows_of(w_query, d * HEAD_SIZE, HEAD_SIZE, 1).T, rows_of(w_out, d * HEAD_SIZE, HEAD_SIZE)]
    heads = gather_rows(jnp.concatenate(heads, axis=0))

    inner = w_down.shape[0]
    inner_part = inner // (n_dp * n_col)

    def hidden_rows(at):
        return jnp.concatenate([rows_of(w, at * inner_part, inner_part) for w in (w_gate.T, w_up.T, w_down)], axis=0)

    hidden_other = swap(hidden_rows(d * n_col + (1 - y)), "col", 1)
    hidden_own = hidden_rows(d * n_col + y)
    kv_theirs, hidden_other = lax.optimization_barrier((kv_theirs, hidden_other))

    positions, segment, counted = token_layout(cont_ids, answer_len)
    row_start = r * rows
    count = jnp.sum(counted.astype(jnp.float32)).reshape(1)
    count = count + swap(count, "dp", 1)
    count = (count + swap(count, "dp", 2))[0]
    counted_here = rows_of(counted, row_start, rows).astype(jnp.float32)[:, None]
    keep_here = keep.astype(jnp.float32)[:, None]
    position = rows_of(positions, row_start, rows).astype(jnp.float32)
    query_seg = rows_of(segment, row_start, rows)
    key_segs = [rows_of(segment, jnp.maximum(r - k, 0) * rows, rows) for k in range(n_row)]
    flags = [jnp.int32(2)]
    for k in range(1, n_row):
        least, most = jnp.min(key_segs[k]), jnp.max(key_segs[k])
        active = (r >= k) & ((least < 0) | (most >= jnp.min(query_seg)))
        flags.append(jnp.where(active, jnp.where(most < 0, 1, 2), 0).astype(jnp.int32))
    flags = jnp.stack(flags + [(r - k) % n_row for k in range(n_row)])
    key_seg = jnp.concatenate(key_segs)[:, None]
    query_seg = query_seg[None, :]
    freqs = ROPE_BASE ** (-2.0 * jnp.arange(HEAD_SIZE // 2, dtype=jnp.float32) / HEAD_SIZE)
    angles_t = freqs[:, None] * position[None, :]
    cos_t, sin_t = jnp.cos(angles_t), jnp.sin(angles_t)
    cos_n, sin_n = cos_t.T, sin_t.T
    cos_n = jnp.concatenate([cos_n, cos_n], axis=1)
    sin_n = jnp.concatenate([-sin_n, sin_n], axis=1)

    def turn(x, sign):
        half = HEAD_SIZE // 2
        turned = jnp.concatenate([x[:, half:], x[:, :half]], axis=1)
        return x * cos_n + turned * (sign * sin_n)

    def turn_heads(x, sign, every):
        return jnp.concatenate(
            [
                turn(x[:, i : i + HEAD_SIZE], sign) if i % every == 0 else x[:, i : i + HEAD_SIZE]
                for i in range(0, x.shape[1], HEAD_SIZE)
            ],
            axis=1,
        )

    states_f = wide(states)
    squares = jnp.sum(states_f * states_f, axis=1)
    scale_attn = lax.rsqrt((squares + swap(squares, "col", 1)) / features + EPSILON)[:, None]
    a1 = low(states_f * scale_attn * gain_attn[None, :])
    kv_own, kv_send = key_value_project(kv_scalars, a1, kv_mine, kv_theirs)
    kv_received, heads, count = lax.optimization_barrier((swap(kv_send, "col", 1), heads, count))
    key_value = low(turn_heads(kv_own + wide(kv_received), 1.0, 2 * HEAD_SIZE))
    key_values = gather_rows(key_value)
    q_part, o_part = [
        jnp.concatenate([heads[(2 * i + j) * HEAD_SIZE : (2 * i + j + 1) * HEAD_SIZE] for i in range(n_row)], axis=0)
        for j in (0, 1)
    ]
    q_far = swap(q_part, "dp", 2)
    q_slots = [q_part, swap(q_part, "dp", 1), q_far, swap(q_far, "dp", 1)]
    q_own, q_send = project(side, a1, q_slots)
    hidden_own, hidden_other = lax.optimization_barrier((hidden_own, hidden_other, q_send))[:2]
    hidden_mine = jnp.concatenate([hidden_own, hidden_other], axis=1)
    gate_up_mine = gather_rows(hidden_mine[: 2 * inner_part])
    down_mine = gather_rows(hidden_mine[2 * inner_part :])
    q_received, key_values = lax.optimization_barrier((swap(q_send, "col", 1), key_values))
    queries = low(turn_heads(q_own + wide(q_received), 1.0, HEAD_SIZE))
    o_slots = dp_slots(after(o_part, q_send))
    queries, *o_slots = lax.optimization_barrier((queries, *o_slots))
    context, lse = attend(flags, queries, query_seg, key_seg, key_values)
    context_other = swap(context, "col", 1)
    hidden_res = states_f + keep_here * merge(side, context, context_other, o_slots)

    squares = jnp.sum(hidden_res * hidden_res, axis=1)
    scale_ffn = lax.rsqrt((squares + swap(squares, "col", 1)) / features + EPSILON)[:, None]
    a2 = low(hidden_res * scale_ffn * gain_ffn[None, :])
    a2_pieces = plane_gather(a2)
    gate_up_mine = after(gate_up_mine, a2_pieces[1])
    gate_up_sides = [gate_up_mine, swap(gate_up_mine, "dp", 1)]
    gate, up, *hids, a2_all = gate_up(a2_pieces, gate_up_sides)
    down_mine, gate, a1_other = lax.optimization_barrier((down_mine, gate, swap(a1, "col", 1)))
    down_sides = [down_mine, swap(down_mine, "dp", 1)]
    result = hidden_res + keep_here * plane_scatter(down(hids, down_sides))[0]
    error = result - wide(teacher)
    error_part = jnp.sum(counted_here * error * error)
    grad_result = wide(out_grad) + 2.0 / (count * features) * counted_here * error

    gm_pieces = plane_gather(low(keep_here * grad_result))
    def both_cores(own, other):
        return [own, swap(other, "dp", 1)]

    hids, a2_sides = both_cores(*hids), both_cores(a2_all, a2_all)
    a1_both = with_core(jnp.concatenate([a1, a1_other], axis=1))
    context_half = context.shape[1] // 2
    context_even, context_odd = [
        jnp.concatenate([context[:, i : i + context_half], context_other[:, i : i + context_half]], axis=1)
        for i in (0, context_half)
    ]
    context_cores = jnp.concatenate([context_even, swap(context_odd, "dp", 1)], axis=0)
    gate, a1_both, context_cores, *hids_sides = lax.optimization_barrier((gate, a1_both, context_cores, *hids, *a2_sides))
    hids, a2_sides = hids_sides[:2], hids_sides[2:]
    *dboth, gm_all = down_back(gm_pieces, gate, up, down_sides)

    def along_row(x):
        return lax.psum_scatter(x, "row", scatter_dimension=0, tiled=True)

    down_joined = outer(hids, both_cores(gm_all, gm_all), 1, inner_part)
    dboth_sides = both_cores(*dboth)
    *dboth, down_joined = lax.optimization_barrier((*dboth, *dboth_sides, down_joined))
    dboth, dboth_sides = dboth[:2], dboth[2:]
    down_part = along_row(down_joined)
    parts = gate_up_back(dboth, gate_up_sides)
    gate_up_joined = outer(dboth_sides, a2_sides, 2, inner_part)
    grad_normed_ffn, gate_up_joined = plane_scatter(parts, gate_up_joined)
    gate_up_joined, down_part = lax.optimization_barrier((gate_up_joined, down_part))
    gate_up_part = along_row(gate_up_joined)

    def hidden_near(part):
        near = jnp.concatenate([part[:, :width], swap(part[:, width:], "col", 1)], axis=0)
        return near, swap(near, "dp", 2)

    def hidden_home(near, far, kinds, turned, *others):
        both = jnp.concatenate([near, far], axis=0)
        if others:
            both = after(both, *others)
        return settle(d, y, near, far, swap(both, "dp", 1), kinds, turned)

    gain_ffn_sum = jnp.sum(grad_normed_ffn * hidden_res * scale_ffn, axis=0)
    weighted = grad_normed_ffn * gain_ffn[None, :]
    inner_sum = jnp.sum(weighted * hidden_res, axis=1)
    inner_sum = jnp.concatenate([inner_sum, jnp.full((128,), error_part)])
    inner_sum = inner_sum + swap(inner_sum, "col", 1)
    error_col = inner_sum[rows:]
    inner_sum = inner_sum[:rows, None]
    grad_hidden_res = grad_result + scale_ffn * weighted - hidden_res * scale_ffn**3 * inner_sum / features

    ga = low(keep_here * grad_hidden_res)
    do_own, do_send = project(side, ga, o_slots)
    context_cores, ga_cores = lax.optimization_barrier((context_cores, with_core(ga), do_send))[:2]
    o_even = low(dot_tn(context_cores, ga_cores))
    o_part = o_even.shape[0] // 4
    o_far = swap(jnp.concatenate([o_even[o_part : 2 * o_part], o_even[3 * o_part :]], axis=0), "dp", 2)
    do_received, o_far = lax.optimization_barrier((swap(do_send, "col", 1), o_far))
    grad_context = low(do_own + wide(do_received))
    dq, dkv_parts = attend_back(flags, queries, grad_context, lse, cos_t, sin_t, query_seg, key_seg, key_values)
    q_even, q_far = heads_sum(dq, a1_both)
    dkv_parts, gate_up_part = lax.optimization_barrier((dkv_parts, gate_up_part))
    dkv_sum = along_row(dkv_parts)
    gate_up_received, dkv_sum = lax.optimization_barrier((swap(gate_up_part[:, width:], "col", 1), dkv_sum))
    down_near = hidden_near(after(down_part, q_even))
    gate_up_near = jnp.concatenate([gate_up_part[:, :width], gate_up_received], axis=0)
    dkv = low(turn_heads(wide(dkv_sum), -1.0, 2 * HEAD_SIZE))
    gate_up_far = swap(gate_up_near, "dp", 2)
    dkv_cores = with_core(dkv)
    q_far = after(q_far, dkv_cores)
    q_sum = wide(q_even[: q_far.shape[0]]) + wide(q_far)
    dq_other = swap(dq, "col", 1)
    kv_part = 2 * HEAD_SIZE // n_dp
    dwkv = low(dot_tn(dkv_cores, a1_both)).reshape(groups, n_dp, kv_part, features)
    dwkv = [dwkv[:, i].reshape(groups * kv_part, features) for i in range(n_dp)]
    kv_near, kv_far = xor_order(dwkv, d)[0], xor_order(dwkv, d ^ 2)[0]
    q_sum = after(q_sum, kv_far)
    kv_far, dkv_other = lax.optimization_barrier((swap(kv_far, "dp", 2), swap(dkv, "col", 1)))
    dwkv = low(wide(kv_near) + wide(kv_far))
    grad_normed_attn = merge(side, dq, dq_other, q_slots) + key_value_back(
        kv_scalars, dkv, dkv_other, kv_mine, kv_theirs
    )

    q_other = swap(low(q_sum[:, width:]), "col", 1)
    grad_query = wide(heads_home(q_sum[:, :width], q_other, y, dkv_sum).T)
    o_own, o_other = [
        wide(o_even[2 * i * o_part : (2 * i + 1) * o_part]) + wide(o_far[i * o_part : (i + 1) * o_part]) for i in (0, 1)
    ]
    grad_out = wide(heads_home(o_own, o_other, y, dkv_sum))
    pieces = []
    for g in range(groups):
        block = dwkv[g * kv_part : (g + 1) * kv_part]
        pieces += xor_order([block[:, :width], block[:, width:]], y)
    dwkv = quarters_home(pieces, r)
    (grad_down,) = hidden_home(*down_near, 1, False, dwkv)
    grad_gate, grad_up = hidden_home(gate_up_near, gate_up_far, 2, True, dwkv)
    later = dwkv
    dwkv = jnp.concatenate(xor_order(dp_slots(dwkv), d), axis=0)
    grad_key = wide(dwkv[:HEAD_SIZE].T)
    grad_value = wide(dwkv[HEAD_SIZE:].T)

    gain_attn_sum = jnp.sum(grad_normed_attn * states_f * scale_attn, axis=0)
    weighted = grad_normed_attn * gain_attn[None, :]
    inner_sum = jnp.sum(weighted * states_f, axis=1)
    inner_sum = (inner_sum + swap(inner_sum, "col", 1))[:, None]
    grad_states = grad_hidden_res + scale_attn * weighted - states_f * scale_attn**3 * inner_sum / features

    sums = after(jnp.concatenate([gain_attn_sum, gain_ffn_sum, error_col]), later)
    for axis, mask in (("dp", 1), ("dp", 2), ("row", 1), ("row", 2)):
        sums = sums + swap(sums, axis, mask)
    return (
        low(result),
        sums[2 * width] / (count * features),
        grad_states,
        sums[:width],
        grad_query,
        grad_key,
        grad_value,
        grad_out,
        sums[width : 2 * width],
        grad_gate,
        grad_up,
        grad_down,
    )


def solution(mesh):
    return jax.shard_map(
        fast_body if dict(mesh.shape) == {"dp": 4, "row": 4, "col": 2} else body,
        mesh=mesh,
        in_specs=(
            P(("dp", "row"), "col"),
            P(("dp", "row")),
            P("dp", None),
            P("dp", None),
            P(("dp", "row"), "col"),
            P(("dp", "row"), "col"),
            P("col"),
            P("col", "row"),
            P("col", "row"),
            P("col", "row"),
            P("row", "col"),
            P("col"),
            P("col", "row"),
            P("col", "row"),
            P("row", "col"),
        ),
        out_specs=(
            P(("dp", "row"), "col"),
            P(),
            P(("dp", "row"), "col"),
            P("col"),
            P("col", "row"),
            P("col", "row"),
            P("col", "row"),
            P("row", "col"),
            P("col"),
            P("col", "row"),
            P("col", "row"),
            P("row", "col"),
        ),
        check_vma=False,
    )
```

```python
import functools

import jax
import jax.numpy as jnp
from jax import lax
from jax.experimental import pallas as pl
from jax.experimental.pallas import tpu as pltpu
from jax.sharding import PartitionSpec as P

MODEL_WIDTH = 2048
HEAD_SIZE = 128
PROMPT = 1024


EPSILON = 1e-05
MASKED = -1e30
ROPE_BASE = 10000.0


def rows_of(values, start, count, axis=0):
    return lax.dynamic_slice_in_dim(values, start, count, axis)


def token_layout(cont_ids, answer_len):
    groups, cont_tokens = cont_ids.shape
    labels = jnp.arange(answer_len.shape[1], dtype=jnp.int32)
    starts = jnp.sum((cont_ids[:, None, :] < labels[None, :, None]).astype(jnp.int32), axis=2)
    member = (cont_ids[:, :, None] == labels[None, None, :]).astype(jnp.int32)
    own_start = jnp.sum(member * starts[:, None, :], axis=2)
    own_limit = jnp.sum(member * answer_len[:, None, :], axis=2)
    offset = jnp.arange(cont_tokens, dtype=jnp.int32)[None, :] - own_start
    prompt_pos = jnp.arange(PROMPT, dtype=jnp.int32)[None, :]
    positions = jnp.concatenate([prompt_pos, PROMPT + offset], axis=1).reshape(-1)
    segment = jnp.concatenate(
        [jnp.full((groups, PROMPT), -1, dtype=jnp.int32), cont_ids], axis=1
    ).reshape(-1)
    counted = jnp.concatenate(
        [jnp.ones((groups, PROMPT), jnp.int32), (offset < own_limit).astype(jnp.int32)], axis=1
    ).reshape(-1)
    return (positions, segment, counted)


def rotary(values, positions, sign):
    half = values.shape[-1] // 2
    freqs = ROPE_BASE ** (-2.0 * jnp.arange(half, dtype=jnp.float32) / values.shape[-1])
    angles = positions.astype(jnp.float32)[:, None] * freqs[None, :]
    cosine = jnp.cos(angles)[:, None, :]
    sine = sign * jnp.sin(angles)[:, None, :]
    first = values[..., :half]
    second = values[..., half:]
    return jnp.concatenate(
        [first * cosine - second * sine, second * cosine + first * sine], axis=-1
    )


def visible(query_index, query_segment, key_index, key_segment):
    earlier = key_index[None, :] <= query_index[:, None]
    shared = (key_segment[None, :] < 0) | (key_segment[None, :] == query_segment[:, None])
    return earlier & shared


def feature_sum(values):
    return lax.psum(values, "col")


def gather_rows(values):
    return lax.all_gather(values, "row", axis=0, tiled=True)


def gather_cols(values):
    return lax.all_gather(values, "col", axis=0, tiled=True)


def partial_cols(term, count):
    return lax.psum_scatter(
        term(jnp.int32(0), count * lax.axis_size("col")), "col", scatter_dimension=0, tiled=True
    )


def partial_rows(term, count):
    return lax.psum_scatter(
        term(jnp.int32(0), count * lax.axis_size("row")), "row", scatter_dimension=0, tiled=True
    )


def body(
    states,
    keep,
    cont_ids,
    answer_len,
    teacher,
    out_grad,
    gain_attn,
    w_query,
    key_projection,
    value_projection,
    w_out,
    gain_ffn,
    w_gate,
    w_up,
    w_down,
):
    local_rows = states.shape[0]
    whole_rows = local_rows * lax.axis_size("row")
    query_rows = whole_rows // lax.axis_size("col")
    group_tokens = PROMPT + cont_ids.shape[1]
    key_heads = key_projection.shape[1] // HEAD_SIZE
    heads_per_group = w_query.shape[1] // key_projection.shape[1]
    query_width = w_query.shape[1]
    scale = HEAD_SIZE ** (-0.5)
    block = min(512, query_rows)
    blocks = query_rows // block
    positions, segment, counted = token_layout(cont_ids, answer_len)
    token_index = jnp.arange(whole_rows, dtype=jnp.int32)
    row_start = lax.axis_index("row") * local_rows
    col_start = lax.axis_index("col") * query_rows
    counted_here = rows_of(counted, row_start, local_rows).astype(jnp.float32)[:, None]
    query_pos = rows_of(positions, col_start, query_rows)
    keep_here = keep.astype(jnp.float32)[:, None]
    states_f = states.astype(jnp.float32)
    scale_attn = lax.rsqrt(
        feature_sum(jnp.sum(states_f * states_f, axis=1)) / MODEL_WIDTH + EPSILON
    )[:, None]
    normed_attn = (states_f * scale_attn * gain_attn[None, :]).astype(jnp.bfloat16)
    normed_all = gather_rows(normed_attn)
    w_kv = jnp.concatenate([key_projection, value_projection], axis=1)
    query_raw = partial_cols(
        lambda start, count: jnp.dot(
            rows_of(normed_all, start, count), w_query, preferred_element_type=jnp.float32
        ),
        query_rows,
    )
    kv_raw = lax.psum(jnp.dot(normed_all, w_kv, preferred_element_type=jnp.float32), "col")
    queries = (
        rotary(
            query_raw.reshape(query_rows, key_heads * heads_per_group, HEAD_SIZE), query_pos, 1.0
        )
        .astype(jnp.bfloat16)
        .reshape(query_rows, key_heads, heads_per_group, HEAD_SIZE)
    )
    keys = rotary(
        kv_raw[:, : key_heads * HEAD_SIZE].reshape(whole_rows, key_heads, HEAD_SIZE), positions, 1.0
    ).astype(jnp.bfloat16)
    values = (
        kv_raw[:, key_heads * HEAD_SIZE :]
        .reshape(whole_rows, key_heads, HEAD_SIZE)
        .astype(jnp.bfloat16)
    )

    def context_of(index):
        first = col_start + index * block
        key_first = first // group_tokens * group_tokens
        query_block = rows_of(queries, index * block, block)
        key_group = rows_of(keys, key_first, group_tokens)
        value_group = rows_of(values, key_first, group_tokens)
        raw = (
            jnp.einsum("qgjd,kgd->gjqk", query_block, key_group, preferred_element_type=jnp.float32)
            * scale
        )
        mask = visible(
            rows_of(token_index, first, block),
            rows_of(segment, first, block),
            rows_of(token_index, key_first, group_tokens),
            rows_of(segment, key_first, group_tokens),
        )
        scores = jnp.where(mask[None, None], raw, MASKED)
        return (query_block, key_group, value_group, scores, key_first)

    def attend(index):
        query_block, key_group, value_group, scores, key_first = context_of(index)
        peak = jnp.max(scores, axis=-1, keepdims=True)
        exponent = jnp.exp(scores - peak)
        totals = jnp.sum(exponent, axis=-1, keepdims=True)
        weights = (exponent / totals).astype(jnp.bfloat16)
        mixed = jnp.einsum(
            "gjqk,kgd->qgjd", weights, value_group, preferred_element_type=jnp.float32
        )
        return (mixed, peak + jnp.log(totals))

    mixed_blocks, log_totals = lax.map(attend, jnp.arange(blocks, dtype=jnp.int32))
    attn_context = mixed_blocks.reshape(query_rows, query_width).astype(jnp.bfloat16)
    context_all = gather_cols(attn_context)
    attention = partial_rows(
        lambda start, count: jnp.dot(
            rows_of(context_all, start, count), w_out, preferred_element_type=jnp.float32
        ),
        local_rows,
    )
    hidden_res = states_f + keep_here * attention
    scale_ffn = lax.rsqrt(
        feature_sum(jnp.sum(hidden_res * hidden_res, axis=1)) / MODEL_WIDTH + EPSILON
    )[:, None]
    normed_ffn = (hidden_res * scale_ffn * gain_ffn[None, :]).astype(jnp.bfloat16)
    ffn_all = gather_rows(normed_ffn)
    w_pair = jnp.concatenate([w_gate, w_up], axis=1)
    inner = w_gate.shape[1]
    gate_up = partial_cols(
        lambda start, count: jnp.dot(
            rows_of(ffn_all, start, count), w_pair, preferred_element_type=jnp.float32
        ),
        query_rows,
    )
    gate = gate_up[:, :inner]
    up_proj = gate_up[:, inner:]
    sigma = jax.nn.sigmoid(gate)
    swish = gate * sigma
    hidden = (swish * up_proj).astype(jnp.bfloat16)
    hidden_all = gather_cols(hidden)
    feed = partial_rows(
        lambda start, count: jnp.dot(
            rows_of(hidden_all, start, count), w_down, preferred_element_type=jnp.float32
        ),
        local_rows,
    )
    result = hidden_res + keep_here * feed
    error = result - teacher.astype(jnp.float32)
    own_count = jnp.where(lax.axis_index("col") == 0, jnp.sum(counted_here), 0.0)
    error_total, token_count_sum = lax.psum(
        (jnp.sum(counted_here * error * error), own_count), ("dp", "row", "col")
    )
    loss = error_total / (token_count_sum * MODEL_WIDTH)
    grad_result = (
        out_grad.astype(jnp.float32) + 2.0 / (token_count_sum * MODEL_WIDTH) * counted_here * error
    )
    grad_feed = (keep_here * grad_result).astype(jnp.bfloat16)
    grad_feed_all = gather_rows(grad_feed)
    grad_down = jnp.einsum(
        "tf,td->fd", hidden_all, grad_feed_all, preferred_element_type=jnp.float32
    )
    grad_hidden = partial_cols(
        lambda start, count: jnp.einsum(
            "td,fd->tf",
            rows_of(grad_feed_all, start, count),
            w_down,
            preferred_element_type=jnp.float32,
        ),
        query_rows,
    )
    grad_gate_in = grad_hidden * up_proj * sigma * (1.0 + gate * (1.0 - sigma))
    grad_up_in = grad_hidden * swish
    grad_pair = jnp.concatenate([grad_gate_in, grad_up_in], axis=1).astype(jnp.bfloat16)
    grad_pair_all = gather_cols(grad_pair)
    grad_w_pair = jnp.einsum(
        "td,tf->df", ffn_all, grad_pair_all, preferred_element_type=jnp.float32
    )
    grad_normed_ffn = partial_rows(
        lambda start, count: jnp.einsum(
            "tf,df->td",
            rows_of(grad_pair_all, start, count),
            w_pair,
            preferred_element_type=jnp.float32,
        ),
        local_rows,
    )
    grad_gain_ffn = jnp.sum(grad_normed_ffn * hidden_res * scale_ffn, axis=0)
    weighted_ffn = grad_normed_ffn * gain_ffn[None, :]
    inner_ffn = feature_sum(jnp.sum(weighted_ffn * hidden_res, axis=1))[:, None]
    grad_hidden_res = (
        grad_result + scale_ffn * weighted_ffn - hidden_res * scale_ffn**3 * inner_ffn / MODEL_WIDTH
    )
    grad_attention = (keep_here * grad_hidden_res).astype(jnp.bfloat16)
    grad_att_all = gather_rows(grad_attention)
    grad_out = jnp.einsum(
        "to,td->od", context_all, grad_att_all, preferred_element_type=jnp.float32
    )
    grad_context = partial_cols(
        lambda start, count: jnp.einsum(
            "td,od->to",
            rows_of(grad_att_all, start, count),
            w_out,
            preferred_element_type=jnp.float32,
        ),
        query_rows,
    )
    grad_context = grad_context.astype(jnp.bfloat16).reshape(
        query_rows, key_heads, heads_per_group, HEAD_SIZE
    )

    def attend_back(carry, item):
        index, log_total = item
        query_block, key_group, value_group, scores, key_first = context_of(index)
        grad_block = rows_of(grad_context, index * block, block)
        probs = jnp.exp(scores - log_total)
        grad_probs = jnp.einsum(
            "qgjd,kgd->gjqk", grad_block, value_group, preferred_element_type=jnp.float32
        )
        row_dot = jnp.sum(probs * grad_probs, axis=-1, keepdims=True)
        grad_scores = (probs * (grad_probs - row_dot)).astype(jnp.bfloat16)
        grad_query_block = (
            jnp.einsum("gjqk,kgd->qgjd", grad_scores, key_group, preferred_element_type=jnp.float32)
            * scale
        )
        grad_key_group = (
            jnp.einsum(
                "gjqk,qgjd->kgd", grad_scores, query_block, preferred_element_type=jnp.float32
            )
            * scale
        )
        grad_value_group = jnp.einsum(
            "gjqk,qgjd->kgd",
            probs.astype(jnp.bfloat16),
            grad_block,
            preferred_element_type=jnp.float32,
        )
        pair = jnp.concatenate([grad_key_group, grad_value_group], axis=1)
        updated = rows_of(carry, key_first, group_tokens) + pair
        return (updated, grad_query_block)

    start_carry = jnp.zeros((whole_rows, 2 * key_heads, HEAD_SIZE), jnp.float32)
    grad_kv_part, grad_query_blocks = lax.scan(
        attend_back, start_carry, (jnp.arange(blocks, dtype=jnp.int32), log_totals)
    )
    grad_kv_sum = (
        lax.psum(
            grad_kv_part.reshape(whole_rows, 2 * key_heads * HEAD_SIZE).astype(jnp.bfloat16), "col"
        )
        .astype(jnp.float32)
        .reshape(whole_rows, 2 * key_heads, HEAD_SIZE)
    )
    grad_keys = rotary(grad_kv_sum[:, :key_heads], positions, -1.0)
    grad_kv = (
        jnp.concatenate([grad_keys, grad_kv_sum[:, key_heads:]], axis=1)
        .reshape(whole_rows, 2 * key_heads * HEAD_SIZE)
        .astype(jnp.bfloat16)
    )
    grad_queries = (
        rotary(
            grad_query_blocks.reshape(query_rows, key_heads * heads_per_group, HEAD_SIZE),
            query_pos,
            -1.0,
        )
        .reshape(query_rows, query_width)
        .astype(jnp.bfloat16)
    )
    grad_queries_all = gather_cols(grad_queries)
    grad_query = jnp.einsum(
        "td,tq->dq", normed_all, grad_queries_all, preferred_element_type=jnp.float32
    )
    grad_kv_weight = jnp.einsum(
        "td,tk->dk", normed_all, grad_kv, preferred_element_type=jnp.float32
    )
    grad_key = grad_kv_weight[:, : key_heads * HEAD_SIZE]
    grad_value = grad_kv_weight[:, key_heads * HEAD_SIZE :]

    def back_terms(start, count):
        from_queries = jnp.einsum(
            "tq,dq->td",
            rows_of(grad_queries_all, start, count),
            w_query,
            preferred_element_type=jnp.float32,
        )
        from_kv = jnp.einsum(
            "tk,dk->td", rows_of(grad_kv, start, count), w_kv, preferred_element_type=jnp.float32
        )
        return from_queries + from_kv

    grad_normed_attn = partial_rows(back_terms, local_rows)
    grad_gain_attn = jnp.sum(grad_normed_attn * states_f * scale_attn, axis=0)
    weighted_attn = grad_normed_attn * gain_attn[None, :]
    inner_attn = feature_sum(jnp.sum(weighted_attn * states_f, axis=1))[:, None]
    grad_states = (
        grad_hidden_res
        + scale_attn * weighted_attn
        - states_f * scale_attn**3 * inner_attn / MODEL_WIDTH
    )
    gain_attn_sum, gain_ffn_sum = lax.psum((grad_gain_attn, grad_gain_ffn), ("dp", "row"))
    summed = (
        lax.psum(grad_query.astype(jnp.bfloat16), "dp").astype(jnp.float32),
        lax.psum(grad_key.astype(jnp.bfloat16), "dp").astype(jnp.float32),
        lax.psum(grad_value.astype(jnp.bfloat16), "dp").astype(jnp.float32),
        lax.psum(grad_out.astype(jnp.bfloat16), "dp").astype(jnp.float32),
        lax.psum(grad_w_pair[:, :inner].astype(jnp.bfloat16), "dp").astype(jnp.float32),
        lax.psum(grad_w_pair[:, inner:].astype(jnp.bfloat16), "dp").astype(jnp.float32),
        lax.psum(grad_down.astype(jnp.bfloat16), "dp").astype(jnp.float32),
    )
    return (
        result.astype(jnp.bfloat16),
        loss,
        grad_states,
        gain_attn_sum,
        summed[0],
        summed[1],
        summed[2],
        summed[3],
        gain_ffn_sum,
        summed[4],
        summed[5],
        summed[6],
    )


LOG2E = 1.4426950408889634
N_ROW = 4
SHARE = 0.1


def cost(flops, moved, exps=0, share=SHARE):
    return pl.CostEstimate(flops=int(share * flops), bytes_accessed=int(share * moved), transcendentals=int(share * exps))

VMEM_BYTES = 58 << 20
ORDER = (0, 2, 1, 3)


def swap(values, axis, mask):
    size = lax.axis_size(axis)
    return lax.ppermute(values, axis, [(i, i ^ mask) for i in range(size)])


def xor_order(slots, mask):
    bit = 1
    while bit < len(slots):
        odd = (mask & bit) != 0
        slots = [jnp.where(odd, slots[i ^ bit], slots[i]) for i in range(len(slots))]
        bit *= 2
    return slots


def after(values, *others):
    return lax.optimization_barrier((values, *others))[0]


def low(values):
    return values.astype(jnp.bfloat16)


def wide(values):
    return values.astype(jnp.float32)


def dot_nn(left, right):
    return lax.dot_general(left, right, (((1,), (0,)), ((), ())), preferred_element_type=jnp.float32)


def dot_nt(left, right):
    return lax.dot_general(left, right, (((1,), (1,)), ((), ())), preferred_element_type=jnp.float32)


def dot_tn(left, right):
    return lax.dot_general(left, right, (((0,), (0,)), ((), ())), preferred_element_type=jnp.float32)


def attend_kernel(slots, scale, flags, q_ref, qseg_ref, kseg_ref, *refs):
    kv_refs = refs[:slots]
    o_ref, lse_ref, peak_ref, total_ref, acc_ref = refs[slots:]
    query = q_ref[...]
    rows = query.shape[0]

    def scores(slot):
        return dot_nt(kv_refs[slot][:, :HEAD_SIZE], query) * (scale * LOG2E)

    def seen(slot):
        key_seg = kseg_ref[slot * rows : (slot + 1) * rows, :]
        return (key_seg < 0) | (key_seg == qseg_ref[...])

    def add(slot, s):
        peak = peak_ref[...]
        higher = jnp.maximum(peak, jnp.max(s, axis=0, keepdims=True))
        fade = jnp.exp2(peak - higher)
        e = jnp.exp2(s - higher)
        total_ref[...] = total_ref[...] * fade + jnp.sum(e, axis=0, keepdims=True)
        acc_ref[...] = acc_ref[...] * fade + dot_tn(kv_refs[slot][:, HEAD_SIZE:], low(e))
        peak_ref[...] = higher

    key_index = lax.broadcasted_iota(jnp.int32, (rows, rows), 0)
    query_index = lax.broadcasted_iota(jnp.int32, (rows, rows), 1)
    s = jnp.where((key_index <= query_index) & seen(0), scores(0), MASKED)
    peak = jnp.max(s, axis=0, keepdims=True)
    e = jnp.exp2(s - peak)
    peak_ref[...] = peak
    total_ref[...] = jnp.sum(e, axis=0, keepdims=True)
    acc_ref[...] = dot_tn(kv_refs[0][:, HEAD_SIZE:], low(e))
    for slot in range(1, slots):

        @pl.when(flags[slot] == 1)
        def _(slot=slot):
            add(slot, scores(slot))

        @pl.when(flags[slot] == 2)
        def _(slot=slot):
            add(slot, jnp.where(seen(slot), scores(slot), MASKED))

    o_ref[...] = low(jnp.transpose(acc_ref[...] / total_ref[...]))
    lse_ref[0] = peak_ref[...] + jnp.log2(total_ref[...])


def attend_back_kernel(slots, scale, flags, q_ref, do_ref, lse_ref, cos_ref, sin_ref, qseg_ref, kseg_ref, *refs):
    kv_refs = refs[:slots]
    dq_ref, dkv_ref, p_ref, dp_ref, dot_ref, dq_acc, dkv_acc = refs[slots:]
    step, steps = pl.program_id(1), pl.num_programs(1)
    query, grad = q_ref[...], do_ref[...]
    rows = query.shape[0]

    @pl.when(step == 0)
    def _():
        dkv_acc[...] = jnp.zeros_like(dkv_acc)

    def seen(slot):
        key_seg = kseg_ref[slot * rows : (slot + 1) * rows, :]
        return (key_seg < 0) | (key_seg == qseg_ref[...])

    def first(slot, mask):
        e = jnp.exp2(dot_nt(kv_refs[slot][:, :HEAD_SIZE], query) * (scale * LOG2E) - lse_ref[0])
        if mask is not None:
            e = jnp.where(mask, e, 0.0)
        dp = dot_nt(kv_refs[slot][:, HEAD_SIZE:], grad)
        p_ref[slot] = e
        dp_ref[slot] = dp
        part = jnp.sum(e * dp, axis=0, keepdims=True)
        if slot == 0:
            dot_ref[...] = part
        else:
            dot_ref[...] += part

    def second(slot):
        p = p_ref[slot]
        ds = low(p * (dp_ref[slot] - dot_ref[...]))
        dkv_acc[slot, :, :HEAD_SIZE] += dot_nn(ds, query)
        dkv_acc[slot, :, HEAD_SIZE:] += dot_nn(low(p), grad)
        part = dot_tn(kv_refs[slot][:, :HEAD_SIZE], ds)
        if slot == 0:
            dq_acc[...] = part
        else:
            dq_acc[...] += part

    key_index = lax.broadcasted_iota(jnp.int32, (rows, rows), 0)
    query_index = lax.broadcasted_iota(jnp.int32, (rows, rows), 1)
    first(0, (key_index <= query_index) & seen(0))
    for slot in range(1, slots):

        @pl.when(flags[slot] == 1)
        def _(slot=slot):
            first(slot, None)

        @pl.when(flags[slot] == 2)
        def _(slot=slot):
            first(slot, seen(slot))

    second(0)
    for slot in range(1, slots):

        @pl.when(flags[slot] > 0)
        def _(slot=slot):
            second(slot)

    half = HEAD_SIZE // 2
    upper, lower = dq_acc[:half, :] * scale, dq_acc[half:, :] * scale
    cosine, sine = cos_ref[...], sin_ref[...]
    turned = jnp.concatenate([upper * cosine + lower * sine, lower * cosine - upper * sine], axis=0)
    dq_ref[...] = low(jnp.transpose(turned))

    @pl.when(step == steps - 1)
    def _():
        for slot in range(slots):
            at = pl.ds(pl.multiple_of(flags[slots + slot] * rows, rows), rows)
            dkv_ref[at, :HEAD_SIZE] = low(dkv_acc[slot, :, :HEAD_SIZE] * scale)
            dkv_ref[at, HEAD_SIZE:] = low(dkv_acc[slot, :, HEAD_SIZE:])


def attend_specs(queries, key_values):
    rows, width = queries.shape
    slots, groups = key_values.shape[0] // rows, key_values.shape[1] // (2 * HEAD_SIZE)
    whole = lambda g, m, f: (0, 0)
    head = pl.BlockSpec((rows, HEAD_SIZE), lambda g, m, f: (0, m * groups + g))
    line = pl.BlockSpec((1, 1, rows), lambda g, m, f: (m * groups + g, 0, 0))
    segs = [pl.BlockSpec((1, rows), whole), pl.BlockSpec((slots * rows, 1), whole)]
    pairs = [
        pl.BlockSpec((rows, 2 * HEAD_SIZE), lambda g, m, f, slot=slot: (f[slots + slot], g)) for slot in range(slots)
    ]
    return rows, width, slots, groups, width // HEAD_SIZE // groups, whole, head, line, segs, pairs


def attend(flags, queries, query_seg, key_seg, key_values):
    rows, width, slots, groups, share, whole, head, line, segs, pairs = attend_specs(queries, key_values)
    return pl.pallas_call(
        functools.partial(attend_kernel, slots, HEAD_SIZE ** (-0.5)),
        out_shape=(
            jax.ShapeDtypeStruct((rows, width), jnp.bfloat16),
            jax.ShapeDtypeStruct((share * groups, 1, rows), jnp.float32),
        ),
        grid_spec=pltpu.PrefetchScalarGridSpec(
            num_scalar_prefetch=1,
            grid=(groups, share),
            in_specs=[head] + segs + pairs,
            out_specs=(head, line),
            scratch_shapes=[
                pltpu.VMEM((1, rows), jnp.float32),
                pltpu.VMEM((1, rows), jnp.float32),
                pltpu.VMEM((HEAD_SIZE, rows), jnp.float32),
            ],
        ),
        compiler_params=pltpu.CompilerParams(vmem_limit_bytes=VMEM_BYTES),
        cost_estimate=cost(3 * rows * rows * width * 4, 8 << 20, 3 * rows * rows * share * groups),
        name="attend",
    )(flags, queries, query_seg, key_seg, *[key_values] * slots)


def attend_back(flags, queries, grads, lse, cosine, sine, query_seg, key_seg, key_values):
    rows, width, slots, groups, share, whole, head, line, segs, pairs = attend_specs(queries, key_values)
    angle = pl.BlockSpec((HEAD_SIZE // 2, rows), whole)
    return pl.pallas_call(
        functools.partial(attend_back_kernel, slots, HEAD_SIZE ** (-0.5)),
        out_shape=(
            jax.ShapeDtypeStruct((rows, width), jnp.bfloat16),
            jax.ShapeDtypeStruct(key_values.shape, jnp.bfloat16),
        ),
        grid_spec=pltpu.PrefetchScalarGridSpec(
            num_scalar_prefetch=1,
            grid=(groups, share),
            in_specs=[head, head, line, angle, angle] + segs + pairs,
            out_specs=(head, pl.BlockSpec((slots * rows, 2 * HEAD_SIZE), lambda g, m, f: (0, g))),
            scratch_shapes=[
                pltpu.VMEM((slots, rows, rows), jnp.float32),
                pltpu.VMEM((slots, rows, rows), jnp.float32),
                pltpu.VMEM((1, rows), jnp.float32),
                pltpu.VMEM((HEAD_SIZE, rows), jnp.float32),
                pltpu.VMEM((slots, rows, 2 * HEAD_SIZE), jnp.float32),
            ],
        ),
        compiler_params=pltpu.CompilerParams(vmem_limit_bytes=VMEM_BYTES),
        cost_estimate=cost(3 * rows * rows * width * 10, 12 << 20, 3 * rows * rows * share * groups),
        name="attend_back",
    )(flags, queries, grads, lse, cosine, sine, query_seg, key_seg, *[key_values] * slots)


def project_kernel(side, a_ref, *refs):
    slots, (own_ref, send_ref) = refs[:-2], refs[-2:]
    part = slots[0].shape[0] // 2
    own = pl.multiple_of(side[0] * part, part)
    other = pl.multiple_of((1 - side[0]) * part, part)
    for place, slot in enumerate(ORDER):
        columns = slice(place * part, (place + 1) * part)
        send_ref[:, columns] = low(dot_nt(a_ref[...], slots[slot][pl.ds(other, part), :]))
        own_ref[:, columns] = dot_nt(a_ref[...], slots[slot][pl.ds(own, part), :])


def merge_kernel(side, own_ref, other_ref, *refs):
    slots, out_ref = refs[:-1], refs[-1]
    part = slots[0].shape[0] // 2
    own = pl.multiple_of(side[0] * part, part)
    other = pl.multiple_of((1 - side[0]) * part, part)
    total = None
    for place, slot in enumerate(ORDER):
        columns = slice(place * part, (place + 1) * part)
        term = dot_nn(own_ref[:, columns], slots[slot][pl.ds(own, part), :])
        term += dot_nn(other_ref[:, columns], slots[slot][pl.ds(other, part), :])
        total = term if total is None else total + term
    out_ref[...] = total


def local_call(kernel, name, scalars, operands, outs, flops, scratch=()):
    vmem = pl.BlockSpec(memory_space=pltpu.VMEM)
    moved = sum(x.size * x.dtype.itemsize for x in operands)
    return pl.pallas_call(
        kernel,
        out_shape=outs,
        in_specs=[pl.BlockSpec(memory_space=pltpu.SMEM)] + [vmem] * len(operands),
        out_specs=jax.tree.map(lambda _: vmem, outs),
        scratch_shapes=list(scratch),
        compiler_params=pltpu.CompilerParams(vmem_limit_bytes=VMEM_BYTES),
        cost_estimate=cost(flops, 2 * moved, 0),
        name=name,
    )(scalars, *operands)


def project(side, a, slots):
    rows, width = a.shape[0], slots[0].shape[0] * len(slots) // 2
    outs = (jax.ShapeDtypeStruct((rows, width), jnp.float32), jax.ShapeDtypeStruct((rows, width), jnp.bfloat16))
    return local_call(project_kernel, "project", side, [a, *slots], outs, 4 * rows * width * a.shape[1])


def merge(side, own, other, slots):
    outs = jax.ShapeDtypeStruct((own.shape[0], slots[0].shape[1]), jnp.float32)
    return local_call(merge_kernel, "merge", side, [own, other, *slots], outs, 4 * own.size * slots[0].shape[1])


def key_value_kernel(scalars, a_ref, mine_ref, theirs_ref, own_ref, send_ref, all_ref):
    order, core = scalars[0], scalars[1]
    count = mine_ref.shape[0] // HEAD_SIZE
    groups = count // 2
    for ref, kind in ((mine_ref, core), (theirs_ref, 1 - core)):
        for slot in range(count):
            place = slot ^ order
            lane = pl.multiple_of(((place % groups) * 2 + kind) * HEAD_SIZE, HEAD_SIZE)
            all_ref[place // groups, :, pl.ds(lane, HEAD_SIZE)] = dot_nt(
                a_ref[...], ref[slot * HEAD_SIZE : (slot + 1) * HEAD_SIZE, :]
            )
    own_ref[...] = all_ref[0]
    send_ref[...] = low(all_ref[1])


def key_value_back_kernel(scalars, own_ref, other_ref, mine_ref, theirs_ref, out_ref, all_ref):
    order, core = scalars[0], scalars[1]
    count = mine_ref.shape[0] // HEAD_SIZE
    groups = count // 2
    all_ref[0] = own_ref[...]
    all_ref[1] = other_ref[...]
    total = None
    for ref, kind in ((mine_ref, core), (theirs_ref, 1 - core)):
        for slot in range(count):
            place = slot ^ order
            lane = pl.multiple_of(((place % groups) * 2 + kind) * HEAD_SIZE, HEAD_SIZE)
            term = dot_nn(
                all_ref[place // groups, :, pl.ds(lane, HEAD_SIZE)], ref[slot * HEAD_SIZE : (slot + 1) * HEAD_SIZE, :]
            )
            total = term if total is None else total + term
    out_ref[...] = total


def key_value_project(scalars, a, mine, theirs):
    rows, width = a.shape[0], mine.shape[0]
    outs = (jax.ShapeDtypeStruct((rows, width), jnp.float32), jax.ShapeDtypeStruct((rows, width), jnp.bfloat16))
    return local_call(
        key_value_kernel, "key_value", scalars, [a, mine, theirs], outs, 4 * rows * width * a.shape[1],
        [pltpu.VMEM((2, rows, width), jnp.float32)],
    )


def key_value_back(scalars, own, other, mine, theirs):
    outs = jax.ShapeDtypeStruct((own.shape[0], mine.shape[1]), jnp.float32)
    return local_call(
        key_value_back_kernel, "key_value_back", scalars, [own, other, mine, theirs], outs, 4 * own.size * mine.shape[1],
        [pltpu.VMEM((2, *own.shape), own.dtype)],
    )


def load_block(step, pieces, all_ref):
    x_ref, ax_ref, by_ref, ay_ref, bx_ref = pieces
    rows, width = ax_ref.shape

    @pl.when(step == 0)
    def _():
        all_ref[:, :width] = x_ref[:rows, :]
        all_ref[:, width:] = ay_ref[:rows, :]

    @pl.when(step == 1)
    def _():
        all_ref[:, :width] = x_ref[rows:, :]
        all_ref[:, width:] = by_ref[...]

    @pl.when(step == 2)
    def _():
        all_ref[:, :width] = ax_ref[...]
        all_ref[:, width:] = ay_ref[rows:, :]

    @pl.when(step == 3)
    def _():
        all_ref[...] = bx_ref[...]


def store_block(step, out, outs):
    a_keep, a_send, b_keep, b_send = outs
    rows, width = a_keep.shape[0], a_keep.shape[1] // 2

    @pl.when(step == 0)
    def _():
        a_keep[...] = out

    @pl.when(step == 2)
    def _():
        a_send[...] = out

    for place, at in ((0, 1), (1, 3)):

        @pl.when(step == at)
        def _(place=place):
            b_keep[place * rows : (place + 1) * rows, :] = out[:, :width]
            b_send[place * rows : (place + 1) * rows, :] = out[:, width:]


class Weights:
    def __init__(self, step, sides, held_ref, sems):
        self.step, self.held_ref = step, held_ref
        kinds, padded = held_ref.shape[0], held_ref.shape[1] // 2
        used = sides[0].shape[0] // kinds
        part = used // N_ROW
        self.copies = []
        for kind in range(kinds):
            self.copies.append([])
            for side, ref in enumerate(sides):
                for row in range(N_ROW):
                    source = ref.at[pl.ds((row * kinds + kind) * part, part), :]
                    target = held_ref.at[kind, pl.ds(side * padded + row * part, part), :]
                    sem = sems.at[(kind * len(sides) + side) * N_ROW + row]
                    self.copies[-1].append(pltpu.make_async_copy(source, target, sem))

        @pl.when(step == 0)
        def _():
            for group in self.copies:
                for copy in group:
                    copy.start()
            for kind in range(kinds):
                for side in range(2):
                    at = side * padded + used
                    held_ref[kind, at : at + padded - used, :] = jnp.zeros(
                        (padded - used, held_ref.shape[2]), held_ref.dtype
                    )

    def get(self, kind):
        @pl.when(self.step == 0)
        def _():
            for copy in self.copies[kind]:
                copy.wait()

        return self.held_ref[kind]


def gate_up_kernel(*refs):
    pieces, sides, (gate_ref, up_ref, own_ref, other_ref, all_ref), scratch = refs[:5], refs[5:7], refs[7:-2], refs[-2:]
    step = pl.program_id(0)
    weights = Weights(step, sides, *scratch)
    load_block(step, pieces, all_ref)
    gate = dot_nt(all_ref[...], weights.get(0))
    gate_ref[...] = gate
    up = dot_nt(all_ref[...], weights.get(1))
    up_ref[...] = up
    hid = low(gate * jax.nn.sigmoid(gate) * up)
    half = own_ref.shape[1]
    own_ref[...] = hid[:, :half]
    other_ref[...] = hid[:, half:]


def down_kernel(own_ref, other_ref, *refs):
    sides, outs, scratch = refs[:2], refs[2:-2], refs[-2:]
    step = pl.program_id(0)
    held = Weights(step, sides, *scratch).get(0)
    half = own_ref.shape[1]
    store_block(step, low(dot_nn(own_ref[...], held[:half]) + dot_nn(other_ref[...], held[half:])), outs)


def down_back_kernel(*refs):
    pieces, (gate_ref, up_ref), sides, outs, scratch = refs[:5], refs[5:7], refs[7:9], refs[9:-2], refs[-2:]
    own_ref, other_ref, all_ref = outs
    step = pl.program_id(0)
    weights = Weights(step, sides, *scratch)
    load_block(step, pieces, all_ref)
    dhid = dot_nt(all_ref[...], weights.get(0))
    gate, up = gate_ref[...], up_ref[...]
    sigma = jax.nn.sigmoid(gate)
    half = gate.shape[1] // 2
    dup = low(dhid * (gate * sigma))
    own_ref[:, half:] = dup[:, :half]
    other_ref[:, half:] = dup[:, half:]
    dgate = low(dhid * up * sigma * (1.0 + gate * (1.0 - sigma)))
    own_ref[:, :half] = dgate[:, :half]
    other_ref[:, :half] = dgate[:, half:]


def gate_up_back_kernel(own_ref, other_ref, *refs):
    sides, outs, scratch = refs[:2], refs[2:-2], refs[-2:]
    step = pl.program_id(0)
    weights = Weights(step, sides, *scratch)
    half = own_ref.shape[1] // 2
    total = None
    for kind in range(2):
        held = weights.get(kind)
        columns = slice(kind * half, (kind + 1) * half)
        term = dot_nn(own_ref[:, columns], held[:half]) + dot_nn(other_ref[:, columns], held[half:])
        total = term if total is None else total + term
    store_block(step, low(total), outs)


def feed_call(kernel, name, pieces, narrow, sides, kinds, outs, share=SHARE):
    features = sides[0].shape[1]
    used = sides[0].shape[0] // kinds
    hidden = 2 * (-(-used // 256) * 256)
    blocks = 4
    rows = (pieces[1].shape[0] if pieces else narrow[0].shape[0] // blocks)
    once = dict(pipeline_mode=pl.Buffered(1))
    fixed = lambda shape, **k: pl.BlockSpec(shape, lambda i: (0, 0), **k)
    by_rows = lambda width: pl.BlockSpec((rows, width), lambda i: (i, 0))
    if outs:
        shapes = [jax.ShapeDtypeStruct((blocks * rows, n * hidden // 2), t) for n, t in outs]
        shapes.append(jax.ShapeDtypeStruct((blocks * rows, features), jnp.bfloat16))
        specs = [by_rows(x.shape[1]) for x in shapes]
    else:
        pair = [(rows, features)] * 2 + [(2 * rows, features // 2)] * 2
        shapes = [jax.ShapeDtypeStruct(x, jnp.bfloat16) for x in pair]
        specs = [fixed(x) for x in pair]
    return pl.pallas_call(
        kernel,
        out_shape=tuple(shapes),
        grid=(blocks,),
        in_specs=[fixed(p.shape, **once) for p in pieces]
        + [by_rows(x.shape[1]) for x in narrow]
        + [pl.BlockSpec(memory_space=pl.ANY)] * 2,
        out_specs=tuple(specs),
        scratch_shapes=[
            pltpu.VMEM((kinds, hidden, features), jnp.bfloat16),
            pltpu.SemaphoreType.DMA((kinds * 2 * N_ROW,)),
        ],
        compiler_params=pltpu.CompilerParams(vmem_limit_bytes=VMEM_BYTES),
        cost_estimate=cost(2 * kinds * blocks * rows * hidden * features, 20 << 20, blocks * rows * hidden, share),
        name=name,
    )(*pieces, *narrow, *sides)


def gate_up(pieces, sides):
    outs = ((2, jnp.float32), (2, jnp.float32), (1, jnp.bfloat16), (1, jnp.bfloat16))
    return feed_call(gate_up_kernel, "gate_up", pieces, [], sides, 2, outs)


def down(hids, sides):
    return feed_call(down_kernel, "down", [], hids, sides, 1, None)


def down_back(pieces, gate, up, sides):
    return feed_call(down_back_kernel, "down_back", pieces, [gate, up], sides, 1, ((2, jnp.bfloat16),) * 2)


def gate_up_back(both, sides):
    return feed_call(gate_up_back_kernel, "gate_up_back", [], both, sides, 2, None)


def outer_kernel(kinds, used, left_ref, left_far_ref, right_ref, right_far_ref, out_ref):
    step = pl.program_id(0)
    block = left_ref.shape[1]
    blocks = pl.num_programs(0) // kinds
    part = used // N_ROW
    total = low(dot_tn(left_ref[...], right_ref[...]) + dot_tn(left_far_ref[...], right_far_ref[...]))
    for kind in range(kinds):
        for index in range(-(-used // block)):

            @pl.when(step == kind * blocks + index)
            def _(kind=kind, index=index):
                at, end = index * block, min((index + 1) * block, used)
                while at < end:
                    row = at // part
                    stop = min(end, (row + 1) * part)
                    target = row * kinds * part + kind * part + at - row * part
                    out_ref[target : target + stop - at, :] = total[at - index * block : stop - index * block, :]
                    at = stop


def outer(lefts, rights, kinds, part):
    tokens, features = rights[0].shape
    columns = lefts[0].shape[1]
    block = 256
    out_rows = N_ROW * kinds * part
    once = pl.BlockSpec((tokens, features), lambda i: (0, 0), pipeline_mode=pl.Buffered(1))
    return pl.pallas_call(
        functools.partial(outer_kernel, kinds, N_ROW * part),
        out_shape=jax.ShapeDtypeStruct((out_rows, features), jnp.bfloat16),
        grid=(columns // block,),
        in_specs=[pl.BlockSpec((tokens, block), lambda i: (0, i))] * 2 + [once] * 2,
        out_specs=pl.BlockSpec((out_rows, features), lambda i: (0, 0)),
        compiler_params=pltpu.CompilerParams(vmem_limit_bytes=VMEM_BYTES),
        cost_estimate=cost(4 * tokens * columns * features, 8 * tokens * features),
        name="outer",
    )(*lefts, *rights)


def settle_kernel(kinds, turned, scalars, *refs):
    slots, outs, held_ref = refs[:4], refs[4:-1], refs[-1]
    d, y = scalars[0], scalars[1]
    part = slots[0].shape[0] // (2 * kinds)
    for kind in range(kinds):
        for slot, ref in enumerate(slots):
            for side in range(2):
                at = ((d ^ slot) * 2 + (y if side == 0 else 1 - y)) * part
                rows = slice((side * kinds + kind) * part, (side * kinds + kind + 1) * part)
                target = held_ref if turned else outs[kind]
                target[pl.ds(pl.multiple_of(at, 16), part), :] = wide(ref[rows, :])
        if turned:
            outs[kind][...] = jnp.transpose(held_ref[...])


def settle(scalars, slots, kinds, turned):
    rows, width = slots[0].shape
    hidden = 4 * rows // kinds
    lanes = 256
    across = lambda n: pl.BlockSpec((n, lanes), lambda i: (0, i))
    shape = (width, hidden) if turned else (hidden, width)
    out_spec = pl.BlockSpec((lanes, hidden), lambda i: (i, 0)) if turned else across(hidden)
    return pl.pallas_call(
        functools.partial(settle_kernel, kinds, turned),
        out_shape=(jax.ShapeDtypeStruct(shape, jnp.float32),) * kinds,
        grid=(width // lanes,),
        in_specs=[pl.BlockSpec(memory_space=pltpu.SMEM)] + [across(rows)] * 4,
        out_specs=(out_spec,) * kinds,
        scratch_shapes=[pltpu.VMEM((hidden, lanes), jnp.float32)],
        compiler_params=pltpu.CompilerParams(vmem_limit_bytes=VMEM_BYTES),
        cost_estimate=cost(hidden * width, 6 * kinds * hidden * width),
        name="settle",
    )(scalars, *slots)


def finish_kernel(scalars, *refs):
    slots, (q_ref, k_ref, v_ref, o_ref, q_held, kv_held) = refs[:4], refs[4:]
    part = kv_held.shape[0] // 4
    for slot, ref in enumerate(slots):
        at = scalars[0] ^ slot
        heads = pl.ds(pl.multiple_of(at * HEAD_SIZE, HEAD_SIZE), HEAD_SIZE)
        q_held[heads, :] = wide(ref[:HEAD_SIZE, :])
        kv_held[pl.ds(pl.multiple_of(at * part, part), part), :] = wide(ref[HEAD_SIZE : HEAD_SIZE + part, :])
        o_ref[heads, :] = wide(ref[HEAD_SIZE + part :, :])
    q_ref[...] = jnp.transpose(q_held[...])
    k_ref[...] = jnp.transpose(kv_held[:HEAD_SIZE, :])
    v_ref[...] = jnp.transpose(kv_held[HEAD_SIZE:, :])


def finish(scalars, slots):
    rows, width = slots[0].shape
    lanes = 256
    across = lambda n: pl.BlockSpec((n, lanes), lambda i: (0, i))
    down = lambda n: pl.BlockSpec((lanes, n), lambda i: (i, 0))
    heads = 4 * HEAD_SIZE
    shapes = [(width, heads), (width, HEAD_SIZE), (width, HEAD_SIZE), (heads, width)]
    return pl.pallas_call(
        finish_kernel,
        out_shape=tuple(jax.ShapeDtypeStruct(shape, jnp.float32) for shape in shapes),
        grid=(width // lanes,),
        in_specs=[pl.BlockSpec(memory_space=pltpu.SMEM)] + [across(rows)] * 4,
        out_specs=(down(heads), down(HEAD_SIZE), down(HEAD_SIZE), across(heads)),
        scratch_shapes=[pltpu.VMEM((heads, lanes), jnp.float32), pltpu.VMEM((2 * HEAD_SIZE, lanes), jnp.float32)],
        compiler_params=pltpu.CompilerParams(vmem_limit_bytes=VMEM_BYTES),
        cost_estimate=cost(rows * width, 24 * rows * width),
        name="finish",
    )(scalars, *slots)


def plane_gather(x):
    half = x.shape[0] // 2
    a, b = x[:half], x[half:]
    a_x = swap(a, "dp", 2)
    b_y = swap(b, "col", 1)
    a_y = swap(jnp.concatenate([a, a_x], axis=0), "col", 1)
    b_x = swap(jnp.concatenate([b, b_y], axis=1), "dp", 2)
    return [x, a_x, b_y, a_y, b_x]


def plane_scatter(parts, *others):
    a_keep, a_send, b_keep, b_send = parts
    half, width = a_keep.shape[0], b_keep.shape[1]
    a_x = swap(a_send, "dp", 2)
    b_y = swap(b_send, "col", 1)
    a_x, b_y, *others = lax.optimization_barrier((a_x, b_y, *others))
    a_y = swap(low(wide(a_keep[:, width:]) + wide(a_x[:, width:])), "col", 1)
    b_x = swap(low(wide(b_keep[half:]) + wide(b_y[half:])), "dp", 2)
    total = jnp.concatenate(
        [
            wide(a_keep[:, :width]) + wide(a_x[:, :width]) + wide(a_y),
            wide(b_keep[:half]) + wide(b_y[:half]) + wide(b_x),
        ],
        axis=0,
    )
    return (total, *others)


def dp_slots(x):
    far = swap(x, "dp", 2)
    other = swap(jnp.concatenate([x, far], axis=0), "dp", 1)
    return [x, other[: x.shape[0]], far, other[x.shape[0] :]]


def with_core(x):
    return jnp.concatenate([x, swap(x, "dp", 1)], axis=0)


def heads_sum(left, right):
    half = left.shape[1] // 2
    both = jnp.concatenate([left[:, :half], swap(left[:, half:], "dp", 1)], axis=0)
    even = low(dot_tn(both, right))
    part = half // 2
    return even, swap(even[part:], "dp", 2)


def fast_body(
    states,
    keep,
    cont_ids,
    answer_len,
    teacher,
    out_grad,
    gain_attn,
    w_query,
    key_projection,
    value_projection,
    w_out,
    gain_ffn,
    w_gate,
    w_up,
    w_down,
):
    rows, width = states.shape
    n_row, n_col, n_dp = lax.axis_size("row"), lax.axis_size("col"), lax.axis_size("dp")
    d, r, y = lax.axis_index("dp"), lax.axis_index("row"), lax.axis_index("col")
    core = d % 2
    groups = n_row // n_col
    features = width * n_col
    order = r ^ (y * groups)
    side = y.reshape(1)
    kv_scalars = jnp.stack([order, core])

    kv_mine = jnp.where(core == 0, key_projection, value_projection).T
    kv_mine = jnp.concatenate([kv_mine] + [swap(kv_mine, "row", k) for k in range(1, n_row)], axis=0)
    kv_theirs = swap(kv_mine, "dp", 1)

    heads = [rows_of(w_query, d * HEAD_SIZE, HEAD_SIZE, 1).T, rows_of(w_out, d * HEAD_SIZE, HEAD_SIZE)]
    heads = gather_rows(jnp.concatenate(heads, axis=0))

    inner = w_down.shape[0]
    inner_part = inner // (n_dp * n_col)

    def hidden_rows(at):
        return jnp.concatenate([rows_of(w, at * inner_part, inner_part) for w in (w_gate.T, w_up.T, w_down)], axis=0)

    hidden_other = swap(hidden_rows(d * n_col + (1 - y)), "col", 1)
    hidden_own = hidden_rows(d * n_col + y)
    kv_theirs, hidden_other = lax.optimization_barrier((kv_theirs, hidden_other))

    positions, segment, counted = token_layout(cont_ids, answer_len)
    row_start = r * rows
    count = jnp.sum(counted.astype(jnp.float32)).reshape(1)
    count = count + swap(count, "dp", 1)
    count = (count + swap(count, "dp", 2))[0]
    counted_here = rows_of(counted, row_start, rows).astype(jnp.float32)[:, None]
    keep_here = keep.astype(jnp.float32)[:, None]
    position = rows_of(positions, row_start, rows).astype(jnp.float32)
    query_seg = rows_of(segment, row_start, rows)
    key_segs = [rows_of(segment, jnp.maximum(r - k, 0) * rows, rows) for k in range(n_row)]
    flags = [jnp.int32(2)]
    for k in range(1, n_row):
        least, most = jnp.min(key_segs[k]), jnp.max(key_segs[k])
        active = (r >= k) & ((least < 0) | (most >= jnp.min(query_seg)))
        flags.append(jnp.where(active, jnp.where(most < 0, 1, 2), 0).astype(jnp.int32))
    flags = jnp.stack(flags + [(r - k) % n_row for k in range(n_row)])
    key_seg = jnp.concatenate(key_segs)[:, None]
    query_seg = query_seg[None, :]
    freqs = ROPE_BASE ** (-2.0 * jnp.arange(HEAD_SIZE // 2, dtype=jnp.float32) / HEAD_SIZE)
    angles_t = freqs[:, None] * position[None, :]
    cos_t, sin_t = jnp.cos(angles_t), jnp.sin(angles_t)
    cos_n, sin_n = cos_t.T, sin_t.T
    cos_n = jnp.concatenate([cos_n, cos_n], axis=1)
    sin_n = jnp.concatenate([-sin_n, sin_n], axis=1)

    def turn(x, sign):
        half = HEAD_SIZE // 2
        turned = jnp.concatenate([x[:, half:], x[:, :half]], axis=1)
        return x * cos_n + turned * (sign * sin_n)

    def turn_heads(x, sign, every):
        return jnp.concatenate(
            [
                turn(x[:, i : i + HEAD_SIZE], sign) if i % every == 0 else x[:, i : i + HEAD_SIZE]
                for i in range(0, x.shape[1], HEAD_SIZE)
            ],
            axis=1,
        )

    states_f = wide(states)
    squares = jnp.sum(states_f * states_f, axis=1)
    scale_attn = lax.rsqrt((squares + swap(squares, "col", 1)) / features + EPSILON)[:, None]
    a1 = low(states_f * scale_attn * gain_attn[None, :])
    kv_own, kv_send = key_value_project(kv_scalars, a1, kv_mine, kv_theirs)
    kv_received, heads, count = lax.optimization_barrier((swap(kv_send, "col", 1), heads, count))
    key_value = low(turn_heads(kv_own + wide(kv_received), 1.0, 2 * HEAD_SIZE))
    key_values = gather_rows(key_value)
    q_part, o_part = [
        jnp.concatenate([heads[(2 * i + j) * HEAD_SIZE : (2 * i + j + 1) * HEAD_SIZE] for i in range(n_row)], axis=0)
        for j in (0, 1)
    ]
    q_far = swap(q_part, "dp", 2)
    q_slots = [q_part, swap(q_part, "dp", 1), q_far, swap(q_far, "dp", 1)]
    q_own, q_send = project(side, a1, q_slots)
    hidden_own, hidden_other = lax.optimization_barrier((hidden_own, hidden_other, q_send))[:2]
    hidden_mine = jnp.concatenate([hidden_own, hidden_other], axis=1)
    gate_up_mine = gather_rows(hidden_mine[: 2 * inner_part])
    down_mine = gather_rows(hidden_mine[2 * inner_part :])
    q_received, key_values = lax.optimization_barrier((swap(q_send, "col", 1), key_values))
    queries = low(turn_heads(q_own + wide(q_received), 1.0, HEAD_SIZE))
    o_slots = dp_slots(after(o_part, q_send))
    queries, *o_slots = lax.optimization_barrier((queries, *o_slots))
    context, lse = attend(flags, queries, query_seg, key_seg, key_values)
    context_other = swap(context, "col", 1)
    hidden_res = states_f + keep_here * merge(side, context, context_other, o_slots)

    squares = jnp.sum(hidden_res * hidden_res, axis=1)
    scale_ffn = lax.rsqrt((squares + swap(squares, "col", 1)) / features + EPSILON)[:, None]
    a2 = low(hidden_res * scale_ffn * gain_ffn[None, :])
    a2_pieces = plane_gather(a2)
    gate_up_mine = after(gate_up_mine, a2_pieces[1])
    gate_up_sides = [gate_up_mine, swap(gate_up_mine, "dp", 1)]
    gate, up, *hids, a2_all = gate_up(a2_pieces, gate_up_sides)
    down_mine, gate, a1_other = lax.optimization_barrier((down_mine, gate, swap(a1, "col", 1)))
    down_sides = [down_mine, swap(down_mine, "dp", 1)]
    result = hidden_res + keep_here * plane_scatter(down(hids, down_sides))[0]
    error = result - wide(teacher)
    error_part = jnp.sum(counted_here * error * error)
    grad_result = wide(out_grad) + 2.0 / (count * features) * counted_here * error

    gm_pieces = plane_gather(low(keep_here * grad_result))
    def both_cores(own, other):
        return [own, swap(other, "dp", 1)]

    hids, a2_sides = both_cores(*hids), both_cores(a2_all, a2_all)
    a1_both = with_core(jnp.concatenate([a1, a1_other], axis=1))
    context_half = context.shape[1] // 2
    context_even, context_odd = [
        jnp.concatenate([context[:, i : i + context_half], context_other[:, i : i + context_half]], axis=1)
        for i in (0, context_half)
    ]
    context_cores = jnp.concatenate([context_even, swap(context_odd, "dp", 1)], axis=0)
    gate, a1_both, context_cores, *hids_sides = lax.optimization_barrier((gate, a1_both, context_cores, *hids, *a2_sides))
    hids, a2_sides = hids_sides[:2], hids_sides[2:]
    *dboth, gm_all = down_back(gm_pieces, gate, up, down_sides)

    def along_row(x):
        return lax.psum_scatter(x, "row", scatter_dimension=0, tiled=True)

    down_joined = outer(hids, both_cores(gm_all, gm_all), 1, inner_part)
    dboth_sides = both_cores(*dboth)
    *dboth, down_joined = lax.optimization_barrier((*dboth, *dboth_sides, down_joined))
    dboth, dboth_sides = dboth[:2], dboth[2:]
    down_part = along_row(down_joined)
    parts = gate_up_back(dboth, gate_up_sides)
    gate_up_joined = outer(dboth_sides, a2_sides, 2, inner_part)
    grad_normed_ffn, gate_up_joined = plane_scatter(parts, gate_up_joined)
    gate_up_joined, down_part = lax.optimization_barrier((gate_up_joined, down_part))
    gate_up_part = along_row(gate_up_joined)

    def hidden_near(part):
        near = jnp.concatenate([part[:, :width], swap(part[:, width:], "col", 1)], axis=0)
        return near, swap(near, "dp", 2)

    place = jnp.stack([d, y])

    def over_cores(near, far):
        return [near, swap(near, "dp", 1), far, swap(far, "dp", 1)]

    gain_ffn_sum = jnp.sum(grad_normed_ffn * hidden_res * scale_ffn, axis=0)
    weighted = grad_normed_ffn * gain_ffn[None, :]
    inner_sum = jnp.sum(weighted * hidden_res, axis=1)
    inner_sum = jnp.concatenate([inner_sum, jnp.full((128,), error_part)])
    inner_sum = inner_sum + swap(inner_sum, "col", 1)
    error_col = inner_sum[rows:]
    inner_sum = inner_sum[:rows, None]
    grad_hidden_res = grad_result + scale_ffn * weighted - hidden_res * scale_ffn**3 * inner_sum / features

    ga = low(keep_here * grad_hidden_res)
    do_own, do_send = project(side, ga, o_slots)
    context_cores, ga_cores = lax.optimization_barrier((context_cores, with_core(ga), do_send))[:2]
    o_even = low(dot_tn(context_cores, ga_cores))
    o_part = o_even.shape[0] // 4
    o_far = swap(jnp.concatenate([o_even[o_part : 2 * o_part], o_even[3 * o_part :]], axis=0), "dp", 2)
    do_received, o_far = lax.optimization_barrier((swap(do_send, "col", 1), o_far))
    grad_context = low(do_own + wide(do_received))
    dq, dkv_parts = attend_back(flags, queries, grad_context, lse, cos_t, sin_t, query_seg, key_seg, key_values)
    q_even, q_far = heads_sum(dq, a1_both)
    q_sum = wide(q_even[: q_far.shape[0]]) + wide(q_far)
    dkv_parts, gate_up_part = lax.optimization_barrier((dkv_parts, gate_up_part))
    dkv_sum = along_row(dkv_parts)
    gate_up_received, dkv_sum, q_other, *down_near = lax.optimization_barrier(
        (
            swap(gate_up_part[:, width:], "col", 1),
            dkv_sum,
            swap(low(q_sum[:, width:]), "col", 1),
            *hidden_near(after(down_part, q_even)),
        )
    )
    gate_up_near = jnp.concatenate([gate_up_part[:, :width], gate_up_received], axis=0)
    dkv = low(turn_heads(wide(dkv_sum), -1.0, 2 * HEAD_SIZE))
    kv_part = 2 * HEAD_SIZE // n_dp
    dwkv = low(dot_tn(with_core(dkv), a1_both)).reshape(groups, n_dp, kv_part, features)
    dwkv = [dwkv[:, i].reshape(groups * kv_part, features) for i in range(n_dp)]
    kv_far, dq_other = lax.optimization_barrier((swap(xor_order(dwkv, d ^ 2)[0], "dp", 2), swap(dq, "col", 1)))
    dwkv = low(wide(xor_order(dwkv, d)[0]) + wide(kv_far))
    kv_other, dkv_other = lax.optimization_barrier((swap(dwkv[:, width:], "col", 1), swap(dkv, "col", 1)))
    kv_heads = xor_order([dwkv[:, :width], kv_other], y)
    q_heads = xor_order([low(q_sum[:, :width]), q_other], y)
    o_heads = xor_order(
        [
            low(wide(o_even[2 * i * o_part : (2 * i + 1) * o_part]) + wide(o_far[i * o_part : (i + 1) * o_part]))
            for i in (0, 1)
        ],
        y,
    )
    o_home = along_row(after(jnp.concatenate(o_heads, axis=0), dkv_sum))
    mixed = [
        x[g * part : (g + 1) * part]
        for i in range(n_col)
        for g in range(groups)
        for x, part in ((q_heads[i], HEAD_SIZE), (kv_heads[i], kv_part))
    ]
    mixed = along_row(jnp.concatenate(mixed, axis=0))
    grad_normed_attn = merge(side, dq, dq_other, q_slots) + key_value_back(
        kv_scalars, dkv, dkv_other, kv_mine, kv_theirs
    )
    gain_attn_sum = jnp.sum(grad_normed_attn * states_f * scale_attn, axis=0)
    weighted = grad_normed_attn * gain_attn[None, :]
    inner_sum = jnp.sum(weighted * states_f, axis=1)
    inner_sum = (inner_sum + swap(inner_sum, "col", 1))[:, None]
    grad_states = grad_hidden_res + scale_attn * weighted - states_f * scale_attn**3 * inner_sum / features

    sums = jnp.concatenate([gain_attn_sum, gain_ffn_sum, error_col])
    for axis, mask in (("dp", 1), ("dp", 2), ("row", 1), ("row", 2)):
        sums = sums + swap(sums, axis, mask)
    mixed, o_home, sums, grad_states, gate_up_far = lax.optimization_barrier(
        (mixed, o_home, sums, grad_states, swap(gate_up_near, "dp", 2))
    )
    (grad_down,) = settle(place, over_cores(*down_near), 1, False)
    grad_gate, grad_up = settle(place, over_cores(gate_up_near, gate_up_far), 2, True)
    home = jnp.concatenate([mixed, o_home], axis=0)
    home_far, grad_down, grad_gate, grad_up = lax.optimization_barrier((swap(home, "dp", 2), grad_down, grad_gate, grad_up))
    grad_query, grad_key, grad_value, grad_out = finish(place, over_cores(home, home_far))
    return (
        low(result),
        sums[2 * width] / (count * features),
        grad_states,
        sums[:width],
        grad_query,
        grad_key,
        grad_value,
        grad_out,
        sums[width : 2 * width],
        grad_gate,
        grad_up,
        grad_down,
    )


def solution(mesh):
    return jax.shard_map(
        fast_body if dict(mesh.shape) == {"dp": 4, "row": 4, "col": 2} else body,
        mesh=mesh,
        in_specs=(
            P(("dp", "row"), "col"),
            P(("dp", "row")),
            P("dp", None),
            P("dp", None),
            P(("dp", "row"), "col"),
            P(("dp", "row"), "col"),
            P("col"),
            P("col", "row"),
            P("col", "row"),
            P("col", "row"),
            P("row", "col"),
            P("col"),
            P("col", "row"),
            P("col", "row"),
            P("row", "col"),
        ),
        out_specs=(
            P(("dp", "row"), "col"),
            P(),
            P(("dp", "row"), "col"),
            P("col"),
            P("col", "row"),
            P("col", "row"),
            P("col", "row"),
            P("row", "col"),
            P("col"),
            P("col", "row"),
            P("col", "row"),
            P("row", "col"),
        ),
        check_vma=False,
    )
```

```python
import functools

import jax
import jax.numpy as jnp
from jax import lax
from jax.experimental import pallas as pl
from jax.experimental.pallas import tpu as pltpu
from jax.sharding import PartitionSpec as P

MODEL_WIDTH = 2048
HEAD_SIZE = 128
PROMPT = 1024


EPSILON = 1e-05
MASKED = -1e30
ROPE_BASE = 10000.0


def rows_of(values, start, count, axis=0):
    return lax.dynamic_slice_in_dim(values, start, count, axis)


def token_layout(cont_ids, answer_len):
    groups, cont_tokens = cont_ids.shape
    labels = jnp.arange(answer_len.shape[1], dtype=jnp.int32)
    starts = jnp.sum((cont_ids[:, None, :] < labels[None, :, None]).astype(jnp.int32), axis=2)
    member = (cont_ids[:, :, None] == labels[None, None, :]).astype(jnp.int32)
    own_start = jnp.sum(member * starts[:, None, :], axis=2)
    own_limit = jnp.sum(member * answer_len[:, None, :], axis=2)
    offset = jnp.arange(cont_tokens, dtype=jnp.int32)[None, :] - own_start
    prompt_pos = jnp.arange(PROMPT, dtype=jnp.int32)[None, :]
    positions = jnp.concatenate([prompt_pos, PROMPT + offset], axis=1).reshape(-1)
    segment = jnp.concatenate(
        [jnp.full((groups, PROMPT), -1, dtype=jnp.int32), cont_ids], axis=1
    ).reshape(-1)
    counted = jnp.concatenate(
        [jnp.ones((groups, PROMPT), jnp.int32), (offset < own_limit).astype(jnp.int32)], axis=1
    ).reshape(-1)
    return (positions, segment, counted)


def rotary(values, positions, sign):
    half = values.shape[-1] // 2
    freqs = ROPE_BASE ** (-2.0 * jnp.arange(half, dtype=jnp.float32) / values.shape[-1])
    angles = positions.astype(jnp.float32)[:, None] * freqs[None, :]
    cosine = jnp.cos(angles)[:, None, :]
    sine = sign * jnp.sin(angles)[:, None, :]
    first = values[..., :half]
    second = values[..., half:]
    return jnp.concatenate(
        [first * cosine - second * sine, second * cosine + first * sine], axis=-1
    )


def visible(query_index, query_segment, key_index, key_segment):
    earlier = key_index[None, :] <= query_index[:, None]
    shared = (key_segment[None, :] < 0) | (key_segment[None, :] == query_segment[:, None])
    return earlier & shared


def feature_sum(values):
    return lax.psum(values, "col")


def gather_rows(values):
    return lax.all_gather(values, "row", axis=0, tiled=True)


def gather_cols(values):
    return lax.all_gather(values, "col", axis=0, tiled=True)


def partial_cols(term, count):
    return lax.psum_scatter(
        term(jnp.int32(0), count * lax.axis_size("col")), "col", scatter_dimension=0, tiled=True
    )


def partial_rows(term, count):
    return lax.psum_scatter(
        term(jnp.int32(0), count * lax.axis_size("row")), "row", scatter_dimension=0, tiled=True
    )


def body(
    states,
    keep,
    cont_ids,
    answer_len,
    teacher,
    out_grad,
    gain_attn,
    w_query,
    key_projection,
    value_projection,
    w_out,
    gain_ffn,
    w_gate,
    w_up,
    w_down,
):
    local_rows = states.shape[0]
    whole_rows = local_rows * lax.axis_size("row")
    query_rows = whole_rows // lax.axis_size("col")
    group_tokens = PROMPT + cont_ids.shape[1]
    key_heads = key_projection.shape[1] // HEAD_SIZE
    heads_per_group = w_query.shape[1] // key_projection.shape[1]
    query_width = w_query.shape[1]
    scale = HEAD_SIZE ** (-0.5)
    block = min(512, query_rows)
    blocks = query_rows // block
    positions, segment, counted = token_layout(cont_ids, answer_len)
    token_index = jnp.arange(whole_rows, dtype=jnp.int32)
    row_start = lax.axis_index("row") * local_rows
    col_start = lax.axis_index("col") * query_rows
    counted_here = rows_of(counted, row_start, local_rows).astype(jnp.float32)[:, None]
    query_pos = rows_of(positions, col_start, query_rows)
    keep_here = keep.astype(jnp.float32)[:, None]
    states_f = states.astype(jnp.float32)
    scale_attn = lax.rsqrt(
        feature_sum(jnp.sum(states_f * states_f, axis=1)) / MODEL_WIDTH + EPSILON
    )[:, None]
    normed_attn = (states_f * scale_attn * gain_attn[None, :]).astype(jnp.bfloat16)
    normed_all = gather_rows(normed_attn)
    w_kv = jnp.concatenate([key_projection, value_projection], axis=1)
    query_raw = partial_cols(
        lambda start, count: jnp.dot(
            rows_of(normed_all, start, count), w_query, preferred_element_type=jnp.float32
        ),
        query_rows,
    )
    kv_raw = lax.psum(jnp.dot(normed_all, w_kv, preferred_element_type=jnp.float32), "col")
    queries = (
        rotary(
            query_raw.reshape(query_rows, key_heads * heads_per_group, HEAD_SIZE), query_pos, 1.0
        )
        .astype(jnp.bfloat16)
        .reshape(query_rows, key_heads, heads_per_group, HEAD_SIZE)
    )
    keys = rotary(
        kv_raw[:, : key_heads * HEAD_SIZE].reshape(whole_rows, key_heads, HEAD_SIZE), positions, 1.0
    ).astype(jnp.bfloat16)
    values = (
        kv_raw[:, key_heads * HEAD_SIZE :]
        .reshape(whole_rows, key_heads, HEAD_SIZE)
        .astype(jnp.bfloat16)
    )

    def context_of(index):
        first = col_start + index * block
        key_first = first // group_tokens * group_tokens
        query_block = rows_of(queries, index * block, block)
        key_group = rows_of(keys, key_first, group_tokens)
        value_group = rows_of(values, key_first, group_tokens)
        raw = (
            jnp.einsum("qgjd,kgd->gjqk", query_block, key_group, preferred_element_type=jnp.float32)
            * scale
        )
        mask = visible(
            rows_of(token_index, first, block),
            rows_of(segment, first, block),
            rows_of(token_index, key_first, group_tokens),
            rows_of(segment, key_first, group_tokens),
        )
        scores = jnp.where(mask[None, None], raw, MASKED)
        return (query_block, key_group, value_group, scores, key_first)

    def attend(index):
        query_block, key_group, value_group, scores, key_first = context_of(index)
        peak = jnp.max(scores, axis=-1, keepdims=True)
        exponent = jnp.exp(scores - peak)
        totals = jnp.sum(exponent, axis=-1, keepdims=True)
        weights = (exponent / totals).astype(jnp.bfloat16)
        mixed = jnp.einsum(
            "gjqk,kgd->qgjd", weights, value_group, preferred_element_type=jnp.float32
        )
        return (mixed, peak + jnp.log(totals))

    mixed_blocks, log_totals = lax.map(attend, jnp.arange(blocks, dtype=jnp.int32))
    attn_context = mixed_blocks.reshape(query_rows, query_width).astype(jnp.bfloat16)
    context_all = gather_cols(attn_context)
    attention = partial_rows(
        lambda start, count: jnp.dot(
            rows_of(context_all, start, count), w_out, preferred_element_type=jnp.float32
        ),
        local_rows,
    )
    hidden_res = states_f + keep_here * attention
    scale_ffn = lax.rsqrt(
        feature_sum(jnp.sum(hidden_res * hidden_res, axis=1)) / MODEL_WIDTH + EPSILON
    )[:, None]
    normed_ffn = (hidden_res * scale_ffn * gain_ffn[None, :]).astype(jnp.bfloat16)
    ffn_all = gather_rows(normed_ffn)
    w_pair = jnp.concatenate([w_gate, w_up], axis=1)
    inner = w_gate.shape[1]
    gate_up = partial_cols(
        lambda start, count: jnp.dot(
            rows_of(ffn_all, start, count), w_pair, preferred_element_type=jnp.float32
        ),
        query_rows,
    )
    gate = gate_up[:, :inner]
    up_proj = gate_up[:, inner:]
    sigma = jax.nn.sigmoid(gate)
    swish = gate * sigma
    hidden = (swish * up_proj).astype(jnp.bfloat16)
    hidden_all = gather_cols(hidden)
    feed = partial_rows(
        lambda start, count: jnp.dot(
            rows_of(hidden_all, start, count), w_down, preferred_element_type=jnp.float32
        ),
        local_rows,
    )
    result = hidden_res + keep_here * feed
    error = result - teacher.astype(jnp.float32)
    own_count = jnp.where(lax.axis_index("col") == 0, jnp.sum(counted_here), 0.0)
    error_total, token_count_sum = lax.psum(
        (jnp.sum(counted_here * error * error), own_count), ("dp", "row", "col")
    )
    loss = error_total / (token_count_sum * MODEL_WIDTH)
    grad_result = (
        out_grad.astype(jnp.float32) + 2.0 / (token_count_sum * MODEL_WIDTH) * counted_here * error
    )
    grad_feed = (keep_here * grad_result).astype(jnp.bfloat16)
    grad_feed_all = gather_rows(grad_feed)
    grad_down = jnp.einsum(
        "tf,td->fd", hidden_all, grad_feed_all, preferred_element_type=jnp.float32
    )
    grad_hidden = partial_cols(
        lambda start, count: jnp.einsum(
            "td,fd->tf",
            rows_of(grad_feed_all, start, count),
            w_down,
            preferred_element_type=jnp.float32,
        ),
        query_rows,
    )
    grad_gate_in = grad_hidden * up_proj * sigma * (1.0 + gate * (1.0 - sigma))
    grad_up_in = grad_hidden * swish
    grad_pair = jnp.concatenate([grad_gate_in, grad_up_in], axis=1).astype(jnp.bfloat16)
    grad_pair_all = gather_cols(grad_pair)
    grad_w_pair = jnp.einsum(
        "td,tf->df", ffn_all, grad_pair_all, preferred_element_type=jnp.float32
    )
    grad_normed_ffn = partial_rows(
        lambda start, count: jnp.einsum(
            "tf,df->td",
            rows_of(grad_pair_all, start, count),
            w_pair,
            preferred_element_type=jnp.float32,
        ),
        local_rows,
    )
    grad_gain_ffn = jnp.sum(grad_normed_ffn * hidden_res * scale_ffn, axis=0)
    weighted_ffn = grad_normed_ffn * gain_ffn[None, :]
    inner_ffn = feature_sum(jnp.sum(weighted_ffn * hidden_res, axis=1))[:, None]
    grad_hidden_res = (
        grad_result + scale_ffn * weighted_ffn - hidden_res * scale_ffn**3 * inner_ffn / MODEL_WIDTH
    )
    grad_attention = (keep_here * grad_hidden_res).astype(jnp.bfloat16)
    grad_att_all = gather_rows(grad_attention)
    grad_out = jnp.einsum(
        "to,td->od", context_all, grad_att_all, preferred_element_type=jnp.float32
    )
    grad_context = partial_cols(
        lambda start, count: jnp.einsum(
            "td,od->to",
            rows_of(grad_att_all, start, count),
            w_out,
            preferred_element_type=jnp.float32,
        ),
        query_rows,
    )
    grad_context = grad_context.astype(jnp.bfloat16).reshape(
        query_rows, key_heads, heads_per_group, HEAD_SIZE
    )

    def attend_back(carry, item):
        index, log_total = item
        query_block, key_group, value_group, scores, key_first = context_of(index)
        grad_block = rows_of(grad_context, index * block, block)
        probs = jnp.exp(scores - log_total)
        grad_probs = jnp.einsum(
            "qgjd,kgd->gjqk", grad_block, value_group, preferred_element_type=jnp.float32
        )
        row_dot = jnp.sum(probs * grad_probs, axis=-1, keepdims=True)
        grad_scores = (probs * (grad_probs - row_dot)).astype(jnp.bfloat16)
        grad_query_block = (
            jnp.einsum("gjqk,kgd->qgjd", grad_scores, key_group, preferred_element_type=jnp.float32)
            * scale
        )
        grad_key_group = (
            jnp.einsum(
                "gjqk,qgjd->kgd", grad_scores, query_block, preferred_element_type=jnp.float32
            )
            * scale
        )
        grad_value_group = jnp.einsum(
            "gjqk,qgjd->kgd",
            probs.astype(jnp.bfloat16),
            grad_block,
            preferred_element_type=jnp.float32,
        )
        pair = jnp.concatenate([grad_key_group, grad_value_group], axis=1)
        updated = rows_of(carry, key_first, group_tokens) + pair
        return (updated, grad_query_block)

    start_carry = jnp.zeros((whole_rows, 2 * key_heads, HEAD_SIZE), jnp.float32)
    grad_kv_part, grad_query_blocks = lax.scan(
        attend_back, start_carry, (jnp.arange(blocks, dtype=jnp.int32), log_totals)
    )
    grad_kv_sum = (
        lax.psum(
            grad_kv_part.reshape(whole_rows, 2 * key_heads * HEAD_SIZE).astype(jnp.bfloat16), "col"
        )
        .astype(jnp.float32)
        .reshape(whole_rows, 2 * key_heads, HEAD_SIZE)
    )
    grad_keys = rotary(grad_kv_sum[:, :key_heads], positions, -1.0)
    grad_kv = (
        jnp.concatenate([grad_keys, grad_kv_sum[:, key_heads:]], axis=1)
        .reshape(whole_rows, 2 * key_heads * HEAD_SIZE)
        .astype(jnp.bfloat16)
    )
    grad_queries = (
        rotary(
            grad_query_blocks.reshape(query_rows, key_heads * heads_per_group, HEAD_SIZE),
            query_pos,
            -1.0,
        )
        .reshape(query_rows, query_width)
        .astype(jnp.bfloat16)
    )
    grad_queries_all = gather_cols(grad_queries)
    grad_query = jnp.einsum(
        "td,tq->dq", normed_all, grad_queries_all, preferred_element_type=jnp.float32
    )
    grad_kv_weight = jnp.einsum(
        "td,tk->dk", normed_all, grad_kv, preferred_element_type=jnp.float32
    )
    grad_key = grad_kv_weight[:, : key_heads * HEAD_SIZE]
    grad_value = grad_kv_weight[:, key_heads * HEAD_SIZE :]

    def back_terms(start, count):
        from_queries = jnp.einsum(
            "tq,dq->td",
            rows_of(grad_queries_all, start, count),
            w_query,
            preferred_element_type=jnp.float32,
        )
        from_kv = jnp.einsum(
            "tk,dk->td", rows_of(grad_kv, start, count), w_kv, preferred_element_type=jnp.float32
        )
        return from_queries + from_kv

    grad_normed_attn = partial_rows(back_terms, local_rows)
    grad_gain_attn = jnp.sum(grad_normed_attn * states_f * scale_attn, axis=0)
    weighted_attn = grad_normed_attn * gain_attn[None, :]
    inner_attn = feature_sum(jnp.sum(weighted_attn * states_f, axis=1))[:, None]
    grad_states = (
        grad_hidden_res
        + scale_attn * weighted_attn
        - states_f * scale_attn**3 * inner_attn / MODEL_WIDTH
    )
    gain_attn_sum, gain_ffn_sum = lax.psum((grad_gain_attn, grad_gain_ffn), ("dp", "row"))
    summed = (
        lax.psum(grad_query.astype(jnp.bfloat16), "dp").astype(jnp.float32),
        lax.psum(grad_key.astype(jnp.bfloat16), "dp").astype(jnp.float32),
        lax.psum(grad_value.astype(jnp.bfloat16), "dp").astype(jnp.float32),
        lax.psum(grad_out.astype(jnp.bfloat16), "dp").astype(jnp.float32),
        lax.psum(grad_w_pair[:, :inner].astype(jnp.bfloat16), "dp").astype(jnp.float32),
        lax.psum(grad_w_pair[:, inner:].astype(jnp.bfloat16), "dp").astype(jnp.float32),
        lax.psum(grad_down.astype(jnp.bfloat16), "dp").astype(jnp.float32),
    )
    return (
        result.astype(jnp.bfloat16),
        loss,
        grad_states,
        gain_attn_sum,
        summed[0],
        summed[1],
        summed[2],
        summed[3],
        gain_ffn_sum,
        summed[4],
        summed[5],
        summed[6],
    )


LOG2E = 1.4426950408889634
N_ROW = 4
SHARE = 0.1


def cost(flops, moved, exps=0, share=SHARE):
    return pl.CostEstimate(flops=int(share * flops), bytes_accessed=int(share * moved), transcendentals=int(share * exps))

VMEM_BYTES = 58 << 20
ORDER = (0, 2, 1, 3)


def swap(values, axis, mask):
    size = lax.axis_size(axis)
    return lax.ppermute(values, axis, [(i, i ^ mask) for i in range(size)])


def xor_order(slots, mask):
    bit = 1
    while bit < len(slots):
        odd = (mask & bit) != 0
        slots = [jnp.where(odd, slots[i ^ bit], slots[i]) for i in range(len(slots))]
        bit *= 2
    return slots


def after(values, *others):
    return lax.optimization_barrier((values, *others))[0]


def low(values):
    return values.astype(jnp.bfloat16)


def wide(values):
    return values.astype(jnp.float32)


def dot_nn(left, right):
    return lax.dot_general(left, right, (((1,), (0,)), ((), ())), preferred_element_type=jnp.float32)


def dot_nt(left, right):
    return lax.dot_general(left, right, (((1,), (1,)), ((), ())), preferred_element_type=jnp.float32)


def dot_tn(left, right):
    return lax.dot_general(left, right, (((0,), (0,)), ((), ())), preferred_element_type=jnp.float32)


def attend_kernel(slots, scale, flags, q_ref, qseg_ref, kseg_ref, *refs):
    kv_refs = refs[:slots]
    o_ref, lse_ref, peak_ref, total_ref, acc_ref = refs[slots:]
    query = q_ref[...]
    rows = query.shape[0]

    def scores(slot):
        return dot_nt(kv_refs[slot][:, :HEAD_SIZE], query) * (scale * LOG2E)

    def seen(slot):
        key_seg = kseg_ref[slot * rows : (slot + 1) * rows, :]
        return (key_seg < 0) | (key_seg == qseg_ref[...])

    def add(slot, s):
        peak = peak_ref[...]
        higher = jnp.maximum(peak, jnp.max(s, axis=0, keepdims=True))
        fade = jnp.exp2(peak - higher)
        e = jnp.exp2(s - higher)
        total_ref[...] = total_ref[...] * fade + jnp.sum(e, axis=0, keepdims=True)
        acc_ref[...] = acc_ref[...] * fade + dot_tn(kv_refs[slot][:, HEAD_SIZE:], low(e))
        peak_ref[...] = higher

    key_index = lax.broadcasted_iota(jnp.int32, (rows, rows), 0)
    query_index = lax.broadcasted_iota(jnp.int32, (rows, rows), 1)
    s = jnp.where((key_index <= query_index) & seen(0), scores(0), MASKED)
    peak = jnp.max(s, axis=0, keepdims=True)
    e = jnp.exp2(s - peak)
    peak_ref[...] = peak
    total_ref[...] = jnp.sum(e, axis=0, keepdims=True)
    acc_ref[...] = dot_tn(kv_refs[0][:, HEAD_SIZE:], low(e))
    for slot in range(1, slots):

        @pl.when(flags[slot] == 1)
        def _(slot=slot):
            add(slot, scores(slot))

        @pl.when(flags[slot] == 2)
        def _(slot=slot):
            add(slot, jnp.where(seen(slot), scores(slot), MASKED))

    o_ref[...] = low(jnp.transpose(acc_ref[...] / total_ref[...]))
    lse_ref[0] = peak_ref[...] + jnp.log2(total_ref[...])


def attend_back_kernel(slots, scale, flags, q_ref, do_ref, lse_ref, cos_ref, sin_ref, qseg_ref, kseg_ref, *refs):
    kv_refs = refs[:slots]
    dq_ref, dkv_ref, p_ref, dp_ref, dot_ref, dq_acc, dkv_acc = refs[slots:]
    step, steps = pl.program_id(1), pl.num_programs(1)
    query, grad = q_ref[...], do_ref[...]
    rows = query.shape[0]

    @pl.when(step == 0)
    def _():
        dkv_acc[...] = jnp.zeros_like(dkv_acc)

    def seen(slot):
        key_seg = kseg_ref[slot * rows : (slot + 1) * rows, :]
        return (key_seg < 0) | (key_seg == qseg_ref[...])

    def first(slot, mask):
        e = jnp.exp2(dot_nt(kv_refs[slot][:, :HEAD_SIZE], query) * (scale * LOG2E) - lse_ref[0])
        if mask is not None:
            e = jnp.where(mask, e, 0.0)
        dp = dot_nt(kv_refs[slot][:, HEAD_SIZE:], grad)
        p_ref[slot] = e
        dp_ref[slot] = dp
        part = jnp.sum(e * dp, axis=0, keepdims=True)
        if slot == 0:
            dot_ref[...] = part
        else:
            dot_ref[...] += part

    def second(slot):
        p = p_ref[slot]
        ds = low(p * (dp_ref[slot] - dot_ref[...]))
        dkv_acc[slot, :, :HEAD_SIZE] += dot_nn(ds, query)
        dkv_acc[slot, :, HEAD_SIZE:] += dot_nn(low(p), grad)
        part = dot_tn(kv_refs[slot][:, :HEAD_SIZE], ds)
        if slot == 0:
            dq_acc[...] = part
        else:
            dq_acc[...] += part

    key_index = lax.broadcasted_iota(jnp.int32, (rows, rows), 0)
    query_index = lax.broadcasted_iota(jnp.int32, (rows, rows), 1)
    first(0, (key_index <= query_index) & seen(0))
    for slot in range(1, slots):

        @pl.when(flags[slot] == 1)
        def _(slot=slot):
            first(slot, None)

        @pl.when(flags[slot] == 2)
        def _(slot=slot):
            first(slot, seen(slot))

    second(0)
    for slot in range(1, slots):

        @pl.when(flags[slot] > 0)
        def _(slot=slot):
            second(slot)

    half = HEAD_SIZE // 2
    upper, lower = dq_acc[:half, :] * scale, dq_acc[half:, :] * scale
    cosine, sine = cos_ref[...], sin_ref[...]
    turned = jnp.concatenate([upper * cosine + lower * sine, lower * cosine - upper * sine], axis=0)
    dq_ref[...] = low(jnp.transpose(turned))

    @pl.when(step == steps - 1)
    def _():
        for slot in range(slots):
            at = pl.ds(pl.multiple_of(flags[slots + slot] * rows, rows), rows)
            dkv_ref[at, :HEAD_SIZE] = low(dkv_acc[slot, :, :HEAD_SIZE] * scale)
            dkv_ref[at, HEAD_SIZE:] = low(dkv_acc[slot, :, HEAD_SIZE:])


def attend_specs(queries, key_values):
    rows, width = queries.shape
    slots, groups = key_values.shape[0] // rows, key_values.shape[1] // (2 * HEAD_SIZE)
    whole = lambda g, m, f: (0, 0)
    head = pl.BlockSpec((rows, HEAD_SIZE), lambda g, m, f: (0, m * groups + g))
    line = pl.BlockSpec((1, 1, rows), lambda g, m, f: (m * groups + g, 0, 0))
    segs = [pl.BlockSpec((1, rows), whole), pl.BlockSpec((slots * rows, 1), whole)]
    pairs = [
        pl.BlockSpec((rows, 2 * HEAD_SIZE), lambda g, m, f, slot=slot: (f[slots + slot], g)) for slot in range(slots)
    ]
    return rows, width, slots, groups, width // HEAD_SIZE // groups, whole, head, line, segs, pairs


def attend(flags, queries, query_seg, key_seg, key_values):
    rows, width, slots, groups, share, whole, head, line, segs, pairs = attend_specs(queries, key_values)
    return pl.pallas_call(
        functools.partial(attend_kernel, slots, HEAD_SIZE ** (-0.5)),
        out_shape=(
            jax.ShapeDtypeStruct((rows, width), jnp.bfloat16),
            jax.ShapeDtypeStruct((share * groups, 1, rows), jnp.float32),
        ),
        grid_spec=pltpu.PrefetchScalarGridSpec(
            num_scalar_prefetch=1,
            grid=(groups, share),
            in_specs=[head] + segs + pairs,
            out_specs=(head, line),
            scratch_shapes=[
                pltpu.VMEM((1, rows), jnp.float32),
                pltpu.VMEM((1, rows), jnp.float32),
                pltpu.VMEM((HEAD_SIZE, rows), jnp.float32),
            ],
        ),
        compiler_params=pltpu.CompilerParams(vmem_limit_bytes=VMEM_BYTES),
        cost_estimate=cost(3 * rows * rows * width * 4, 8 << 20, 3 * rows * rows * share * groups),
        name="attend",
    )(flags, queries, query_seg, key_seg, *[key_values] * slots)


def attend_back(flags, queries, grads, lse, cosine, sine, query_seg, key_seg, key_values):
    rows, width, slots, groups, share, whole, head, line, segs, pairs = attend_specs(queries, key_values)
    angle = pl.BlockSpec((HEAD_SIZE // 2, rows), whole)
    return pl.pallas_call(
        functools.partial(attend_back_kernel, slots, HEAD_SIZE ** (-0.5)),
        out_shape=(
            jax.ShapeDtypeStruct((rows, width), jnp.bfloat16),
            jax.ShapeDtypeStruct(key_values.shape, jnp.bfloat16),
        ),
        grid_spec=pltpu.PrefetchScalarGridSpec(
            num_scalar_prefetch=1,
            grid=(groups, share),
            in_specs=[head, head, line, angle, angle] + segs + pairs,
            out_specs=(head, pl.BlockSpec((slots * rows, 2 * HEAD_SIZE), lambda g, m, f: (0, g))),
            scratch_shapes=[
                pltpu.VMEM((slots, rows, rows), jnp.float32),
                pltpu.VMEM((slots, rows, rows), jnp.float32),
                pltpu.VMEM((1, rows), jnp.float32),
                pltpu.VMEM((HEAD_SIZE, rows), jnp.float32),
                pltpu.VMEM((slots, rows, 2 * HEAD_SIZE), jnp.float32),
            ],
        ),
        compiler_params=pltpu.CompilerParams(vmem_limit_bytes=VMEM_BYTES),
        cost_estimate=cost(3 * rows * rows * width * 10, 12 << 20, 3 * rows * rows * share * groups),
        name="attend_back",
    )(flags, queries, grads, lse, cosine, sine, query_seg, key_seg, *[key_values] * slots)


def project_kernel(side, a_ref, *refs):
    slots, (own_ref, send_ref) = refs[:-2], refs[-2:]
    part = slots[0].shape[0] // 2
    own = pl.multiple_of(side[0] * part, part)
    other = pl.multiple_of((1 - side[0]) * part, part)
    for place, slot in enumerate(ORDER):
        columns = slice(place * part, (place + 1) * part)
        send_ref[:, columns] = low(dot_nt(a_ref[...], slots[slot][pl.ds(other, part), :]))
        own_ref[:, columns] = dot_nt(a_ref[...], slots[slot][pl.ds(own, part), :])


def merge_kernel(side, own_ref, other_ref, *refs):
    slots, out_ref = refs[:-1], refs[-1]
    part = slots[0].shape[0] // 2
    own = pl.multiple_of(side[0] * part, part)
    other = pl.multiple_of((1 - side[0]) * part, part)
    total = None
    for place, slot in enumerate(ORDER):
        columns = slice(place * part, (place + 1) * part)
        term = dot_nn(own_ref[:, columns], slots[slot][pl.ds(own, part), :])
        term += dot_nn(other_ref[:, columns], slots[slot][pl.ds(other, part), :])
        total = term if total is None else total + term
    out_ref[...] = total


def local_call(kernel, name, scalars, operands, outs, flops, scratch=()):
    vmem = pl.BlockSpec(memory_space=pltpu.VMEM)
    moved = sum(x.size * x.dtype.itemsize for x in operands)
    return pl.pallas_call(
        kernel,
        out_shape=outs,
        in_specs=[pl.BlockSpec(memory_space=pltpu.SMEM)] + [vmem] * len(operands),
        out_specs=jax.tree.map(lambda _: vmem, outs),
        scratch_shapes=list(scratch),
        compiler_params=pltpu.CompilerParams(vmem_limit_bytes=VMEM_BYTES),
        cost_estimate=cost(flops, 2 * moved, 0),
        name=name,
    )(scalars, *operands)


def project(side, a, slots):
    rows, width = a.shape[0], slots[0].shape[0] * len(slots) // 2
    outs = (jax.ShapeDtypeStruct((rows, width), jnp.float32), jax.ShapeDtypeStruct((rows, width), jnp.bfloat16))
    return local_call(project_kernel, "project", side, [a, *slots], outs, 4 * rows * width * a.shape[1])


def merge(side, own, other, slots):
    outs = jax.ShapeDtypeStruct((own.shape[0], slots[0].shape[1]), jnp.float32)
    return local_call(merge_kernel, "merge", side, [own, other, *slots], outs, 4 * own.size * slots[0].shape[1])


def key_value_kernel(scalars, a_ref, mine_ref, theirs_ref, own_ref, send_ref, all_ref):
    order, core = scalars[0], scalars[1]
    count = mine_ref.shape[0] // HEAD_SIZE
    groups = count // 2
    for ref, kind in ((mine_ref, core), (theirs_ref, 1 - core)):
        for slot in range(count):
            place = slot ^ order
            lane = pl.multiple_of(((place % groups) * 2 + kind) * HEAD_SIZE, HEAD_SIZE)
            all_ref[place // groups, :, pl.ds(lane, HEAD_SIZE)] = dot_nt(
                a_ref[...], ref[slot * HEAD_SIZE : (slot + 1) * HEAD_SIZE, :]
            )
    own_ref[...] = all_ref[0]
    send_ref[...] = low(all_ref[1])


def key_value_back_kernel(scalars, own_ref, other_ref, mine_ref, theirs_ref, out_ref, all_ref):
    order, core = scalars[0], scalars[1]
    count = mine_ref.shape[0] // HEAD_SIZE
    groups = count // 2
    all_ref[0] = own_ref[...]
    all_ref[1] = other_ref[...]
    total = None
    for ref, kind in ((mine_ref, core), (theirs_ref, 1 - core)):
        for slot in range(count):
            place = slot ^ order
            lane = pl.multiple_of(((place % groups) * 2 + kind) * HEAD_SIZE, HEAD_SIZE)
            term = dot_nn(
                all_ref[place // groups, :, pl.ds(lane, HEAD_SIZE)], ref[slot * HEAD_SIZE : (slot + 1) * HEAD_SIZE, :]
            )
            total = term if total is None else total + term
    out_ref[...] = total


def key_value_project(scalars, a, mine, theirs):
    rows, width = a.shape[0], mine.shape[0]
    outs = (jax.ShapeDtypeStruct((rows, width), jnp.float32), jax.ShapeDtypeStruct((rows, width), jnp.bfloat16))
    return local_call(
        key_value_kernel, "key_value", scalars, [a, mine, theirs], outs, 4 * rows * width * a.shape[1],
        [pltpu.VMEM((2, rows, width), jnp.float32)],
    )


def key_value_back(scalars, own, other, mine, theirs):
    outs = jax.ShapeDtypeStruct((own.shape[0], mine.shape[1]), jnp.float32)
    return local_call(
        key_value_back_kernel, "key_value_back", scalars, [own, other, mine, theirs], outs, 4 * own.size * mine.shape[1],
        [pltpu.VMEM((2, *own.shape), own.dtype)],
    )


def load_block(step, pieces, all_ref):
    x_ref, ax_ref, by_ref, ay_ref, bx_ref = pieces
    rows, width = ax_ref.shape

    @pl.when(step == 0)
    def _():
        all_ref[:, :width] = x_ref[:rows, :]
        all_ref[:, width:] = ay_ref[:rows, :]

    @pl.when(step == 1)
    def _():
        all_ref[:, :width] = x_ref[rows:, :]
        all_ref[:, width:] = by_ref[...]

    @pl.when(step == 2)
    def _():
        all_ref[:, :width] = ax_ref[...]
        all_ref[:, width:] = ay_ref[rows:, :]

    @pl.when(step == 3)
    def _():
        all_ref[...] = bx_ref[...]


def store_block(step, out, outs):
    a_keep, a_send, b_keep, b_send = outs
    rows, width = a_keep.shape[0], a_keep.shape[1] // 2

    @pl.when(step == 0)
    def _():
        a_keep[...] = out

    @pl.when(step == 2)
    def _():
        a_send[...] = out

    for place, at in ((0, 1), (1, 3)):

        @pl.when(step == at)
        def _(place=place):
            b_keep[place * rows : (place + 1) * rows, :] = out[:, :width]
            b_send[place * rows : (place + 1) * rows, :] = out[:, width:]


class Weights:
    def __init__(self, step, sides, held_ref, sems):
        self.step, self.held_ref = step, held_ref
        kinds, padded = held_ref.shape[0], held_ref.shape[1] // 2
        used = sides[0].shape[0] // kinds
        part = used // N_ROW
        self.copies = []
        for kind in range(kinds):
            self.copies.append([])
            for side, ref in enumerate(sides):
                for row in range(N_ROW):
                    source = ref.at[pl.ds((row * kinds + kind) * part, part), :]
                    target = held_ref.at[kind, pl.ds(side * padded + row * part, part), :]
                    sem = sems.at[(kind * len(sides) + side) * N_ROW + row]
                    self.copies[-1].append(pltpu.make_async_copy(source, target, sem))

        @pl.when(step == 0)
        def _():
            for group in self.copies:
                for copy in group:
                    copy.start()
            for kind in range(kinds):
                for side in range(2):
                    at = side * padded + used
                    held_ref[kind, at : at + padded - used, :] = jnp.zeros(
                        (padded - used, held_ref.shape[2]), held_ref.dtype
                    )

    def get(self, kind):
        @pl.when(self.step == 0)
        def _():
            for copy in self.copies[kind]:
                copy.wait()

        return self.held_ref[kind]


def gate_up_kernel(*refs):
    pieces, sides, (gate_ref, up_ref, own_ref, other_ref, all_ref), scratch = refs[:5], refs[5:7], refs[7:-2], refs[-2:]
    step = pl.program_id(0)
    weights = Weights(step, sides, *scratch)
    load_block(step, pieces, all_ref)
    gate = dot_nt(all_ref[...], weights.get(0))
    gate_ref[...] = gate
    up = dot_nt(all_ref[...], weights.get(1))
    up_ref[...] = up
    hid = low(gate * jax.nn.sigmoid(gate) * up)
    half = own_ref.shape[1]
    own_ref[...] = hid[:, :half]
    other_ref[...] = hid[:, half:]


def down_kernel(own_ref, other_ref, *refs):
    sides, outs, scratch = refs[:2], refs[2:-2], refs[-2:]
    step = pl.program_id(0)
    held = Weights(step, sides, *scratch).get(0)
    half = own_ref.shape[1]
    store_block(step, low(dot_nn(own_ref[...], held[:half]) + dot_nn(other_ref[...], held[half:])), outs)


def down_back_kernel(*refs):
    pieces, (gate_ref, up_ref), sides, outs, scratch = refs[:5], refs[5:7], refs[7:9], refs[9:-2], refs[-2:]
    own_ref, other_ref, all_ref = outs
    step = pl.program_id(0)
    weights = Weights(step, sides, *scratch)
    load_block(step, pieces, all_ref)
    dhid = dot_nt(all_ref[...], weights.get(0))
    gate, up = gate_ref[...], up_ref[...]
    sigma = jax.nn.sigmoid(gate)
    half = gate.shape[1] // 2
    dup = low(dhid * (gate * sigma))
    own_ref[:, half:] = dup[:, :half]
    other_ref[:, half:] = dup[:, half:]
    dgate = low(dhid * up * sigma * (1.0 + gate * (1.0 - sigma)))
    own_ref[:, :half] = dgate[:, :half]
    other_ref[:, :half] = dgate[:, half:]


def gate_up_back_kernel(own_ref, other_ref, *refs):
    sides, outs, scratch = refs[:2], refs[2:-2], refs[-2:]
    step = pl.program_id(0)
    weights = Weights(step, sides, *scratch)
    half = own_ref.shape[1] // 2
    total = None
    for kind in range(2):
        held = weights.get(kind)
        columns = slice(kind * half, (kind + 1) * half)
        term = dot_nn(own_ref[:, columns], held[:half]) + dot_nn(other_ref[:, columns], held[half:])
        total = term if total is None else total + term
    store_block(step, low(total), outs)


def feed_call(kernel, name, pieces, narrow, sides, kinds, outs, share=SHARE):
    features = sides[0].shape[1]
    used = sides[0].shape[0] // kinds
    hidden = 2 * (-(-used // 256) * 256)
    blocks = 4
    rows = (pieces[1].shape[0] if pieces else narrow[0].shape[0] // blocks)
    once = dict(pipeline_mode=pl.Buffered(1))
    fixed = lambda shape, **k: pl.BlockSpec(shape, lambda i: (0, 0), **k)
    by_rows = lambda width: pl.BlockSpec((rows, width), lambda i: (i, 0))
    if outs:
        shapes = [jax.ShapeDtypeStruct((blocks * rows, n * hidden // 2), t) for n, t in outs]
        shapes.append(jax.ShapeDtypeStruct((blocks * rows, features), jnp.bfloat16))
        specs = [by_rows(x.shape[1]) for x in shapes]
    else:
        pair = [(rows, features)] * 2 + [(2 * rows, features // 2)] * 2
        shapes = [jax.ShapeDtypeStruct(x, jnp.bfloat16) for x in pair]
        specs = [fixed(x) for x in pair]
    return pl.pallas_call(
        kernel,
        out_shape=tuple(shapes),
        grid=(blocks,),
        in_specs=[fixed(p.shape, **once) for p in pieces]
        + [by_rows(x.shape[1]) for x in narrow]
        + [pl.BlockSpec(memory_space=pl.ANY)] * 2,
        out_specs=tuple(specs),
        scratch_shapes=[
            pltpu.VMEM((kinds, hidden, features), jnp.bfloat16),
            pltpu.SemaphoreType.DMA((kinds * 2 * N_ROW,)),
        ],
        compiler_params=pltpu.CompilerParams(vmem_limit_bytes=VMEM_BYTES),
        cost_estimate=cost(2 * kinds * blocks * rows * hidden * features, 20 << 20, blocks * rows * hidden, share),
        name=name,
    )(*pieces, *narrow, *sides)


def gate_up(pieces, sides):
    outs = ((2, jnp.float32), (2, jnp.float32), (1, jnp.bfloat16), (1, jnp.bfloat16))
    return feed_call(gate_up_kernel, "gate_up", pieces, [], sides, 2, outs)


def down(hids, sides):
    return feed_call(down_kernel, "down", [], hids, sides, 1, None)


def down_back(pieces, gate, up, sides):
    return feed_call(down_back_kernel, "down_back", pieces, [gate, up], sides, 1, ((2, jnp.bfloat16),) * 2)


def gate_up_back(both, sides):
    return feed_call(gate_up_back_kernel, "gate_up_back", [], both, sides, 2, None)


def outer_kernel(kinds, used, left_ref, left_far_ref, right_ref, right_far_ref, out_ref):
    step = pl.program_id(0)
    block = left_ref.shape[1]
    blocks = pl.num_programs(0) // kinds
    part = used // N_ROW
    total = low(dot_tn(left_ref[...], right_ref[...]) + dot_tn(left_far_ref[...], right_far_ref[...]))
    for kind in range(kinds):
        for index in range(-(-used // block)):

            @pl.when(step == kind * blocks + index)
            def _(kind=kind, index=index):
                at, end = index * block, min((index + 1) * block, used)
                while at < end:
                    row = at // part
                    stop = min(end, (row + 1) * part)
                    target = row * kinds * part + kind * part + at - row * part
                    out_ref[target : target + stop - at, :] = total[at - index * block : stop - index * block, :]
                    at = stop


def outer(lefts, rights, kinds, part):
    tokens, features = rights[0].shape
    columns = lefts[0].shape[1]
    block = 256
    out_rows = N_ROW * kinds * part
    once = pl.BlockSpec((tokens, features), lambda i: (0, 0), pipeline_mode=pl.Buffered(1))
    return pl.pallas_call(
        functools.partial(outer_kernel, kinds, N_ROW * part),
        out_shape=jax.ShapeDtypeStruct((out_rows, features), jnp.bfloat16),
        grid=(columns // block,),
        in_specs=[pl.BlockSpec((tokens, block), lambda i: (0, i))] * 2 + [once] * 2,
        out_specs=pl.BlockSpec((out_rows, features), lambda i: (0, 0)),
        compiler_params=pltpu.CompilerParams(vmem_limit_bytes=VMEM_BYTES),
        cost_estimate=cost(4 * tokens * columns * features, 8 * tokens * features),
        name="outer",
    )(*lefts, *rights)


def settle_kernel(kinds, turned, scalars, *refs):
    slots, outs, held_ref = refs[:4], refs[4:-1], refs[-1]
    d, y = scalars[0], scalars[1]
    part = slots[0].shape[0] // (2 * kinds)
    for kind in range(kinds):
        for slot, ref in enumerate(slots):
            for side in range(2):
                at = ((d ^ slot) * 2 + (y if side == 0 else 1 - y)) * part
                rows = slice((side * kinds + kind) * part, (side * kinds + kind + 1) * part)
                target = held_ref if turned else outs[kind]
                target[pl.ds(pl.multiple_of(at, 16), part), :] = wide(ref[rows, :])
        if turned:
            outs[kind][...] = jnp.transpose(held_ref[...])


def settle(scalars, slots, kinds, turned):
    rows, width = slots[0].shape
    hidden = 4 * rows // kinds
    lanes = 256
    across = lambda n: pl.BlockSpec((n, lanes), lambda i: (0, i))
    shape = (width, hidden) if turned else (hidden, width)
    out_spec = pl.BlockSpec((lanes, hidden), lambda i: (i, 0)) if turned else across(hidden)
    return pl.pallas_call(
        functools.partial(settle_kernel, kinds, turned),
        out_shape=(jax.ShapeDtypeStruct(shape, jnp.float32),) * kinds,
        grid=(width // lanes,),
        in_specs=[pl.BlockSpec(memory_space=pltpu.SMEM)] + [across(rows)] * 4,
        out_specs=(out_spec,) * kinds,
        scratch_shapes=[pltpu.VMEM((hidden, lanes), jnp.float32)],
        compiler_params=pltpu.CompilerParams(vmem_limit_bytes=VMEM_BYTES),
        cost_estimate=cost(hidden * width, 6 * kinds * hidden * width),
        name="settle",
    )(scalars, *slots)


def finish_kernel(scalars, *refs):
    slots, (q_ref, k_ref, v_ref, o_ref, q_held, kv_held) = refs[:4], refs[4:]
    part = kv_held.shape[0] // 4
    for slot, ref in enumerate(slots):
        at = scalars[0] ^ slot
        heads = pl.ds(pl.multiple_of(at * HEAD_SIZE, HEAD_SIZE), HEAD_SIZE)
        q_held[heads, :] = wide(ref[:HEAD_SIZE, :])
        kv_held[pl.ds(pl.multiple_of(at * part, part), part), :] = wide(ref[HEAD_SIZE : HEAD_SIZE + part, :])
        o_ref[heads, :] = wide(ref[HEAD_SIZE + part :, :])
    q_ref[...] = jnp.transpose(q_held[...])
    k_ref[...] = jnp.transpose(kv_held[:HEAD_SIZE, :])
    v_ref[...] = jnp.transpose(kv_held[HEAD_SIZE:, :])


def finish(scalars, slots):
    rows, width = slots[0].shape
    lanes = 256
    across = lambda n: pl.BlockSpec((n, lanes), lambda i: (0, i))
    down = lambda n: pl.BlockSpec((lanes, n), lambda i: (i, 0))
    heads = 4 * HEAD_SIZE
    shapes = [(width, heads), (width, HEAD_SIZE), (width, HEAD_SIZE), (heads, width)]
    return pl.pallas_call(
        finish_kernel,
        out_shape=tuple(jax.ShapeDtypeStruct(shape, jnp.float32) for shape in shapes),
        grid=(width // lanes,),
        in_specs=[pl.BlockSpec(memory_space=pltpu.SMEM)] + [across(rows)] * 4,
        out_specs=(down(heads), down(HEAD_SIZE), down(HEAD_SIZE), across(heads)),
        scratch_shapes=[pltpu.VMEM((heads, lanes), jnp.float32), pltpu.VMEM((2 * HEAD_SIZE, lanes), jnp.float32)],
        compiler_params=pltpu.CompilerParams(vmem_limit_bytes=VMEM_BYTES),
        cost_estimate=cost(rows * width, 24 * rows * width),
        name="finish",
    )(scalars, *slots)


def plane_gather(x):
    half = x.shape[0] // 2
    a, b = x[:half], x[half:]
    a_x = swap(a, "dp", 2)
    b_y = swap(b, "col", 1)
    a_y = swap(jnp.concatenate([a, a_x], axis=0), "col", 1)
    b_x = swap(jnp.concatenate([b, b_y], axis=1), "dp", 2)
    return [x, a_x, b_y, a_y, b_x]


def plane_scatter(parts, *others):
    a_keep, a_send, b_keep, b_send = parts
    half, width = a_keep.shape[0], b_keep.shape[1]
    a_x = swap(a_send, "dp", 2)
    b_y = swap(b_send, "col", 1)
    a_x, b_y, *others = lax.optimization_barrier((a_x, b_y, *others))
    a_y = swap(low(wide(a_keep[:, width:]) + wide(a_x[:, width:])), "col", 1)
    b_x = swap(low(wide(b_keep[half:]) + wide(b_y[half:])), "dp", 2)
    total = jnp.concatenate(
        [
            wide(a_keep[:, :width]) + wide(a_x[:, :width]) + wide(a_y),
            wide(b_keep[:half]) + wide(b_y[:half]) + wide(b_x),
        ],
        axis=0,
    )
    return (total, *others)


def dp_slots(x):
    far = swap(x, "dp", 2)
    other = swap(jnp.concatenate([x, far], axis=0), "dp", 1)
    return [x, other[: x.shape[0]], far, other[x.shape[0] :]]


def with_core(x):
    return jnp.concatenate([x, swap(x, "dp", 1)], axis=0)


def heads_sum(left, right):
    half = left.shape[1] // 2
    both = jnp.concatenate([left[:, :half], swap(left[:, half:], "dp", 1)], axis=0)
    even = low(dot_tn(both, right))
    part = half // 2
    return even, swap(even[part:], "dp", 2)


def fast_body(
    states,
    keep,
    cont_ids,
    answer_len,
    teacher,
    out_grad,
    gain_attn,
    w_query,
    key_projection,
    value_projection,
    w_out,
    gain_ffn,
    w_gate,
    w_up,
    w_down,
):
    rows, width = states.shape
    n_row, n_col, n_dp = lax.axis_size("row"), lax.axis_size("col"), lax.axis_size("dp")
    d, r, y = lax.axis_index("dp"), lax.axis_index("row"), lax.axis_index("col")
    core = d % 2
    groups = n_row // n_col
    features = width * n_col
    order = r ^ (y * groups)
    side = y.reshape(1)
    kv_scalars = jnp.stack([order, core])

    kv_mine = jnp.where(core == 0, key_projection, value_projection).T
    kv_mine = jnp.concatenate([kv_mine] + [swap(kv_mine, "row", k) for k in range(1, n_row)], axis=0)
    kv_theirs = swap(kv_mine, "dp", 1)

    heads = [rows_of(w_query, d * HEAD_SIZE, HEAD_SIZE, 1).T, rows_of(w_out, d * HEAD_SIZE, HEAD_SIZE)]
    heads = gather_rows(jnp.concatenate(heads, axis=0))

    inner = w_down.shape[0]
    inner_part = inner // (n_dp * n_col)

    def hidden_rows(at):
        return jnp.concatenate([rows_of(w, at * inner_part, inner_part) for w in (w_gate.T, w_up.T, w_down)], axis=0)

    hidden_other = swap(hidden_rows(d * n_col + (1 - y)), "col", 1)
    hidden_own = hidden_rows(d * n_col + y)
    kv_theirs, hidden_other = lax.optimization_barrier((kv_theirs, hidden_other))

    positions, segment, counted = token_layout(cont_ids, answer_len)
    row_start = r * rows
    count = jnp.sum(counted.astype(jnp.float32)).reshape(1)
    count = count + swap(count, "dp", 1)
    count = (count + swap(count, "dp", 2))[0]
    counted_here = rows_of(counted, row_start, rows).astype(jnp.float32)[:, None]
    keep_here = keep.astype(jnp.float32)[:, None]
    position = rows_of(positions, row_start, rows).astype(jnp.float32)
    query_seg = rows_of(segment, row_start, rows)
    key_segs = [rows_of(segment, jnp.maximum(r - k, 0) * rows, rows) for k in range(n_row)]
    flags = [jnp.int32(2)]
    for k in range(1, n_row):
        least, most = jnp.min(key_segs[k]), jnp.max(key_segs[k])
        active = (r >= k) & ((least < 0) | (most >= jnp.min(query_seg)))
        flags.append(jnp.where(active, jnp.where(most < 0, 1, 2), 0).astype(jnp.int32))
    flags = jnp.stack(flags + [(r - k) % n_row for k in range(n_row)])
    key_seg = jnp.concatenate(key_segs)[:, None]
    query_seg = query_seg[None, :]
    freqs = ROPE_BASE ** (-2.0 * jnp.arange(HEAD_SIZE // 2, dtype=jnp.float32) / HEAD_SIZE)
    angles_t = freqs[:, None] * position[None, :]
    cos_t, sin_t = jnp.cos(angles_t), jnp.sin(angles_t)
    cos_n, sin_n = cos_t.T, sin_t.T
    cos_n = jnp.concatenate([cos_n, cos_n], axis=1)
    sin_n = jnp.concatenate([-sin_n, sin_n], axis=1)

    def turn(x, sign):
        half = HEAD_SIZE // 2
        turned = jnp.concatenate([x[:, half:], x[:, :half]], axis=1)
        return x * cos_n + turned * (sign * sin_n)

    def turn_heads(x, sign, every):
        return jnp.concatenate(
            [
                turn(x[:, i : i + HEAD_SIZE], sign) if i % every == 0 else x[:, i : i + HEAD_SIZE]
                for i in range(0, x.shape[1], HEAD_SIZE)
            ],
            axis=1,
        )

    states_f = wide(states)
    squares = jnp.sum(states_f * states_f, axis=1)
    scale_attn = lax.rsqrt((squares + swap(squares, "col", 1)) / features + EPSILON)[:, None]
    a1 = low(states_f * scale_attn * gain_attn[None, :])
    kv_own, kv_send = key_value_project(kv_scalars, a1, kv_mine, kv_theirs)
    kv_received, heads, count = lax.optimization_barrier((swap(kv_send, "col", 1), heads, count))
    key_value = low(turn_heads(kv_own + wide(kv_received), 1.0, 2 * HEAD_SIZE))
    key_values = gather_rows(key_value)
    q_part, o_part = [
        jnp.concatenate([heads[(2 * i + j) * HEAD_SIZE : (2 * i + j + 1) * HEAD_SIZE] for i in range(n_row)], axis=0)
        for j in (0, 1)
    ]
    q_far = swap(q_part, "dp", 2)
    q_slots = [q_part, swap(q_part, "dp", 1), q_far, swap(q_far, "dp", 1)]
    q_own, q_send = project(side, a1, q_slots)
    hidden_own, hidden_other = lax.optimization_barrier((hidden_own, hidden_other, q_send))[:2]
    hidden_mine = jnp.concatenate([hidden_own, hidden_other], axis=1)
    gate_up_mine = gather_rows(hidden_mine[: 2 * inner_part])
    down_mine = gather_rows(hidden_mine[2 * inner_part :])
    q_received, key_values = lax.optimization_barrier((swap(q_send, "col", 1), key_values))
    queries = low(turn_heads(q_own + wide(q_received), 1.0, HEAD_SIZE))
    o_slots = dp_slots(after(o_part, q_send))
    queries, *o_slots = lax.optimization_barrier((queries, *o_slots))
    context, lse = attend(flags, queries, query_seg, key_seg, key_values)
    context_other = swap(context, "col", 1)
    hidden_res = states_f + keep_here * merge(side, context, context_other, o_slots)

    squares = jnp.sum(hidden_res * hidden_res, axis=1)
    scale_ffn = lax.rsqrt((squares + swap(squares, "col", 1)) / features + EPSILON)[:, None]
    a2 = low(hidden_res * scale_ffn * gain_ffn[None, :])
    a2_pieces = plane_gather(a2)
    gate_up_mine = after(gate_up_mine, a2_pieces[1])
    gate_up_sides = [gate_up_mine, swap(gate_up_mine, "dp", 1)]
    gate, up, *hids, a2_all = gate_up(a2_pieces, gate_up_sides)
    down_mine, gate, a1_other = lax.optimization_barrier((down_mine, gate, swap(a1, "col", 1)))
    down_sides = [down_mine, swap(down_mine, "dp", 1)]
    result = hidden_res + keep_here * plane_scatter(down(hids, down_sides))[0]
    error = result - wide(teacher)
    error_part = jnp.sum(counted_here * error * error)
    grad_result = wide(out_grad) + 2.0 / (count * features) * counted_here * error

    gm_pieces = plane_gather(low(keep_here * grad_result))
    def both_cores(own, other):
        return [own, swap(other, "dp", 1)]

    hids, a2_sides = both_cores(*hids), both_cores(a2_all, a2_all)
    a1_both = with_core(jnp.concatenate([a1, a1_other], axis=1))
    context_half = context.shape[1] // 2
    context_even, context_odd = [
        jnp.concatenate([context[:, i : i + context_half], context_other[:, i : i + context_half]], axis=1)
        for i in (0, context_half)
    ]
    context_cores = jnp.concatenate([context_even, swap(context_odd, "dp", 1)], axis=0)
    gate, a1_both, context_cores, *hids_sides = lax.optimization_barrier((gate, a1_both, context_cores, *hids, *a2_sides))
    hids, a2_sides = hids_sides[:2], hids_sides[2:]
    *dboth, gm_all = down_back(gm_pieces, gate, up, down_sides)

    def along_row(x):
        return lax.psum_scatter(x, "row", scatter_dimension=0, tiled=True)

    down_joined = outer(hids, both_cores(gm_all, gm_all), 1, inner_part)
    dboth_sides = both_cores(*dboth)
    *dboth, down_joined = lax.optimization_barrier((*dboth, *dboth_sides, down_joined))
    dboth, dboth_sides = dboth[:2], dboth[2:]
    down_part = along_row(down_joined)
    parts = gate_up_back(dboth, gate_up_sides)
    gate_up_joined = outer(dboth_sides, a2_sides, 2, inner_part)
    grad_normed_ffn, gate_up_joined = plane_scatter(parts, gate_up_joined)
    gate_up_joined, down_part = lax.optimization_barrier((gate_up_joined, down_part))
    gate_up_part = along_row(gate_up_joined)

    def hidden_near(part):
        near = jnp.concatenate([part[:, :width], swap(part[:, width:], "col", 1)], axis=0)
        return near, swap(near, "dp", 2)

    place = jnp.stack([d, y])

    def over_cores(near, far):
        return [near, swap(near, "dp", 1), far, swap(far, "dp", 1)]

    gain_ffn_sum = jnp.sum(grad_normed_ffn * hidden_res * scale_ffn, axis=0)
    weighted = grad_normed_ffn * gain_ffn[None, :]
    inner_sum = jnp.sum(weighted * hidden_res, axis=1)
    inner_sum = jnp.concatenate([inner_sum, jnp.full((128,), error_part)])
    inner_sum = inner_sum + swap(inner_sum, "col", 1)
    error_col = inner_sum[rows:]
    inner_sum = inner_sum[:rows, None]
    grad_hidden_res = grad_result + scale_ffn * weighted - hidden_res * scale_ffn**3 * inner_sum / features

    ga = low(keep_here * grad_hidden_res)
    do_own, do_send = project(side, ga, o_slots)
    context_cores, ga_cores = lax.optimization_barrier((context_cores, with_core(ga), do_send))[:2]
    o_even = low(dot_tn(context_cores, ga_cores))
    o_part = o_even.shape[0] // 4
    o_far = swap(jnp.concatenate([o_even[o_part : 2 * o_part], o_even[3 * o_part :]], axis=0), "dp", 2)
    do_received, o_far = lax.optimization_barrier((swap(do_send, "col", 1), o_far))
    grad_context = low(do_own + wide(do_received))
    dq, dkv_parts = attend_back(flags, queries, grad_context, lse, cos_t, sin_t, query_seg, key_seg, key_values)
    q_even, q_far = heads_sum(dq, a1_both)
    q_sum = wide(q_even[: q_far.shape[0]]) + wide(q_far)
    dkv_parts, gate_up_part = lax.optimization_barrier((dkv_parts, gate_up_part))
    dkv_sum = along_row(dkv_parts)
    gate_up_received, dkv_sum, q_other, *down_near = lax.optimization_barrier(
        (
            swap(gate_up_part[:, width:], "col", 1),
            dkv_sum,
            swap(low(q_sum[:, width:]), "col", 1),
            *hidden_near(after(down_part, q_even)),
        )
    )
    gate_up_near = jnp.concatenate([gate_up_part[:, :width], gate_up_received], axis=0)
    dkv = low(turn_heads(wide(dkv_sum), -1.0, 2 * HEAD_SIZE))
    kv_part = 2 * HEAD_SIZE // n_dp
    dwkv = low(dot_tn(with_core(dkv), a1_both)).reshape(groups, n_dp, kv_part, features)
    dwkv = [dwkv[:, i].reshape(groups * kv_part, features) for i in range(n_dp)]
    kv_far, dq_other = lax.optimization_barrier((swap(xor_order(dwkv, d ^ 2)[0], "dp", 2), swap(dq, "col", 1)))
    dwkv = low(wide(xor_order(dwkv, d)[0]) + wide(kv_far))
    kv_other, dkv_other = lax.optimization_barrier((swap(dwkv[:, width:], "col", 1), swap(dkv, "col", 1)))
    kv_heads = xor_order([dwkv[:, :width], kv_other], y)
    q_heads = xor_order([low(q_sum[:, :width]), q_other], y)
    o_heads = xor_order(
        [
            low(wide(o_even[2 * i * o_part : (2 * i + 1) * o_part]) + wide(o_far[i * o_part : (i + 1) * o_part]))
            for i in (0, 1)
        ],
        y,
    )
    o_home = along_row(after(jnp.concatenate(o_heads, axis=0), dkv_sum))
    mixed = [
        x[g * part : (g + 1) * part]
        for i in range(n_col)
        for g in range(groups)
        for x, part in ((q_heads[i], HEAD_SIZE), (kv_heads[i], kv_part))
    ]
    mixed = along_row(after(jnp.concatenate(mixed, axis=0), o_home))
    grad_normed_attn = merge(side, dq, dq_other, q_slots) + key_value_back(
        kv_scalars, dkv, dkv_other, kv_mine, kv_theirs
    )
    gain_attn_sum = jnp.sum(grad_normed_attn * states_f * scale_attn, axis=0)
    weighted = grad_normed_attn * gain_attn[None, :]
    inner_sum = jnp.sum(weighted * states_f, axis=1)
    inner_sum = (inner_sum + swap(inner_sum, "col", 1))[:, None]
    grad_states = grad_hidden_res + scale_attn * weighted - states_f * scale_attn**3 * inner_sum / features

    sums = jnp.concatenate([gain_attn_sum, gain_ffn_sum, error_col])
    for axis, mask in (("dp", 1), ("dp", 2), ("row", 1), ("row", 2)):
        sums = sums + swap(sums, axis, mask)
    gate_up_far = swap(gate_up_near, "dp", 2)
    (grad_down,) = settle(place, over_cores(*down_near), 1, False)
    grad_gate, grad_up = settle(place, over_cores(gate_up_near, gate_up_far), 2, True)
    home = jnp.concatenate([mixed, o_home], axis=0)
    home_far, grad_down, grad_gate, grad_up, sums = lax.optimization_barrier(
        (swap(home, "dp", 2), grad_down, grad_gate, grad_up, sums)
    )
    grad_query, grad_key, grad_value, grad_out = finish(place, over_cores(home, home_far))
    return (
        low(result),
        sums[2 * width] / (count * features),
        grad_states,
        sums[:width],
        grad_query,
        grad_key,
        grad_value,
        grad_out,
        sums[width : 2 * width],
        grad_gate,
        grad_up,
        grad_down,
    )


def solution(mesh):
    return jax.shard_map(
        fast_body if dict(mesh.shape) == {"dp": 4, "row": 4, "col": 2} else body,
        mesh=mesh,
        in_specs=(
            P(("dp", "row"), "col"),
            P(("dp", "row")),
            P("dp", None),
            P("dp", None),
            P(("dp", "row"), "col"),
            P(("dp", "row"), "col"),
            P("col"),
            P("col", "row"),
            P("col", "row"),
            P("col", "row"),
            P("row", "col"),
            P("col"),
            P("col", "row"),
            P("col", "row"),
            P("row", "col"),
        ),
        out_specs=(
            P(("dp", "row"), "col"),
            P(),
            P(("dp", "row"), "col"),
            P("col"),
            P("col", "row"),
            P("col", "row"),
            P("col", "row"),
            P("row", "col"),
            P("col"),
            P("col", "row"),
            P("col", "row"),
            P("row", "col"),
        ),
        check_vma=False,
    )
```
